32 devices in a mesh: dp: 2 (over x), row: 4 (over z), col: 4 (over y, core).
Axes of the slice: x: 2, y: 2, z: 4, core: 2. Of those that a mesh axis runs over, the one named last changes fastest.
Arguments:
- tokens: bfloat16 [2, 768, 4096], P(None, 'row', ('dp', 'col')), may hold values from -6 to 6
- w_query: bfloat16 [768, 768], P(('row', 'dp'), 'col'), may hold values from -0.21875 to 0.21875
- w_key: bfloat16 [768, 768], P(('row', 'dp'), 'col'), may hold values from -0.21875 to 0.21875
- w_value: bfloat16 [768, 768], P(('row', 'dp'), 'col'), may hold values from -0.21875 to 0.21875
- w_output: bfloat16 [768, 768], P(('col', 'dp'), 'row'), may hold values from -6 to 6
- w_inner: bfloat16 [768, 3072], P(('row', 'dp'), 'col'), may hold values from -0.21875 to 0.21875
- w_outer: bfloat16 [3072, 768], P(('col', 'dp'), 'row'), may hold values from -0.109375 to 0.109375
- first_gain: float32 [768], P('row'), may hold values from 0.1 to 1.9
- first_shift: float32 [768], P('row'), may hold values from -3 to 3
- second_gain: float32 [768], P('row'), may hold values from 0.1 to 1.9
- second_shift: float32 [768], P('row'), may hold values from -3 to 3
- seq_lengths: int32 [2, 2], replicated, may hold values from 512 to 2048, as said below
- out_grad: bfloat16 [2, 768, 4096], P(None, 'row', ('dp', 'col')), may hold values from -6 to 6
Outputs:
- mixed: bfloat16 [2, 768, 4096], P(None, 'row', ('dp', 'col'))
- d_input: float32 [2, 768, 4096], P(None, 'row', ('dp', 'col'))
- grad_w_query: float32 [768, 768], P(('row', 'dp'), 'col')
- grad_w_key: float32 [768, 768], P(('row', 'dp'), 'col')
- grad_w_value: float32 [768, 768], P(('row', 'dp'), 'col')
- grad_w_output: float32 [768, 768], P(('col', 'dp'), 'row')
- grad_w_inner: float32 [768, 3072], P(('row', 'dp'), 'col')
- grad_w_outer: float32 [3072, 768], P(('col', 'dp'), 'row')
- grad_first_gain: float32 [768], P('row')
- grad_first_shift: float32 [768], P('row')
- grad_second_gain: float32 [768], P('row')
- grad_second_shift: float32 [768], P('row')
The draws below stay inside these ranges and needn't reach their ends.
Inputs may be any that keep to these rules, and one draw needn't show every extreme that they name: micro-batch m's sequence in data group g fills the first seq_lengths[m, g] positions of the group's slot of 2048 token slots; in every draw some sequence has exactly 2048 tokens and some exactly 512.
All inputs are finite; a program needn't handle non-finite values.
Results may differ from the reference program's by a relative error of at most 0.02.
Values may be sent and summed in bfloat16 or wider, within the bound.
No kernel may reach another device: no remote copies, remote signals or barrier semaphores. Data moves between devices by JAX's collectives and lax.ppermute only.
A program may use at most 128 MiB of HBM per device.

```python
import jax
import jax.numpy as jnp
from jax import lax

D = 768
HEADS = 12
HD = 64
FF = 3072
MB = 2
SEQ = 2048
GROUPS = 2
TOKENS = 4096


def draw_seq_lengths(key, part):
    key_length, key_order = jax.random.split(jax.random.fold_in(key, 7), 2)
    slot_count = MB * GROUPS
    lengths_drawn = jax.random.randint(key_length, (slot_count,), SEQ // 4, SEQ + 1)
    slot_order = jax.random.permutation(key_order, slot_count)
    lengths_drawn = lengths_drawn.at[slot_order[0]].set(SEQ)
    lengths_drawn = lengths_drawn.at[slot_order[1]].set(SEQ // 4)
    return lengths_drawn.reshape(MB, GROUPS).astype(jnp.int32)


def levels(stream_key, dims, shards, least, high):
    def one(position, blocks):
        heights = jax.random.uniform(jax.random.fold_in(jax.random.fold_in(stream_key, 6), position), (blocks,), jnp.float32, least / len(shards), high / len(shards))
        return jnp.repeat(jnp.exp(heights), dims[position] // blocks).reshape((-1,) + (1,) * (len(dims) - position - 1))

    loudness = one(*shards[0])
    for cut in shards[1:]:
        loudness = loudness * one(*cut)
    return loudness


def scatter_about(stream_key, extent, width, most, pieces=(), held_as=jnp.bfloat16):
    array = width * jax.random.normal(stream_key, extent, jnp.float32)
    if pieces:
        array = array * levels(stream_key, extent, pieces, -0.22, 0.18)
    return jnp.clip(array, -most, most).astype(held_as)


def setup_inputs(seed: int = 0) -> dict:
    keys = jax.random.split(jax.random.key(seed), 14)
    tokens = scatter_about(keys[0], (MB, D, TOKENS), 1.0, 6.0, ((1, 4), (2, 8)))
    w_query = scatter_about(keys[1], (D, D), D ** -0.5, 0.21875, ((0, 8), (1, 4)))
    w_key = scatter_about(keys[2], (D, D), D ** -0.5, 0.21875, ((0, 8), (1, 4)))
    w_value = scatter_about(keys[3], (D, D), D ** -0.5, 0.21875, ((0, 8), (1, 4)))
    w_output = scatter_about(keys[4], (D, D), 1.0, 6.0, ((0, 8), (1, 4)))
    w_inner = scatter_about(keys[5], (D, FF), D ** -0.5, 0.21875, ((0, 8), (1, 4)))
    w_outer = scatter_about(keys[6], (FF, D), FF ** -0.5, 0.109375, ((0, 8), (1, 4)))
    first_gain = jnp.clip(1.0 + 0.18 * jax.random.normal(keys[7], (D,), jnp.float32), 0.1, 1.9)
    first_shift = scatter_about(keys[8], (D,), 0.5, 3.0, ((0, 4),), jnp.float32)
    second_gain = jnp.clip(1.0 + 0.18 * jax.random.normal(keys[9], (D,), jnp.float32), 0.1, 1.9)
    second_shift = scatter_about(keys[10], (D,), 0.5, 3.0, ((0, 4),), jnp.float32)
    seq_lengths = draw_seq_lengths(jax.random.fold_in(keys[13], 71), 0)
    out_grad = scatter_about(keys[12], (MB, D, TOKENS), 1.0, 6.0, ((1, 4), (2, 8)))
    return {"tokens": tokens, "w_query": w_query, "w_key": w_key, "w_value": w_value, "w_output": w_output, "w_inner": w_inner, "w_outer": w_outer, "first_gain": first_gain, "first_shift": first_shift, "second_gain": second_gain, "second_shift": second_shift, "seq_lengths": seq_lengths, "out_grad": out_grad}


norm_eps = 1e-05
masked_score = -1e+30

@jax.custom_vjp
def low(v):
    return lax.optimization_barrier(v.astype(jnp.bfloat16)).astype(jnp.float32)

@jax.custom_vjp
def low_back(v):
    return v

def low_keep(v):
    return (low(v), None)

def low_pass(kept, grad):
    return (grad,)

def back_keep(v):
    return (v, None)

def back_low(kept, grad):
    return (low(grad),)
low.defvjp(low_keep, low_pass)
low_back.defvjp(back_keep, back_low)

def rotate_pairs(values, positions, head_size, direction):
    row_count = values.shape[0]
    row_width = values.shape[1]
    half_size = head_size // 2
    frequency = 10000.0 ** (-2.0 * jnp.arange(half_size, dtype=jnp.float32) / head_size)
    angles = positions.astype(jnp.float32)[:, None] * frequency[None, :]
    cosine = jnp.cos(angles)[:, None, :]
    sine_part = direction * jnp.sin(angles)[:, None, :]
    paired = values.reshape(row_count, row_width // head_size, half_size, 2)
    even_part = paired[..., 0]
    odd_part = paired[..., 1]
    turned = jnp.stack([even_part * cosine - odd_part * sine_part, even_part * sine_part + odd_part * cosine], axis=-1)
    return turned.reshape(row_count, row_width)

def matmul_high(left, right):
    return jnp.dot(left, right, precision=lax.Precision.HIGHEST)

def layer_norm(values, gain_vec, shift_vec):
    row_mean = lax.optimization_barrier(jnp.mean(values, axis=-1, keepdims=True))
    row_var = lax.optimization_barrier(jnp.mean(values * values, axis=-1, keepdims=True)) - row_mean * row_mean
    return (values - row_mean) * lax.rsqrt(row_var + norm_eps) * gain_vec + shift_vec

def attend_head(query_rows, key_rows, value_rows, key_valid):
    raw_scores = matmul_high(query_rows, key_rows.T) * HD ** (-0.5)
    scores = jnp.where(key_valid[None, :], low_back(raw_scores), masked_score)
    probs_low = low(jax.nn.softmax(scores, axis=-1))
    return matmul_high(probs_low, value_rows)

def layer(params, slot_tokens, length_now):
    w_query, w_key, w_value, w_output, w_inner, w_outer, first_gain, first_shift, second_gain, second_shift = params
    positions = jnp.arange(SEQ, dtype=jnp.int32)
    key_valid = positions < length_now
    query_raw = low_back(matmul_high(slot_tokens, w_query))
    key_raw = low_back(matmul_high(slot_tokens, w_key))
    value_low = low(low_back(matmul_high(slot_tokens, w_value)))
    query_rot = low(rotate_pairs(query_raw, positions, HD, 1.0))
    key_rot = low(rotate_pairs(key_raw, positions, HD, 1.0))

    def split_heads(values):
        return values.reshape(SEQ, HEADS, HD).transpose(1, 0, 2)

    def head_step(head_items):
        return attend_head(head_items[0], head_items[1], head_items[2], key_valid)
    head_outs = lax.map(jax.checkpoint(head_step), (split_heads(query_rot), split_heads(key_rot), split_heads(value_low)))
    attn_low = low(low_back(head_outs.transpose(1, 0, 2).reshape(SEQ, D)))
    hidden = layer_norm(slot_tokens + low_back(matmul_high(attn_low, w_output)), first_gain, first_shift)
    inner = low_back(matmul_high(low(hidden), w_inner))
    act_low = low(jax.nn.gelu(inner, approximate=False))
    return layer_norm(hidden + low_back(matmul_high(act_low, w_outer)), second_gain, second_shift)

def add_arrays(left, right):
    return left + right

def reference(tokens, w_query, w_key, w_value, w_output, w_inner, w_outer, first_gain, first_shift, second_gain, second_shift, seq_lengths, out_grad):
    slot_count = MB * GROUPS
    float_params = (w_query.astype(jnp.float32), w_key.astype(jnp.float32), w_value.astype(jnp.float32), w_output.astype(jnp.float32), w_inner.astype(jnp.float32), w_outer.astype(jnp.float32), first_gain.astype(jnp.float32), first_shift.astype(jnp.float32), second_gain.astype(jnp.float32), second_shift.astype(jnp.float32))
    slot_tokens = tokens.astype(jnp.float32).transpose(0, 2, 1).reshape(slot_count, SEQ, D)
    slot_grads = out_grad.astype(jnp.float32).transpose(0, 2, 1).reshape(slot_count, SEQ, D)
    slot_lengths = seq_lengths.reshape(slot_count).astype(jnp.int32)

    def slot_step(totals, slot_items):
        tokens_now, grad_now, length_now = slot_items

        def forward_fn(params, tokens_in):
            return layer(params, tokens_in, length_now)
        result, pullback = jax.vjp(forward_fn, float_params, tokens_now)
        keep_rows = (jnp.arange(SEQ, dtype=jnp.int32) < length_now).astype(jnp.float32)[:, None]
        param_grads, token_grads = pullback(grad_now * keep_rows)
        totals = jax.tree.map(add_arrays, totals, param_grads)
        return (totals, (result.astype(jnp.bfloat16), token_grads))
    initial = jax.tree.map(jnp.zeros_like, float_params)
    totals, (results, token_grads) = lax.scan(slot_step, initial, (slot_tokens, slot_grads, slot_lengths))
    return (results.reshape(MB, TOKENS, D).transpose(0, 2, 1), token_grads.reshape(MB, TOKENS, D).transpose(0, 2, 1), totals[0], totals[1], totals[2], totals[3], totals[4], totals[5], totals[6], totals[7], totals[8], totals[9])
```

```python
import jax
import jax.numpy as jnp
from jax import lax
from jax.sharding import Mesh, PartitionSpec as P

HD = 64
norm_eps = 1e-05
masked_score = -1e30
EVERY = ("dp", "rm", "rz", "cy", "cc")
ROW = ("rm", "rz")
SQUARE = ("rz", "cy")
bf16 = jnp.bfloat16
f32 = jnp.float32


def swap_by(blocks, index):
    pairs = blocks.reshape((2, 2) + blocks.shape[1:])
    high = (index // 2) == 1
    low = (index % 2) == 1
    pairs = jnp.where(high, pairs[::-1], pairs)
    pairs = jnp.where(low, pairs[:, ::-1], pairs)
    return pairs.reshape(blocks.shape)


def exchange4(blocks, axes):
    parts = [blocks[0]]
    for step in range(1, 4):
        parts.append(lax.ppermute(blocks[step], axes, [(i, i ^ step) for i in range(4)]))
    return parts


def gather4(block, axes):
    parts = [block]
    for step in range(1, 4):
        parts.append(lax.ppermute(block, axes, [(i, i ^ step) for i in range(4)]))
    return parts


def core_swap(value):
    return lax.ppermute(value, "cc", [(0, 1), (1, 0)])


def dp_gather(value):
    if lax.axis_size("dp") != 2:
        return lax.all_gather(value, "dp", axis=0, tiled=True)
    other = lax.ppermute(value, "dp", [(0, 1), (1, 0)])
    mine_first = lax.axis_index("dp") == 0
    return jnp.concatenate(
        [jnp.where(mine_first, value, other), jnp.where(mine_first, other, value)], axis=0
    )


def dp_reduce(value):
    if lax.axis_size("dp") != 2:
        return lax.psum_scatter(value.astype(bf16), "dp", scatter_dimension=0, tiled=True).astype(f32)
    half = value.shape[0] // 2
    second = lax.axis_index("dp") == 1
    keep = jnp.where(second, value[half:], value[:half])
    send = jnp.where(second, value[:half], value[half:]).astype(bf16)
    return keep + lax.ppermute(send, "dp", [(0, 1), (1, 0)]).astype(f32)


def group_route(rounds, inverse):
    pairs = []
    for m in range(2):
        for z in range(2):
            for y in range(2):
                for c in range(2):
                    source = ((m * 2 + z) * 2 + y) * 2 + c
                    target = (((m ^ rounds[0]) * 2 + c) * 2 + y) * 2 + (z ^ rounds[1])
                    pairs.append((target, source) if inverse else (source, target))
    return pairs


GROUP = ("rm", "rz", "cy", "cc")


def rotate_rows(values, positions, direction):
    heads, size, count = values.shape
    half = size // 2
    frequency = 10000.0 ** (-2.0 * jnp.arange(half, dtype=f32) / size)
    angles = frequency[:, None] * positions.astype(f32)[None, :]
    cosine = jnp.cos(angles)[None]
    sine = direction * jnp.sin(angles)[None]
    paired = values.reshape(heads, half, 2, count)
    even = paired[:, :, 0]
    odd = paired[:, :, 1]
    turned = jnp.stack([even * cosine - odd * sine, even * sine + odd * cosine], axis=2)
    return turned.reshape(values.shape)


def dot(left, right, dims):
    return lax.dot_general(left, right, ((dims[0], dims[1]), ((), ())), preferred_element_type=f32)


def attend_forward(queries, keys, values, key_valid, scale):
    def one_head(items):
        q, k, v = items
        scores = dot(q, k, ((0,), (0,))) * scale
        scores = jnp.where(key_valid[None, :], scores, masked_score)
        top = jnp.max(scores, axis=1, keepdims=True)
        total = jnp.sum(jnp.exp(scores - top), axis=1, keepdims=True)
        log_total = top + jnp.log(total)
        probs = jnp.exp(scores - log_total).astype(bf16)
        return dot(v, probs, ((1,), (1,))), log_total[:, 0]

    return lax.map(one_head, (queries, keys, values))


def attend_backward(queries, keys, values, log_totals, grads, key_valid, scale):
    def one_head(items):
        q, k, v, log_total, g = items
        scores = dot(q, k, ((0,), (0,))) * scale
        scores = jnp.where(key_valid[None, :], scores, masked_score)
        probs = jnp.exp(scores - log_total[:, None])
        grad_probs = dot(g, v, ((0,), (0,)))
        delta = jnp.sum(probs * grad_probs, axis=1, keepdims=True)
        grad_scores = (probs * (grad_probs - delta)).astype(bf16)
        grad_q = dot(k, grad_scores, ((1,), (1,))) * scale
        grad_k = dot(q, grad_scores, ((1,), (0,))) * scale
        grad_v = dot(g, probs.astype(bf16), ((1,), (0,)))
        return grad_q, grad_k, grad_v

    return lax.map(one_head, (queries, keys, values, log_totals, grads))


def layer_norm(summed, gain, shift):
    width = summed.shape[0]
    mean = jnp.sum(summed, axis=0, keepdims=True) / width
    var = jnp.sum(summed * summed, axis=0, keepdims=True) / width - mean * mean
    inv = lax.rsqrt(var + norm_eps)
    centered = (summed - mean) * inv
    return centered * gain[:, None] + shift[:, None], centered, inv


def layer_norm_back(grad, centered, inv, gain):
    width = grad.shape[0]
    cent = grad * gain[:, None]
    first = jnp.sum(cent, axis=0, keepdims=True) / width
    second = jnp.sum(cent * centered, axis=0, keepdims=True) / width
    return inv * (cent - first - centered * second)


def gelu_exact(values):
    return jax.nn.gelu(values, approximate=False)


def local(
    tokens, w_query, w_key, w_value, w_output, w_inner, w_outer,
    first_gain, first_shift, second_gain, second_shift, seq_lengths, out_grad,
):
    feat = tokens.shape[1]
    cols = tokens.shape[2]
    half = cols // 2
    width = feat * 4
    head_width = w_query.shape[1]
    heads = head_width // HD
    inner_cols = w_inner.shape[1]
    dp_count = lax.axis_size("dp")
    shard_rows = w_query.shape[0]
    scale = HD ** (-0.5)
    row = lax.axis_index(ROW)
    square = lax.axis_index(SQUARE)
    group = lax.axis_index("dp")
    m = lax.axis_index("rm")
    z = lax.axis_index("rz")
    y = lax.axis_index("cy")
    c = lax.axis_index("cc")

    def to_tokens(array):
        blocks = array.reshape(2, feat, 2, half).transpose(0, 2, 1, 3).reshape(4, feat, half)
        return swap_by(jnp.stack(exchange4(swap_by(blocks, row), ROW)), row).reshape(width, half)

    def from_tokens(array):
        blocks = array.reshape(4, feat, half)
        back = swap_by(jnp.stack(exchange4(swap_by(blocks, row), ROW)), row)
        return back.reshape(2, 2, feat, half).transpose(0, 2, 1, 3).reshape(2, feat, cols)

    x_own = to_tokens(tokens)
    x_core = jnp.stack(gather4(x_own, SQUARE))
    x_blocks = jnp.concatenate([x_core, core_swap(x_core)], axis=0)

    qkv_rows = dp_gather(jnp.concatenate([w_query, w_key, w_value], axis=1))
    half_rows = feat // 2
    row_halves = qkv_rows.reshape(2, half_rows, 3 * head_width)
    pieces = []
    for r1 in range(2):
        for r2 in range(2):
            part = jnp.where((z ^ r2) == 0, row_halves[0], row_halves[1])
            pieces.append(lax.ppermute(part, GROUP, group_route((r1, r2), False)))
    mine = swap_by(jnp.stack(pieces), m * 2 + c)
    theirs = core_swap(mine)
    first_half = jnp.where(c == 0, mine, theirs)
    second_half = jnp.where(c == 0, theirs, mine)
    w_qkv = jnp.stack([first_half, second_half], axis=1).reshape(width, 3 * head_width)

    def whole(shard):
        return lax.all_gather(shard, EVERY)

    inner_all = (
        whole(w_inner).reshape(dp_count, 4, 4, shard_rows, inner_cols)
        .transpose(1, 0, 3, 2, 4).reshape(width, 4 * inner_cols)
    )
    outer_all = (
        whole(w_outer).reshape(dp_count, 4, 4, inner_cols // dp_count, feat)
        .transpose(2, 0, 3, 1, 4).reshape(4 * inner_cols, width)
    )
    output_all = (
        whole(w_output).reshape(dp_count, 4, 4, head_width // dp_count, feat)
        .transpose(2, 0, 3, 1, 4).reshape(width, width)
    )
    norms = jnp.stack([first_gain, first_shift, second_gain, second_shift])
    norms_all = swap_by(jnp.stack(gather4(norms, ROW)), row).transpose(1, 0, 2).reshape(4, width)
    gain_one, shift_one, gain_two, shift_two = norms_all

    length = lax.dynamic_index_in_dim(seq_lengths[m], group, keepdims=False)
    starts = []
    for kc in range(2):
        for k in range(4):
            starts.append(((y ^ (k % 2)) * 2 + (c ^ kc)) * cols + (z ^ (k // 2)) * half)
    positions = (jnp.stack(starts)[:, None] + jnp.arange(half, dtype=jnp.int32)[None, :]).reshape(-1)
    own_positions = positions[: 4 * half]
    key_valid = positions < length

    def heads_of(values):
        return values.reshape(heads, HD, -1)

    x_all = x_blocks.transpose(1, 0, 2).reshape(width, 8 * half)
    x_mine = x_all[:, : 4 * half]
    q_rot = rotate_rows(heads_of(dot(w_qkv[:, :head_width], x_mine, ((0,), (0,)))), own_positions, 1.0).astype(bf16)
    kv = dot(w_qkv[:, head_width:], x_all, ((0,), (0,)))
    k_rot = rotate_rows(heads_of(kv[:head_width]), positions, 1.0).astype(bf16)
    v_low = heads_of(kv[head_width:]).astype(bf16)
    head_outs, log_totals = attend_forward(q_rot, k_rot, v_low, key_valid, scale)

    def head_to_token(values):
        blocks = values.reshape(head_width, 4, half).transpose(1, 0, 2)
        back = swap_by(jnp.stack(exchange4(blocks, SQUARE)), square)
        return back.reshape(2, 2, head_width, half).transpose(1, 0, 2, 3).reshape(width, half)

    def token_to_head(values):
        blocks = values.reshape(2, 2, head_width, half).transpose(1, 0, 2, 3).reshape(4, head_width, half)
        back = jnp.stack(exchange4(swap_by(blocks, square), SQUARE))
        return back.transpose(1, 0, 2).reshape(head_width, 4 * half)

    attn_low = head_to_token(head_outs.astype(bf16).reshape(head_width, 4 * half))

    branch = dot(output_all, attn_low, ((0,), (0,)))
    hidden, cent_one, inv_one = layer_norm(x_own.astype(f32) + branch, gain_one, shift_one)
    hidden_low = hidden.astype(bf16)
    inner = dot(inner_all, hidden_low, ((0,), (0,)))
    act_low = gelu_exact(inner).astype(bf16)
    outer = dot(outer_all, act_low, ((0,), (0,)))
    result, cent_two, inv_two = layer_norm(hidden + outer, gain_two, shift_two)
    mixed = from_tokens(result.astype(bf16))

    own_start = (y * 2 + c) * cols + z * half
    own_valid = (own_start + jnp.arange(half, dtype=jnp.int32)) < length
    cot = to_tokens(out_grad).astype(f32) * own_valid[None, :].astype(f32)
    d_gain_two = jnp.sum(cot * cent_two, axis=1)
    d_shift_two = jnp.sum(cot, axis=1)
    grad_two = layer_norm_back(cot, cent_two, inv_two, gain_two)
    outer_low = grad_two.astype(bf16)
    grad_act = dot(outer_all, outer_low, ((1,), (0,)))
    d_outer = dot(act_low, outer_low, ((1,), (1,)))
    inner_low = jax.vjp(gelu_exact, inner)[1](grad_act)[0].astype(bf16)
    grad_hidden = grad_two + dot(inner_all, inner_low, ((1,), (0,)))
    d_inner = dot(hidden_low, inner_low, ((1,), (1,)))
    d_gain_one = jnp.sum(grad_hidden * cent_one, axis=1)
    d_shift_one = jnp.sum(grad_hidden, axis=1)
    grad_one = layer_norm_back(grad_hidden, cent_one, inv_one, gain_one)
    branch_low = grad_one.astype(bf16)
    grad_attn = dot(output_all, branch_low, ((1,), (0,))).astype(bf16)
    d_output = dot(attn_low, branch_low, ((1,), (1,)))

    def spread(value):
        return lax.psum_scatter(value.astype(bf16), EVERY, scatter_dimension=0)

    d_inner_blocks = (
        d_inner.astype(bf16).reshape(4, dp_count, shard_rows, 4, inner_cols).transpose(1, 0, 3, 2, 4)
        .reshape(-1, shard_rows, inner_cols)
    )
    d_outer_blocks = (
        d_outer.astype(bf16).reshape(4, dp_count, inner_cols // dp_count, 4, feat).transpose(1, 3, 0, 2, 4)
        .reshape(-1, inner_cols // dp_count, feat)
    )
    d_output_blocks = (
        d_output.astype(bf16).reshape(4, dp_count, head_width // dp_count, 4, feat).transpose(1, 3, 0, 2, 4)
        .reshape(-1, head_width // dp_count, feat)
    )
    norm_sums = jnp.stack([d_gain_one, d_shift_one, d_gain_two, d_shift_two]).astype(bf16)
    norm_blocks = norm_sums.reshape(4, 4, feat).transpose(1, 0, 2)
    norm_blocks = jnp.broadcast_to(norm_blocks[None, :, None], (dp_count, 4, 4, 4, feat)).reshape(-1, 4, feat)
    out_and_norms = spread(jnp.concatenate([d_output_blocks, norm_blocks], axis=1))
    g_output = out_and_norms[: head_width // dp_count].astype(f32)
    g_norms = out_and_norms[head_width // dp_count :].astype(f32)
    g_inner = spread(d_inner_blocks).astype(f32)
    g_outer = spread(d_outer_blocks).astype(f32)

    grad_heads = heads_of(token_to_head(grad_attn))
    dq, dk, dv = attend_backward(q_rot, k_rot, v_low, log_totals, grad_heads, key_valid, scale)
    dkv = jnp.concatenate([dk.reshape(head_width, -1), dv.reshape(head_width, -1)], axis=0)
    kept = dkv[:, : 4 * half] + core_swap(dkv[:, 4 * half :].astype(bf16)).astype(f32)
    dq_low = rotate_rows(dq, own_positions, -1.0).astype(bf16).reshape(head_width, -1)
    dk_low = rotate_rows(heads_of(kept[:head_width]), own_positions, -1.0).astype(bf16).reshape(head_width, -1)
    dv_low = kept[head_width:].astype(bf16)
    d_proj = jnp.concatenate([dq_low, dk_low, dv_low], axis=0)

    dx = dot(w_qkv, d_proj, ((1,), (0,))).astype(bf16)
    dx_blocks = exchange4(dx.reshape(width, 4, half).transpose(1, 0, 2), SQUARE)
    d_x = grad_one
    for part in dx_blocks:
        d_x = d_x + part.astype(f32)
    d_input = from_tokens(d_x.astype(bf16)).astype(f32)

    d_qkv = dot(x_mine, d_proj, ((1,), (1,)))
    d_halves = d_qkv.reshape(4, 2, half_rows, 3 * head_width)
    keep = jnp.where(c == 0, d_halves[:, 0], d_halves[:, 1])
    give = jnp.where(c == 0, d_halves[:, 1], d_halves[:, 0]).astype(bf16)
    summed = (keep + core_swap(give).astype(f32)).astype(bf16)
    by_round = swap_by(summed, m * 2 + c)
    got = []
    for r1 in range(2):
        for r2 in range(2):
            got.append(lax.ppermute(by_round[r1 * 2 + r2], GROUP, group_route((r1, r2), True)))
    lower = got[0].astype(f32) + got[2].astype(f32)
    upper = got[1].astype(f32) + got[3].astype(f32)
    low_rows = jnp.where(z == 0, lower, upper)
    high_rows = jnp.where(z == 0, upper, lower)
    g_qkv = dp_reduce(jnp.concatenate([low_rows, high_rows], axis=0))

    return (
        mixed, d_input,
        g_qkv[:, :head_width], g_qkv[:, head_width : 2 * head_width], g_qkv[:, 2 * head_width :],
        g_output, g_inner, g_outer,
        g_norms[0], g_norms[1], g_norms[2], g_norms[3],
    )


def solution(mesh):
    shape = mesh.devices.shape
    fine = Mesh(mesh.devices.reshape(shape[0], 2, shape[1] // 2, 2, shape[2] // 2), EVERY)
    col = ("cy", "cc")
    acts = P(None, ROW, ("dp",) + col)
    by_row = P(ROW + ("dp",), col)
    by_col = P(col + ("dp",), ROW)
    vec = P(ROW)
    return jax.shard_map(
        local,
        mesh=fine,
        in_specs=(
            acts, by_row, by_row, by_row, by_col, by_row, by_col, vec, vec, vec, vec, P(), acts,
        ),
        out_specs=(
            acts, acts, by_row, by_row, by_row, by_col, by_row, by_col, vec, vec, vec, vec,
        ),
        check_vma=False,
    )
```

```python
import jax
import jax.numpy as jnp
from jax import lax
from jax.experimental import pallas as pl
from jax.experimental.pallas import tpu as pltpu
from jax.sharding import Mesh, PartitionSpec as P

HD = 64
EVERY = ("dp", "rm", "rz", "cy", "cc")
GROUP = ("rm", "rz", "cy", "cc")
ROW = ("rm", "rz")
SQUARE = ("rz", "cy")
bf16=jnp.bfloat16; f32=jnp.float32
LOG2E=1.4426950408889634
LN2=0.6931471805599453
masked_score=-1e30

def mm(a,b,dims=((1,),(0,))):
    return lax.dot_general(a,b,(dims,((),())),preferred_element_type=f32)
NT=((1,),(1,))

def pair_turn(values, cosine, signed_sine):
    shape = values.shape
    v3 = values.reshape(shape[0]//8, 8, shape[1])
    up = pltpu.roll(v3, 7, 1); down = pltpu.roll(v3, 1, 1)
    even = (lax.broadcasted_iota(jnp.int32, v3.shape, 1) % 2) == 0
    other = jnp.where(even, up, down).reshape(shape)
    return values*cosine + other*signed_sine

KB=1024
QB=2
def one_row(shape, dtype, value=1.0):
    return jnp.where(lax.broadcasted_iota(jnp.int32, shape, 0)==0, value, 0.0).astype(dtype)

def attend_kernel(q_ref, ko_ref, vo_ref, kx_ref, vx_ref, bias_ref, o_ref, lse_ref, l0, l1, l2, l3, kaug, vall):
    head=pl.program_id(0); qb=pl.program_id(1)
    span=ko_ref.shape[1]
    @pl.when(qb==0)
    def _():
        for part,(kr,vr) in enumerate(((ko_ref,vo_ref),(kx_ref,vx_ref))):
            aug=jnp.concatenate([kr[...], bias_ref[:, part*span:(part+1)*span]],axis=0)
            kaug[part*span:(part+1)*span,:]=aug.T
            vall[:, part*span:(part+1)*span]=vr[...]
    n=q_ref.shape[1]
    qaug=jnp.concatenate([q_ref[...], one_row((HD,n),bf16)],axis=0)
    top=jnp.full((1,n),-3e38,f32); total=jnp.zeros((1,n),f32); acc=jnp.zeros((HD,n),f32)
    s=mm(kaug[0:KB,:],qaug)
    for kb in range(0,2*span,KB):
        following=mm(kaug[kb+KB:kb+2*KB,:],qaug) if kb+KB<2*span else None
        new=jnp.maximum(top,jnp.max(s,axis=0,keepdims=True))
        alpha=jnp.exp2(top-new)
        p=jnp.exp2(s-new)
        total=total*alpha+jnp.sum(p,axis=0,keepdims=True)
        acc=acc*alpha+mm(vall[:,kb:kb+KB],p.astype(bf16))
        top=new
        s=following
    out=acc/total
    o_ref[...]=out
    lse_ref[0]=top+jnp.log2(total)
    low=out.astype(bf16)
    part=n//QB
    for k,ref in enumerate((l0,l1,l2,l3)):
        @pl.when(qb==k//QB)
        def _(): ref[pl.ds(pl.multiple_of(head*HD,HD),HD),:]=low[:,(k%QB)*part:(k%QB+1)*part]

def attend(q,kv,kvx,bias):
    width,n4=q.shape; heads=width//HD; n=n4//4*QB; span=kv.shape[1]
    kspec=pl.BlockSpec((HD,span),lambda h,b:(h,0)); vspec=pl.BlockSpec((HD,span),lambda h,b:(heads+h,0))
    lowspec=pl.BlockSpec((width,n4//4),lambda h,b:(0,0))
    return pl.pallas_call(attend_kernel,grid=(heads,4//QB),
        in_specs=[pl.BlockSpec((HD,n),lambda h,b:(h,b)),kspec,vspec,kspec,vspec,pl.BlockSpec((HD,2*span),lambda h,b:(0,0))],
        out_specs=[pl.BlockSpec((HD,n),lambda h,b:(h,b)),pl.BlockSpec((1,1,n),lambda h,b:(h,0,b))]+[lowspec]*4,
        out_shape=[jax.ShapeDtypeStruct((width,n4),f32),jax.ShapeDtypeStruct((heads,1,n4),f32)]+[jax.ShapeDtypeStruct((width,n4//4),bf16)]*4,
        scratch_shapes=[pltpu.VMEM((2*span,2*HD),bf16),pltpu.VMEM((HD,2*span),bf16)],
        name="attend")(q,kv,kv,kvx,kvx,bias)

BKB=512
def attend_back_kernel(q_ref, ko_ref, vo_ref, kx_ref, vx_ref, bias_ref, o_ref, lse_ref, g0,g1,g2,g3, cos_ref, sin_ref,
                       dq_ref, own_ref, give_ref, kaug, vtm, kall, acc):
    head=pl.program_id(0); qb=pl.program_id(1)
    span=ko_ref.shape[1]; n=q_ref.shape[1]
    @pl.when(qb==0)
    def _():
        for part,(kr,vr) in enumerate(((ko_ref,vo_ref),(kx_ref,vx_ref))):
            sl=slice(part*span,(part+1)*span)
            kaug[sl,:]=jnp.concatenate([kr[...], bias_ref[:, sl]],axis=0).T
            vtm[sl,:]=jnp.concatenate([vr[...], jnp.zeros((HD,span),bf16)],axis=0).T
            kall[:,sl]=kr[...]
        acc[...]=jnp.zeros_like(acc)
    q=q_ref[...]
    zeros=jnp.zeros((HD,n),bf16)
    qaug=jnp.concatenate([q, one_row((HD,n),bf16)],axis=0)
    g=jnp.concatenate([jnp.where(qb==0,g0[...],g2[...]),jnp.where(qb==0,g1[...],g3[...])],axis=1)
    qpad=jnp.concatenate([q,zeros],axis=0).T
    gpad=jnp.concatenate([zeros,g],axis=0).T
    gaug=jnp.concatenate([g,zeros],axis=0)
    delta=jnp.sum(g.astype(f32)*o_ref[...],axis=0,keepdims=True)
    lse=lse_ref[0]
    dq=jnp.zeros((HD,n),f32)
    s=mm(kaug[0:BKB,:],qaug); dp=mm(vtm[0:BKB,:],gaug)
    for kb in range(0,2*span,BKB):
        last=kb+BKB>=2*span
        s_next=None if last else mm(kaug[kb+BKB:kb+2*BKB,:],qaug)
        dp_next=None if last else mm(vtm[kb+BKB:kb+2*BKB,:],gaug)
        p=jnp.exp2(s-lse)
        ds=(p*(dp-delta)).astype(bf16)
        dq=dq+mm(kall[:,kb:kb+BKB],ds)
        acc[kb:kb+BKB,:]=acc[kb:kb+BKB,:]+mm(ds,qpad)+mm(p.astype(bf16),gpad)
        s=s_next; dp=dp_next
    dq_ref[...]=pair_turn(dq*(HD**-0.5),cos_ref[...],-sin_ref[...]).astype(bf16)
    @pl.when(qb==4//QB-1)
    def _():
        own_ref[0]=acc[:span,:]
        give_ref[0]=acc[span:,:].astype(bf16)

def attend_back(q,kv,kvx,bias,o,lse,grads,cos,sin):
    width,n4=q.shape; heads=width//HD; n=n4//4*QB; span=kv.shape[1]
    kspec=pl.BlockSpec((HD,span),lambda h,b:(h,0)); vspec=pl.BlockSpec((HD,span),lambda h,b:(heads+h,0))
    gspec=pl.BlockSpec((HD,n4//4),lambda h,b:(h,0)); hb=pl.BlockSpec((HD,n),lambda h,b:(h,b)); tb=pl.BlockSpec((HD,n),lambda h,b:(0,b))
    dspec=pl.BlockSpec((1,span,2*HD),lambda h,b:(h,0,0))
    return pl.pallas_call(attend_back_kernel,grid=(heads,4//QB),
        in_specs=[hb,kspec,vspec,kspec,vspec,pl.BlockSpec((HD,2*span),lambda h,b:(0,0)),hb,pl.BlockSpec((1,1,n),lambda h,b:(h,0,b)),gspec,gspec,gspec,gspec,tb,tb],
        out_specs=[hb,dspec,dspec],
        out_shape=[jax.ShapeDtypeStruct((width,n4),bf16),jax.ShapeDtypeStruct((heads,span,2*HD),f32),jax.ShapeDtypeStruct((heads,span,2*HD),bf16)],
        scratch_shapes=[pltpu.VMEM((2*span,2*HD),bf16),pltpu.VMEM((2*span,2*HD),bf16),pltpu.VMEM((HD,2*span),bf16),pltpu.VMEM((2*span,2*HD),f32)],
        name="attend_back")(q,kv,kv,kvx,kvx,bias,o,lse,*grads,cos,sin)
def xor(a,b):
    return lax.bitwise_xor(jnp.asarray(a,jnp.int32),jnp.asarray(b,jnp.int32))

def rows_at(index,size,align):
    return pl.ds(pl.multiple_of(index*size,align),size)

def place_qkv_weights(info, mine_ref, theirs_ref, w_s):
    c=info[3]; mc=info[2]
    half=mine_ref.shape[1]
    for r in range(4):
        a=mine_ref[xor(r,mc)]; b=theirs_ref[xor(r,xor(mc,1))]
        for h in range(2):
            w_s[(2*r+h)*half:(2*r+h+1)*half,:]=jnp.where(c==h,a,b)

def place_tokens(info, x_ref, kz, x_s):
    feat=x_ref.shape[1]; base=xor(info[0],kz)
    for r in range(4):
        x_s[r*feat:(r+1)*feat,:]=x_ref[xor(r,base)]

def qkv_kernel(info, x0,x1,x2,x3, mine_ref, theirs_ref, cos_ref, sin_ref, q_ref, kv_ref, w_s, wt_s, x_s):
    place_qkv_weights(info,mine_ref,theirs_ref,w_s)
    wt_s[...]=w_s[...].T
    hw=q_ref.shape[0]; n=x0.shape[2]
    for k,xr in enumerate((x0,x1,x2,x3)):
        place_tokens(info,xr,k//2,x_s)
        out=mm(wt_s[...],x_s[...])
        sl=slice(k*n,(k+1)*n)
        cos=cos_ref[:,sl]; sin=sin_ref[:,sl]
        for h in range(2*hw//HD):
            turned=pair_turn(out[h*HD:(h+1)*HD],cos,sin)
            if h*HD<hw: q_ref[h*HD:(h+1)*HD,sl]=(turned*(HD**-0.5*LOG2E)).astype(bf16)
            else: kv_ref[h*HD-hw:(h+1)*HD-hw,sl]=turned.astype(bf16)
        kv_ref[hw:,sl]=out[2*hw:].astype(bf16)

VM=pl.BlockSpec(memory_space=pltpu.VMEM)
SM=pl.BlockSpec(memory_space=pltpu.SMEM)
HB=pl.BlockSpec(memory_space=pl.ANY)

def qkv(info,xs,mine,theirs,cos,sin):
    _,feat,n=xs[0].shape; w3=mine.shape[2]; hw=w3//3; width=4*feat
    return pl.pallas_call(qkv_kernel,in_specs=[SM]+[VM]*8,out_specs=[VM,VM],
        out_shape=[jax.ShapeDtypeStruct((hw,4*n),bf16),jax.ShapeDtypeStruct((2*hw,4*n),bf16)],
        scratch_shapes=[pltpu.VMEM((width,w3),bf16),pltpu.VMEM((w3,width),bf16),pltpu.VMEM((width,n),bf16)],
        name="qkv")(info,*xs,mine,theirs,cos,sin)

def finish_kernel(info, dq_ref, own_ref, got_ref, x0,x1,x2,x3, mine_ref, theirs_ref, cos_ref, sin_ref,
                  d0,d1,d2,d3, keep_ref, give_ref, w_s, x_s, p_s, g_s):
    hw=dq_ref.shape[0]; n=x0.shape[2]; feat=x0.shape[1]; half=mine_ref.shape[1]
    p_s[:hw,:]=dq_ref[...]
    for h in range(hw//HD):
        t=(own_ref[h]+got_ref[h].astype(f32)).T
        p_s[hw+h*HD:hw+(h+1)*HD,:]=pair_turn(t[:HD]*LN2,cos_ref[...],-sin_ref[...]).astype(bf16)
        p_s[2*hw+h*HD:2*hw+(h+1)*HD,:]=t[HD:].astype(bf16)
    place_qkv_weights(info,mine_ref,theirs_ref,w_s)
    for k,(xr,dr) in enumerate(((x0,d0),(x1,d1),(x2,d2),(x3,d3))):
        sl=slice(k*n,(k+1)*n)
        base=xor(info[0],k//2)
        for r in range(4):
            part=mm(w_s[r*feat:(r+1)*feat,:],p_s[:,sl])
            dr[xor(r,base)]=part.astype(dr.dtype)
    for k,xr in enumerate((x0,x1,x2,x3)):
        place_tokens(info,xr,k//2,x_s.at[:,k*n:(k+1)*n])
    g_s[...]=mm(x_s[...],p_s[...],NT)
    c=info[3]; mc=info[2]
    for r in range(4):
        for h in range(2):
            block=g_s[(2*r+h)*half:(2*r+h+1)*half,:]
            @pl.when(c==h)
            def _(): keep_ref[xor(r,mc)]=block
            @pl.when(c!=h)
            def _(): give_ref[xor(r,xor(mc,1))]=block.astype(bf16)

def finish(info,dq,own,got,xs,mine,theirs,cos,sin):
    _,feat,n=xs[0].shape; w3=mine.shape[2]; hw=w3//3; width=4*feat; half=mine.shape[1]
    part=[jax.ShapeDtypeStruct((4,feat,n),f32)]+[jax.ShapeDtypeStruct((4,feat,n),bf16)]*3
    return pl.pallas_call(finish_kernel,in_specs=[SM]+[VM]*11,out_specs=[VM]*6,
        out_shape=part+[jax.ShapeDtypeStruct((4,half,w3),f32),jax.ShapeDtypeStruct((4,half,w3),bf16)],
        scratch_shapes=[pltpu.VMEM((width,w3),bf16),pltpu.VMEM((width,4*n),bf16),pltpu.VMEM((w3,4*n),bf16),pltpu.VMEM((width,w3),f32)],
        name="finish")(info,dq,own,got,*xs,mine,theirs,cos,sin)

def middle_kernel(info, a0,a1,a2,a3, x_ref, c0,c1,c2,c3, ag_ref,
                  mixed_ref, e0,e1,e2,e3, g1_ref, attnT_ref, hidT_ref, outT_ref, bl_ref, act_ref, il_ref, norm_ref,
                  win, woT, wo, ns, gp_s, t_s, f_s, sems):
    row=info[0]; zy=info[1]
    feat=a0.shape[0]; n=a0.shape[1]; width=4*feat; ffc=ag_ref.shape[2]; half=feat//2; fh=ffc//2
    copies=[]
    def go(src,dst,s): pltpu.make_async_copy(src,dst,sems.at[s]).start()
    for g in range(2):
        for r in range(4):
            for col in range(4):
                b=(g*4+r)*4+col
                for j in range(3):
                    o=(col*2+g)*half+j*(half//3)
                    go(ag_ref.at[b,2*half:2*half+half//3,j*256:(j+1)*256],wo.at[r,o:o+half//3,:],0)
    for r in range(4):
        go(ag_ref.at[r*4,ag_ref.shape[1]-16:,:],ns.at[r],3)
    for g in range(2):
        for r in range(4):
            for col in range(4):
                b=(g*4+r)*4+col
                go(ag_ref.at[b,0:half,:],win.at[r*feat+g*half:r*feat+(g+1)*half,col*ffc:(col+1)*ffc],1)
    for g in range(2):
        for r in range(4):
            for col in range(4):
                b=(g*4+r)*4+col
                for t in range(2):
                    o=(col*2+g)*fh
                    go(ag_ref.at[b,half:2*half,t*fh:(t+1)*fh],woT.at[r*feat+t*half:r*feat+(t+1)*half,o:o+fh],2)
    def group_of(k):
        other=xor(zy,k)
        return (other%2)*2+other//2
    for k,ar in enumerate((a0,a1,a2,a3)):
        attnT_ref[rows_at(group_of(k),feat,64),:]=ar[...]
    for i in range(4):
        t_s[rows_at(xor(i,row),feat,64),:]=x_ref[i]
    attn=attnT_ref[...].T
    x=t_s[...].T.astype(f32)
    pltpu.make_async_copy(wo,wo,sems.at[0]).wait()
    pltpu.make_async_copy(ns,ns,sems.at[3]).wait()
    def vector(which):
        out=[]
        for r in range(4):
            v=ns[r].astype(f32)[0:3,which*feat:(which+1)*feat]
            out.append(jnp.sum(v,axis=0,keepdims=True))
        return jnp.concatenate(out,axis=1)
    gain1=vector(0); shift1=vector(1); gain2=vector(2); shift2=vector(3)
    branch=jnp.concatenate([mm(attn,wo[r])[:,:feat] for r in range(4)],axis=1)
    def stats(v):
        mean=jnp.sum(v,axis=1,keepdims=True)*(1.0/width)
        var=jnp.sum(v*v,axis=1,keepdims=True)*(1.0/width)-mean*mean
        inv=lax.rsqrt(var+1e-5)
        return (v-mean)*inv,inv
    cent1,inv1=stats(x+branch)
    hidden=cent1*gain1+shift1
    hid=hidden.astype(bf16)
    hidT_ref[...]=hid.T
    pltpu.make_async_copy(win,win,sems.at[1]).wait()
    pltpu.make_async_copy(woT,woT,sems.at[2]).wait()
    f_s[...]=jnp.zeros_like(f_s)
    nb=2; bw=ffc//nb
    def forward(j,carry):
        sl=pl.ds(pl.multiple_of(j*bw,128),bw)
        inner=mm(hid,win[:,sl])
        cdf=0.5+0.5*lax.erf(inner*0.7071067811865476)
        act=(inner*cdf).astype(bf16)
        gp_s[:,sl]=cdf+inner*(jnp.exp(inner*inner*-0.5)*0.3989422804014327)
        act_ref[:,sl]=act
        f_s[...]+=mm(act,woT[:,sl],NT)
        return carry
    lax.fori_loop(0,4*nb,forward,0)
    cent2,inv2=stats(hidden+f_s[...])
    t_s[...]=(cent2*gain2+shift2).astype(bf16).T
    for i in range(4):
        mixed_ref[i]=t_s[rows_at(xor(i,row),feat,64),:]
    for k,cr in enumerate((c0,c1,c2,c3)):
        t_s[rows_at(xor(k,row),feat,64),:]=cr[...]
    valid=(lax.broadcasted_iota(jnp.int32,(n,1),0)<info[4]).astype(f32)
    cot=t_s[...].T.astype(f32)*valid
    norm_ref[...]=jnp.zeros_like(norm_ref)
    norm_ref[2:3,:]=jnp.sum(cot*cent2,axis=0,keepdims=True)
    norm_ref[3:4,:]=jnp.sum(cot,axis=0,keepdims=True)
    def back(e,cent,inv):
        first=jnp.sum(e,axis=1,keepdims=True)*(1.0/width)
        second=jnp.sum(e*cent,axis=1,keepdims=True)*(1.0/width)
        return inv*(e-first-cent*second)
    grad2=back(cot*gain2,cent2,inv2)
    low=grad2.astype(bf16)
    outT_ref[...]=low.T
    f_s[...]=grad2
    def backward(j,carry):
        sl=pl.ds(pl.multiple_of(j*bw,128),bw)
        il=(mm(low,woT[:,sl])*gp_s[:,sl]).astype(bf16)
        il_ref[:,sl]=il
        f_s[...]+=mm(il,win[:,sl],NT)
        return carry
    lax.fori_loop(0,4*nb,backward,0)
    gh=f_s[...]
    norm_ref[0:1,:]=jnp.sum(gh*cent1,axis=0,keepdims=True)
    norm_ref[1:2,:]=jnp.sum(gh,axis=0,keepdims=True)
    grad1=back(gh*gain1,cent1,inv1)
    bl=grad1.astype(bf16)
    padded=jnp.concatenate([bl,jnp.zeros((n,256-feat),bf16)],axis=1)
    da=jnp.zeros((width,n),f32)
    for r in range(4):
        piece=padded[:,r*feat:r*feat+256]
        bl_ref[r]=piece
        da=da+mm(wo[r],piece,NT)
    t_s[...]=da.astype(bf16)
    for k,er in enumerate((e0,e1,e2,e3)):
        er[...]=t_s[rows_at(group_of(k),feat,64),:]
    f2=grad1.T
    for r in range(4):
        g1_ref[xor(r,row)]=f2[r*feat:(r+1)*feat]

def middle(info,attn_parts,x_own,cot_parts,ag):
    feat,n=attn_parts[0].shape; width=4*feat; ff=4*ag.shape[2]
    S=jax.ShapeDtypeStruct
    return pl.pallas_call(middle_kernel,in_specs=[SM]+[VM]*9+[HB],out_specs=[VM]*13,
        out_shape=[S((4,feat,n),bf16)]+[S((feat,n),bf16)]*4+[S((4,feat,n),f32),S((width,n),bf16),S((width,n),bf16),S((width,n),bf16),
                   S((4,n,256),bf16),S((n,ff),bf16),S((n,ff),bf16),S((8,width),f32)],
        scratch_shapes=[pltpu.VMEM((width,ff),bf16),pltpu.VMEM((width,ff),bf16),pltpu.VMEM((4,width,256),bf16),pltpu.VMEM((4,16,width),bf16),
                        pltpu.VMEM((n,ff),f32),pltpu.VMEM((width,n),bf16),pltpu.VMEM((n,width),f32),pltpu.SemaphoreType.DMA((4,))],
        compiler_params=pltpu.CompilerParams(vmem_limit_bytes=56*1024*1024),
        name="middle")(info,*attn_parts,x_own,*cot_parts,ag)

def destination(info,g,r,y):
    return (xor(g,info[5])*2+xor(y,info[6]))*4+xor(r,info[0])

def outer_grad_kernel(info, outT_ref, act_ref, keep_ref, give_ref):
    col=pl.program_id(0); y=col//2; same=(col%2)==info[3]
    half=keep_ref.shape[1]; fh=act_ref.shape[1]//2; feat=2*half
    for g in range(2):
        value=mm(outT_ref[...],act_ref[:,g*fh:(g+1)*fh]).astype(bf16)
        for ref,cond in ((keep_ref,same),(give_ref,jnp.logical_not(same))):
            @pl.when(cond)
            def _():
                for r in range(4):
                    d=destination(info,g,r,y)
                    ref[d,:,:fh]=value[r*feat:r*feat+half]
                    ref[d,:,fh:]=value[r*feat+half:(r+1)*feat]

def outer_grad(info,outT,act):
    width,n=outT.shape; ffc=act.shape[1]//4
    S=jax.ShapeDtypeStruct((16,width//8,ffc),bf16)
    whole=pl.BlockSpec((16,width//8,ffc),lambda i:(0,0,0))
    return pl.pallas_call(outer_grad_kernel,grid=(4,),in_specs=[SM,pl.BlockSpec((width,n),lambda i:(0,0)),pl.BlockSpec((n,ffc),lambda i:(0,i))],
        out_specs=[whole,whole],out_shape=[S,S],name="outer_grad")(info,outT,act)

def inner_grad_kernel(info, hidT_ref, il_ref, attnT_ref, bl_ref, norm_ref, keep_ref, give_ref):
    col=pl.program_id(0); y=col//2; same=(col%2)==info[3]
    half=hidT_ref.shape[0]//8; feat=2*half; third=half//3
    value=mm(hidT_ref[...],il_ref[...]).astype(bf16)
    rows=attnT_ref[rows_at(col,feat,64),:]
    outs=[mm(rows,bl_ref[r]).astype(bf16) for r in range(4)]
    norms=[]
    for r in range(4):
        line=jnp.concatenate([norm_ref[i:i+1,r*feat:(r+1)*feat] for i in range(4)],axis=1)
        norms.append(jnp.concatenate([line,jnp.zeros((15,line.shape[1]),f32)],axis=0).astype(bf16))
    for ref,cond in ((keep_ref,same),(give_ref,jnp.logical_not(same))):
        @pl.when(cond)
        def _():
            for g in range(2):
                for r in range(4):
                    d=destination(info,g,r,y)
                    ref[d,:half,:]=value[r*feat+g*half:r*feat+(g+1)*half]
                    for j in range(3):
                        ref[d,half:half+third,j*256:(j+1)*256]=outs[r][g*half+j*third:g*half+(j+1)*third]
                    ref[d,half+third:,:]=norms[r]

def inner_grad(info,hidT,il,attnT,bl,norm):
    width,n=hidT.shape; ffc=il.shape[1]//4; half=width//8; rows=half+half//3+16
    S=jax.ShapeDtypeStruct((16,rows,ffc),bf16)
    whole=pl.BlockSpec((16,rows,ffc),lambda i:(0,0,0)); fix=pl.BlockSpec((width,n),lambda i:(0,0))
    return pl.pallas_call(inner_grad_kernel,grid=(4,),in_specs=[SM,fix,pl.BlockSpec((n,ffc),lambda i:(0,i)),fix,pl.BlockSpec((4,n,256),lambda i:(0,0,0)),pl.BlockSpec((8,width),lambda i:(0,0))],
        out_specs=[whole,whole],out_shape=[S,S],name="inner_grad")(info,hidT,il,attnT,bl,norm)

def exchange4(blocks, axes):
    parts = [blocks[0]]
    for step in range(1, 4):
        parts.append(lax.ppermute(blocks[step], axes, [(i, i ^ step) for i in range(4)]))
    return parts


def core_swap(value):
    return lax.ppermute(value, "cc", [(0, 1), (1, 0)])


def swap_by(blocks, index):
    pairs = blocks.reshape((2, 2) + blocks.shape[1:])
    pairs = jnp.where((index // 2) == 1, pairs[::-1], pairs)
    pairs = jnp.where((index % 2) == 1, pairs[:, ::-1], pairs)
    return pairs.reshape(blocks.shape)


def dp_gather(value):
    if lax.axis_size("dp") != 2:
        return lax.all_gather(value, "dp", axis=0, tiled=True)
    other = lax.ppermute(value, "dp", [(0, 1), (1, 0)])
    first = lax.axis_index("dp") == 0
    return jnp.concatenate([jnp.where(first, value, other), jnp.where(first, other, value)], axis=0)


def dp_reduce(value):
    if lax.axis_size("dp") != 2:
        return lax.psum_scatter(value.astype(bf16), "dp", scatter_dimension=0, tiled=True).astype(f32)
    half = value.shape[0] // 2
    second = lax.axis_index("dp") == 1
    keep = jnp.where(second, value[half:], value[:half])
    send = jnp.where(second, value[:half], value[half:]).astype(bf16)
    return keep + lax.ppermute(send, "dp", [(0, 1), (1, 0)]).astype(f32)


def group_route(rounds, inverse):
    pairs = []
    for m in range(2):
        for z in range(2):
            for y in range(2):
                for c in range(2):
                    source = ((m * 2 + z) * 2 + y) * 2 + c
                    target = (((m ^ rounds[0]) * 2 + c) * 2 + y) * 2 + (z ^ rounds[1])
                    pairs.append((target, source) if inverse else (source, target))
    return pairs


def pack_outer(part):
    turned = part.T
    half = turned.shape[0] // 2
    return jnp.concatenate([turned[:half], turned[half:]], axis=1)


def unpack_outer(packed):
    wide = packed.shape[1] // 2
    return jnp.concatenate([packed[:, :wide], packed[:, wide:]], axis=0).T


def pack_output(part):
    third = part.shape[0] // 3
    padded = jnp.pad(part, ((0, 0), (0, 256 - part.shape[1])))
    return jnp.concatenate([padded[j * third : (j + 1) * third] for j in range(3)], axis=1)


def unpack_output(packed, feat):
    return jnp.concatenate([packed[:, j * 256 : j * 256 + feat] for j in range(3)], axis=0)


def pack_norms(first_gain, first_shift, second_gain, second_shift):
    line = jnp.concatenate([first_gain, first_shift, second_gain, second_shift])
    high = lax.reduce_precision(line, 8, 7)
    middle_part = lax.reduce_precision(line - high, 8, 7)
    rest = line - high - middle_part
    rows = jnp.stack([high, middle_part, rest]).astype(bf16)
    return jnp.pad(rows, ((0, 13), (0, 0)))


def gather_weights(w_output, w_inner, w_outer, norms):
    if lax.axis_size("dp") == 2:
        packed = jnp.concatenate([w_inner, pack_outer(w_outer), pack_output(w_output), norms], axis=0)
        return lax.all_gather(packed, EVERY)
    inner, outer, output = (lax.all_gather(w, "dp", axis=0, tiled=True) for w in (w_inner, w_outer, w_output))
    halves = []
    for g in range(2):
        parts = [w.reshape((2, w.shape[0] // 2) + w.shape[1:])[g] for w in (inner, outer, output)]
        halves.append(jnp.concatenate([parts[0], pack_outer(parts[1]), pack_output(parts[2]), norms], axis=0))
    whole = lax.all_gather(jnp.stack(halves), GROUP)
    return jnp.concatenate([whole[:, 0], whole[:, 1]], axis=0)


def add_parts(parts):
    total = parts[0].astype(f32)
    for part in parts[1:]:
        total = total + part.astype(f32)
    return total


def reduce_blocks(keep, give):
    got = core_swap(give)
    core = (keep.astype(f32) + got.astype(f32)).astype(bf16)
    core = core.reshape((4, 4) + core.shape[1:])
    if lax.axis_size("dp") == 2:
        plane = [add_parts(exchange4(core, ("dp", "cy"))).astype(bf16)]
    else:
        plane = []
        for g in range(2):
            other = lax.ppermute(core[2 * g + 1], "cy", [(0, 1), (1, 0)])
            plane.append(add_parts([core[2 * g], other]).astype(bf16))
    return [add_parts(exchange4(p, ROW)) for p in plane]


def local(
    tokens, w_query, w_key, w_value, w_output, w_inner, w_outer,
    first_gain, first_shift, second_gain, second_shift, seq_lengths, out_grad,
):
    feat = tokens.shape[1]
    cols = tokens.shape[2]
    half = cols // 2
    head_width = w_query.shape[1]
    two = lax.axis_size("dp") == 2
    row = lax.axis_index(ROW)
    group = lax.axis_index("dp")
    m = lax.axis_index("rm")
    z = lax.axis_index("rz")
    y = lax.axis_index("cy")
    c = lax.axis_index("cc")
    length = lax.dynamic_index_in_dim(seq_lengths[m], group, keepdims=False)
    own_start = (y * 2 + c) * cols + z * half
    info = jnp.stack([
        row, z * 2 + y, m * 2 + c, c, length - own_start, group if two else 0 * group, y, 0 * y,
    ]).astype(jnp.int32)

    weights = gather_weights(
        w_output, w_inner, w_outer, pack_norms(first_gain, first_shift, second_gain, second_shift)
    )

    def to_row_order(array):
        blocks = array.reshape(2, feat, 2, half).transpose(0, 2, 1, 3).reshape(4, feat, half)
        return swap_by(blocks, row)

    def from_row_order(parts):
        back = swap_by(jnp.stack(parts), row)
        return back.reshape(2, 2, feat, half).transpose(0, 2, 1, 3).reshape(2, feat, cols)

    x_own = jnp.stack(exchange4(to_row_order(tokens), ROW))
    xs = exchange4([x_own] * 4, SQUARE)

    qkv_rows = dp_gather(jnp.concatenate([w_query, w_key, w_value], axis=1))
    row_halves = qkv_rows.reshape(2, feat // 2, 3 * head_width)
    pieces = []
    for r1 in range(2):
        for r2 in range(2):
            part = jnp.where((z ^ r2) == 0, row_halves[0], row_halves[1])
            pieces.append(lax.ppermute(part, GROUP, group_route((r1, r2), False)))
    mine = jnp.stack(pieces)
    theirs = core_swap(mine)

    starts = []
    for kc in range(2):
        for k in range(4):
            starts.append(((y ^ (k % 2)) * 2 + (c ^ kc)) * cols + (z ^ (k // 2)) * half)
    positions = (jnp.stack(starts)[:, None] + jnp.arange(half, dtype=jnp.int32)[None, :]).reshape(-1)
    invalid = jnp.where(positions < length, 0.0, masked_score)
    bias = jnp.where(jnp.arange(HD)[:, None] == 0, invalid[None, :], 0.0).astype(bf16)
    frequency = 10000.0 ** (-2.0 * jnp.arange(HD // 2, dtype=f32) / HD)
    angles = frequency[:, None] * positions[: 4 * half].astype(f32)[None, :]
    cosine = jnp.repeat(jnp.cos(angles), 2, axis=0)
    sines = jnp.sin(angles)
    sine = jnp.stack([-sines, sines], axis=1).reshape(HD, 4 * half)

    q_rot, kv_own = qkv(info, xs, mine, theirs, cosine, sine)
    kv_other = core_swap(kv_own)
    out, log_totals, *lows = attend(q_rot, kv_own, kv_other, bias)
    attn_parts = exchange4(lows, SQUARE)
    cot_parts = exchange4(to_row_order(out_grad), ROW)
    mixed, e0, e1, e2, e3, grad_one, attn_t, hidden_t, outer_t, branch_low, act_low, inner_low, norm_sums = middle(
        info, attn_parts, x_own, cot_parts, weights
    )
    grads = exchange4([e0, e1, e2, e3], SQUARE)
    outer_sums = reduce_blocks(*outer_grad(info, outer_t, act_low))
    inner_sums = reduce_blocks(*inner_grad(info, hidden_t, inner_low, attn_t, branch_low, norm_sums))
    mixed_out = from_row_order(exchange4(mixed, ROW))

    dq, dkv_own, dkv_give = attend_back(
        q_rot, kv_own, kv_other, bias, out, log_totals, grads, cosine, sine
    )
    dkv_got = core_swap(dkv_give)
    d0, d1, d2, d3, keep, give = finish(info, dq, dkv_own, dkv_got, xs, mine, theirs, cosine, sine)
    d_x = add_parts([grad_one] + exchange4([d0, d1, d2, d3], SQUARE)).astype(bf16)
    d_input = from_row_order(exchange4(d_x, ROW)).astype(f32)

    by_round = (keep + core_swap(give).astype(f32)).astype(bf16)
    got = []
    for r1 in range(2):
        for r2 in range(2):
            got.append(
                lax.ppermute(by_round[r1 * 2 + r2], GROUP, group_route((r1, r2), True)).astype(f32)
            )
    lower = got[0] + got[2]
    upper = got[1] + got[3]
    g_qkv = dp_reduce(
        jnp.concatenate([jnp.where(z == 0, lower, upper), jnp.where(z == 0, upper, lower)], axis=0)
    )

    half_rows = feat // 2
    third = half_rows // 3
    g_outer = jnp.concatenate([unpack_outer(part) for part in outer_sums], axis=0)
    g_inner = jnp.concatenate([part[:half_rows] for part in inner_sums], axis=0)
    g_output = jnp.concatenate(
        [unpack_output(part[half_rows : half_rows + third], feat) for part in inner_sums], axis=0
    )
    g_norms = inner_sums[0][half_rows + third].reshape(4, feat)
    if not two:
        g_outer, g_inner, g_output = (
            lax.psum_scatter(g.astype(bf16), "dp", scatter_dimension=0, tiled=True).astype(f32)
            for g in (g_outer, g_inner, g_output)
        )
        g_norms = lax.psum(g_norms, "dp")

    return (
        mixed_out, d_input,
        g_qkv[:, :head_width], g_qkv[:, head_width : 2 * head_width], g_qkv[:, 2 * head_width :],
        g_output, g_inner, g_outer,
        g_norms[0], g_norms[1], g_norms[2], g_norms[3],
    )


def solution(mesh):
    shape = mesh.devices.shape
    fine = Mesh(mesh.devices.reshape(shape[0], 2, shape[1] // 2, 2, shape[2] // 2), EVERY)
    col = ("cy", "cc")
    acts = P(None, ROW, ("dp",) + col)
    by_row = P(ROW + ("dp",), col)
    by_col = P(col + ("dp",), ROW)
    vec = P(ROW)
    return jax.shard_map(
        local,
        mesh=fine,
        in_specs=(
            acts, by_row, by_row, by_row, by_col, by_row, by_col, vec, vec, vec, vec, P(), acts,
        ),
        out_specs=(
            acts, acts, by_row, by_row, by_row, by_col, by_row, by_col, vec, vec, vec, vec,
        ),
        check_vma=False,
    )
```

```python
import functools

import jax
import jax.numpy as jnp
from jax import lax
from jax.experimental import pallas as pl
from jax.experimental.pallas import tpu as pltpu
from jax.sharding import Mesh, PartitionSpec as P

HD = 64
EVERY = ("dp", "rm", "rz", "cy", "cc")
GROUP = ("rm", "rz", "cy", "cc")
ROW = ("rm", "rz")
SQUARE = ("rz", "cy")
bf16=jnp.bfloat16; f32=jnp.float32
LOG2E=1.4426950408889634
LN2=0.6931471805599453
masked_score=-1e30

def mm(a,b,dims=((1,),(0,))):
    return lax.dot_general(a,b,(dims,((),())),preferred_element_type=f32)
NT=((1,),(1,))

def pair_turn(values, cosine, signed_sine):
    shape = values.shape
    v3 = values.reshape(shape[0]//8, 8, shape[1])
    up = pltpu.roll(v3, 7, 1); down = pltpu.roll(v3, 1, 1)
    even = (lax.broadcasted_iota(jnp.int32, v3.shape, 1) % 2) == 0
    other = jnp.where(even, up, down).reshape(shape)
    return values*cosine + other*signed_sine

KB=1024
QB=2
def one_row(shape, dtype, value=1.0):
    return jnp.where(lax.broadcasted_iota(jnp.int32, shape, 0)==0, value, 0.0).astype(dtype)

def attend_kernel(q_ref, ko_ref, vo_ref, kx_ref, vx_ref, bias_ref, o_ref, lse_ref, l0, l1, l2, l3, kaug, vall):
    head=pl.program_id(0); qb=pl.program_id(1)
    span=ko_ref.shape[1]
    @pl.when(qb==0)
    def _():
        for part,(kr,vr) in enumerate(((ko_ref,vo_ref),(kx_ref,vx_ref))):
            aug=jnp.concatenate([kr[...], bias_ref[:, part*span:(part+1)*span]],axis=0)
            kaug[part*span:(part+1)*span,:]=aug.T
            vall[:, part*span:(part+1)*span]=vr[...]
    n=q_ref.shape[1]
    qaug=jnp.concatenate([q_ref[...], one_row((HD,n),bf16)],axis=0)
    top=jnp.full((1,n),-3e38,f32); total=jnp.zeros((1,n),f32); acc=jnp.zeros((HD,n),f32)
    s=mm(kaug[0:KB,:],qaug)
    for kb in range(0,2*span,KB):
        following=mm(kaug[kb+KB:kb+2*KB,:],qaug) if kb+KB<2*span else None
        new=jnp.maximum(top,jnp.max(s,axis=0,keepdims=True))
        alpha=jnp.exp2(top-new)
        p=jnp.exp2(s-new)
        total=total*alpha+jnp.sum(p,axis=0,keepdims=True)
        acc=acc*alpha+mm(vall[:,kb:kb+KB],p.astype(bf16))
        top=new
        s=following
    out=acc/total
    o_ref[...]=out
    lse_ref[0]=top+jnp.log2(total)
    low=out.astype(bf16)
    part=n//QB
    for k,ref in enumerate((l0,l1,l2,l3)):
        @pl.when(qb==k//QB)
        def _(): ref[pl.ds(pl.multiple_of(head*HD,HD),HD),:]=low[:,(k%QB)*part:(k%QB+1)*part]

def attend(q,kv,kvx,bias):
    width,n4=q.shape; heads=width//HD; n=n4//4*QB; span=kv.shape[1]
    kspec=pl.BlockSpec((HD,span),lambda h,b:(h,0)); vspec=pl.BlockSpec((HD,span),lambda h,b:(heads+h,0))
    lowspec=pl.BlockSpec((width,n4//4),lambda h,b:(0,0))
    return pl.pallas_call(attend_kernel,grid=(heads,4//QB),
        in_specs=[pl.BlockSpec((HD,n),lambda h,b:(h,b)),kspec,vspec,kspec,vspec,pl.BlockSpec((HD,2*span),lambda h,b:(0,0))],
        out_specs=[pl.BlockSpec((HD,n),lambda h,b:(h,b)),pl.BlockSpec((1,1,n),lambda h,b:(h,0,b))]+[lowspec]*4,
        out_shape=[jax.ShapeDtypeStruct((width,n4),f32),jax.ShapeDtypeStruct((heads,1,n4),f32)]+[jax.ShapeDtypeStruct((width,n4//4),bf16)]*4,
        scratch_shapes=[pltpu.VMEM((2*span,2*HD),bf16),pltpu.VMEM((HD,2*span),bf16)],
        cost_estimate=pl.CostEstimate(flops=4*width*n4//HD*2*span*256,bytes_accessed=4*n4*2*span,transcendentals=heads*n4*2*span),
        name="attend")(q,kv,kv,kvx,kvx,bias)

BKB=512
def attend_back_kernel(q_ref, ko_ref, vo_ref, kx_ref, vx_ref, bias_ref, o_ref, lse_ref, g0,g1,g2,g3, cos_ref, sin_ref,
                       dq_ref, own_ref, give_ref, kaug, vtm, kall, acc):
    qb=pl.program_id(0)
    span=ko_ref.shape[1]; n=q_ref.shape[1]
    @pl.when(qb==0)
    def _():
        for part,(kr,vr) in enumerate(((ko_ref,vo_ref),(kx_ref,vx_ref))):
            sl=slice(part*span,(part+1)*span)
            kaug[sl,:]=jnp.concatenate([kr[...], bias_ref[:, sl]],axis=0).T
            vtm[sl,:]=jnp.concatenate([vr[...], jnp.zeros((HD,span),bf16)],axis=0).T
            kall[:,sl]=kr[...]
        acc[...]=jnp.zeros_like(acc)
    q=q_ref[...]
    zeros=jnp.zeros((HD,n),bf16)
    qaug=jnp.concatenate([q, one_row((HD,n),bf16)],axis=0)
    g=jnp.concatenate([jnp.where(qb==0,g0[...],g2[...]),jnp.where(qb==0,g1[...],g3[...])],axis=1)
    qpad=jnp.concatenate([q,zeros],axis=0).T
    gpad=jnp.concatenate([zeros,g],axis=0).T
    gaug=jnp.concatenate([g,zeros],axis=0)
    delta=jnp.sum(g.astype(f32)*o_ref[...],axis=0,keepdims=True)
    lse=lse_ref[0]
    dq=jnp.zeros((HD,n),f32)
    s=mm(kaug[0:BKB,:],qaug); dp=mm(vtm[0:BKB,:],gaug)
    for kb in range(0,2*span,BKB):
        last=kb+BKB>=2*span
        s_next=None if last else mm(kaug[kb+BKB:kb+2*BKB,:],qaug)
        dp_next=None if last else mm(vtm[kb+BKB:kb+2*BKB,:],gaug)
        p=jnp.exp2(s-lse)
        ds=(p*(dp-delta)).astype(bf16)
        dq=dq+mm(kall[:,kb:kb+BKB],ds)
        acc[kb:kb+BKB,:]=acc[kb:kb+BKB,:]+mm(ds,qpad)+mm(p.astype(bf16),gpad)
        s=s_next; dp=dp_next
    dq_ref[...]=pair_turn(dq*(HD**-0.5),cos_ref[...],-sin_ref[...]).astype(bf16)
    @pl.when(qb==4//QB-1)
    def _():
        own_ref[...]=acc[:span,:]
        give_ref[...]=acc[span:,:].astype(bf16)

def attend_back(head,q,kv,kvx,bias,o,lse,grads,cos,sin):
    width,n4=q.shape; heads=width//HD; n=n4//4*QB; span=kv.shape[1]
    kspec=pl.BlockSpec((HD,span),lambda b:(head,0)); vspec=pl.BlockSpec((HD,span),lambda b:(heads+head,0))
    gspec=pl.BlockSpec((HD,n4//4),lambda b:(head,0)); hb=pl.BlockSpec((HD,n),lambda b:(head,b)); tb=pl.BlockSpec((HD,n),lambda b:(0,b))
    dspec=pl.BlockSpec((span,2*HD),lambda b:(0,0))
    return pl.pallas_call(attend_back_kernel,grid=(4//QB,),
        in_specs=[hb,kspec,vspec,kspec,vspec,pl.BlockSpec((HD,2*span),lambda b:(0,0)),hb,pl.BlockSpec((1,1,n),lambda b:(head,0,b)),gspec,gspec,gspec,gspec,tb,tb],
        out_specs=[tb,dspec,dspec],
        out_shape=[jax.ShapeDtypeStruct((HD,n4),bf16),jax.ShapeDtypeStruct((span,2*HD),f32),jax.ShapeDtypeStruct((span,2*HD),bf16)],
        scratch_shapes=[pltpu.VMEM((2*span,2*HD),bf16),pltpu.VMEM((2*span,2*HD),bf16),pltpu.VMEM((HD,2*span),bf16),pltpu.VMEM((2*span,2*HD),f32)],
        cost_estimate=pl.CostEstimate(flops=10*n4*2*span*256,bytes_accessed=4*n4*2*span,transcendentals=n4*2*span),
        name="attend_back")(q,kv,kv,kvx,kvx,bias,o,lse,*grads,cos,sin)
def xor(a,b):
    return lax.bitwise_xor(jnp.asarray(a,jnp.int32),jnp.asarray(b,jnp.int32))

def rows_at(index,size,align):
    return pl.ds(pl.multiple_of(index*size,align),size)

def place_qkv_weights(info, mine_ref, theirs_ref, w_s):
    c=info[3]; mc=info[2]
    half=mine_ref.shape[1]
    for r in range(4):
        a=mine_ref[xor(r,mc)]; b=theirs_ref[xor(r,xor(mc,1))]
        for h in range(2):
            w_s[(2*r+h)*half:(2*r+h+1)*half,:]=jnp.where(c==h,a,b)

def place_tokens(info, x_ref, kz, x_s):
    feat=x_ref.shape[1]; base=xor(info[0],kz)
    for r in range(4):
        x_s[r*feat:(r+1)*feat,:]=x_ref[xor(r,base)]

def qkv_kernel(info, x0,x1,x2,x3, mine_ref, theirs_ref, cos_ref, sin_ref, q_ref, kv_ref, w_s, wt_s, x_s):
    place_qkv_weights(info,mine_ref,theirs_ref,w_s)
    wt_s[...]=w_s[...].T
    hw=q_ref.shape[0]; n=x0.shape[2]
    for k,xr in enumerate((x0,x1,x2,x3)):
        place_tokens(info,xr,k//2,x_s)
        out=mm(wt_s[...],x_s[...])
        sl=slice(k*n,(k+1)*n)
        cos=cos_ref[:,sl]; sin=sin_ref[:,sl]
        for h in range(2*hw//HD):
            turned=pair_turn(out[h*HD:(h+1)*HD],cos,sin)
            if h*HD<hw: q_ref[h*HD:(h+1)*HD,sl]=(turned*(HD**-0.5*LOG2E)).astype(bf16)
            else: kv_ref[h*HD-hw:(h+1)*HD-hw,sl]=turned.astype(bf16)
        kv_ref[hw:,sl]=out[2*hw:].astype(bf16)

VM=pl.BlockSpec(memory_space=pltpu.VMEM)
SM=pl.BlockSpec(memory_space=pltpu.SMEM)
HB=pl.BlockSpec(memory_space=pl.ANY)

def qkv(info,xs,mine,theirs,cos,sin):
    _,feat,n=xs[0].shape; w3=mine.shape[2]; hw=w3//3; width=4*feat
    return pl.pallas_call(qkv_kernel,in_specs=[SM]+[VM]*8,out_specs=[VM,VM],
        out_shape=[jax.ShapeDtypeStruct((hw,4*n),bf16),jax.ShapeDtypeStruct((2*hw,4*n),bf16)],
        scratch_shapes=[pltpu.VMEM((width,w3),bf16),pltpu.VMEM((w3,width),bf16),pltpu.VMEM((width,n),bf16)],
        name="qkv")(info,*xs,mine,theirs,cos,sin)

def finish_dx_kernel(info, *refs):
    heads=refs[0].shape[0]
    del heads
    (q0,q1,q2,o0,o1,o2,r0,r1,r2,mine_ref,theirs_ref,cos_ref,sin_ref,d0,d1,d2,d3,p_ref,w_s)=refs
    hw=3*HD; n=d0.shape[2]; feat=d0.shape[1]
    place_qkv_weights(info,mine_ref,theirs_ref,w_s)
    for h,(qr,orr,rr) in enumerate(((q0,o0,r0),(q1,o1,r1),(q2,o2,r2))):
        p_ref[h*HD:(h+1)*HD,:]=qr[...]
        t=(orr[...]+rr[...].astype(f32)).T
        p_ref[hw+h*HD:hw+(h+1)*HD,:]=pair_turn(t[:HD]*LN2,cos_ref[...],-sin_ref[...]).astype(bf16)
        p_ref[2*hw+h*HD:2*hw+(h+1)*HD,:]=t[HD:].astype(bf16)
    for k,dr in ((3,d3),(1,d1),(2,d2),(0,d0)):
        sl=slice(k*n,(k+1)*n)
        base=xor(info[0],k//2)
        for r in range(4):
            dr[xor(r,base)]=mm(w_s[r*feat:(r+1)*feat,:],p_ref[:,sl]).astype(dr.dtype)

def finish_dx(info,dqs,owns,gots,mine,theirs,cos,sin):
    w3=mine.shape[2]; half=mine.shape[1]; feat=2*half; width=4*feat; n=dqs[0].shape[1]//4
    S=jax.ShapeDtypeStruct
    return pl.pallas_call(finish_dx_kernel,in_specs=[SM]+[VM]*13,out_specs=[VM]*5,
        out_shape=[S((4,feat,n),f32)]+[S((4,feat,n),bf16)]*3+[S((w3,4*n),bf16)],
        scratch_shapes=[pltpu.VMEM((width,w3),bf16)],
        cost_estimate=pl.CostEstimate(flops=8*width*w3*n,bytes_accessed=8*width*n*4,transcendentals=0),
        name="finish_dx")(info,*dqs,*owns,*gots,mine,theirs,cos,sin)

def finish_dw_kernel(info, p_ref, x0,x1,x2,x3, keep_ref, give_ref, x_s, g_s):
    n=x0.shape[2]; half=keep_ref.shape[1]
    for k,xr in enumerate((x0,x1,x2,x3)):
        place_tokens(info,xr,k//2,x_s.at[:,k*n:(k+1)*n])
    g_s[...]=mm(x_s[...],p_ref[...],NT)
    c=info[3]; mc=info[2]
    for r in range(4):
        mine_rows=pl.ds(pl.multiple_of((2*r+c)*half,32),half); their_rows=pl.ds(pl.multiple_of((2*r+1-c)*half,32),half)
        keep_ref[xor(r,mc)]=g_s[mine_rows,:]
        give_ref[xor(r,xor(mc,1))]=g_s[their_rows,:].astype(bf16)

def finish_dw(info,proj,xs):
    _,feat,n=xs[0].shape; w3=proj.shape[0]; width=4*feat; half=feat//2
    return pl.pallas_call(finish_dw_kernel,in_specs=[SM]+[VM]*5,out_specs=[VM]*2,
        out_shape=[jax.ShapeDtypeStruct((4,half,w3),f32),jax.ShapeDtypeStruct((4,half,w3),bf16)],
        scratch_shapes=[pltpu.VMEM((width,4*n),bf16),pltpu.VMEM((width,w3),f32)],
        cost_estimate=pl.CostEstimate(flops=8*width*w3*n,bytes_accessed=8*width*n*2,transcendentals=0),
        name="finish_dw")(info,proj,*xs)

def middle_kernel(info, a0,a1,a2,a3, x_ref, c0,c1,c2,c3, *refs):
    chunk_a=refs[:10]; chunk_b=refs[10:20]
    (mixed_ref, e0,e1,e2,e3, g1_ref, attnT_ref, hidT_ref, outT_ref, bl_ref, act_ref, il_ref, norm_ref,
                  win, woT, wo, ns, gp_s, t_s, f_s, sems)=refs[20:]
    row=info[0]; zy=info[1]; c=info[3]; group=info[5]; y=info[6]
    feat=a0.shape[0]; n=a0.shape[1]; width=4*feat; ffc=chunk_a[0].shape[2]; half=feat//2; fh=ffc//2; third=half//3
    def go(src,dst,s): pltpu.make_async_copy(src,dst,sems.at[s]).start()
    spots=((0,0,0),(0,1,0),(0,0,1),(0,1,1),(2,1,1))
    def each(chunk):
        for kc in range(2):
            for ref,(first,kx,ky) in zip(chunk[5*kc:5*kc+5],spots):
                g=xor(group,kx); col=xor(y,ky)*2+xor(c,kc)
                for i in range(ref.shape[0]):
                    yield ref.at[i],xor(row,first+i),g,col,(kc,kx,ky,first+i)
    for ref,r,g,col,_ in each(chunk_a):
        for j in range(3):
            go(ref.at[half:half+third,j*256:(j+1)*256],wo.at[r,pl.ds(pl.multiple_of((col*2+g)*half+j*third,16),third),:],0)
    for ref,r,g,col,where in each(chunk_a):
        if where[:3]==(0,0,0):
            go(ref.at[half+third:half+third+16,:],ns.at[r],3)
    for ref,r,g,col,_ in each(chunk_a):
        go(ref.at[0:half,:],win.at[pl.ds(pl.multiple_of(r*feat+g*half,16),half),pl.ds(pl.multiple_of(col*ffc,128),ffc)],1)
    for ref,r,g,col,_ in each(chunk_b):
        for t in range(2):
            go(ref.at[:,t*fh:(t+1)*fh],woT.at[pl.ds(pl.multiple_of(r*feat+t*half,16),half),pl.ds(pl.multiple_of((col*2+g)*fh,128),fh)],2)
    def group_of(k):
        other=xor(zy,k)
        return (other%2)*2+other//2
    for k,ar in enumerate((a0,a1,a2,a3)):
        attnT_ref[rows_at(group_of(k),feat,64),:]=ar[...]
    for i in range(4):
        t_s[rows_at(xor(i,row),feat,64),:]=x_ref[i]
    attn=attnT_ref[...].T
    x=t_s[...].T.astype(f32)
    pltpu.make_async_copy(wo,wo,sems.at[0]).wait()
    pltpu.make_async_copy(ns,ns,sems.at[3]).wait()
    def vector(which):
        out=[]
        for r in range(4):
            v=ns[r].astype(f32)[0:3,which*feat:(which+1)*feat]
            out.append(jnp.sum(v,axis=0,keepdims=True))
        return jnp.concatenate(out,axis=1)
    gain1=vector(0); shift1=vector(1); gain2=vector(2); shift2=vector(3)
    branch=jnp.concatenate([mm(attn,wo[r])[:,:feat] for r in range(4)],axis=1)
    def stats(v):
        mean=jnp.sum(v,axis=1,keepdims=True)*(1.0/width)
        var=jnp.sum(v*v,axis=1,keepdims=True)*(1.0/width)-mean*mean
        inv=lax.rsqrt(var+1e-5)
        return (v-mean)*inv,inv
    cent1,inv1=stats(x+branch)
    hidden=cent1*gain1+shift1
    hid=hidden.astype(bf16)
    hidT_ref[...]=hid.T
    pltpu.make_async_copy(win,win,sems.at[1]).wait()
    pltpu.make_async_copy(woT,woT,sems.at[2]).wait()
    f_s[...]=jnp.zeros_like(f_s)
    nb=2; bw=ffc//nb
    def forward(j,carry):
        sl=pl.ds(pl.multiple_of(j*bw,128),bw)
        inner=mm(hid,win[:,sl])
        cdf=0.5+0.5*lax.erf(inner*0.7071067811865476)
        act=(inner*cdf).astype(bf16)
        gp_s[:,sl]=cdf+inner*(jnp.exp(inner*inner*-0.5)*0.3989422804014327)
        act_ref[:,sl]=act
        f_s[...]+=mm(act,woT[:,sl],NT)
        return carry
    lax.fori_loop(0,4*nb,forward,0)
    cent2,inv2=stats(hidden+f_s[...])
    t_s[...]=(cent2*gain2+shift2).astype(bf16).T
    for i in range(4):
        mixed_ref[i]=t_s[rows_at(xor(i,row),feat,64),:]
    for k,cr in enumerate((c0,c1,c2,c3)):
        t_s[rows_at(xor(k,row),feat,64),:]=cr[...]
    valid=(lax.broadcasted_iota(jnp.int32,(n,1),0)<info[4]).astype(f32)
    cot=t_s[...].T.astype(f32)*valid
    norm_ref[...]=jnp.zeros_like(norm_ref)
    norm_ref[2:3,:]=jnp.sum(cot*cent2,axis=0,keepdims=True)
    norm_ref[3:4,:]=jnp.sum(cot,axis=0,keepdims=True)
    def back(e,cent,inv):
        first=jnp.sum(e,axis=1,keepdims=True)*(1.0/width)
        second=jnp.sum(e*cent,axis=1,keepdims=True)*(1.0/width)
        return inv*(e-first-cent*second)
    grad2=back(cot*gain2,cent2,inv2)
    low=grad2.astype(bf16)
    outT_ref[...]=low.T
    f_s[...]=grad2
    def backward(j,carry):
        sl=pl.ds(pl.multiple_of(j*bw,128),bw)
        il=(mm(low,woT[:,sl])*gp_s[:,sl]).astype(bf16)
        il_ref[:,sl]=il
        f_s[...]+=mm(il,win[:,sl],NT)
        return carry
    lax.fori_loop(0,4*nb,backward,0)
    gh=f_s[...]
    norm_ref[0:1,:]=jnp.sum(gh*cent1,axis=0,keepdims=True)
    norm_ref[1:2,:]=jnp.sum(gh,axis=0,keepdims=True)
    grad1=back(gh*gain1,cent1,inv1)
    bl=grad1.astype(bf16)
    padded=jnp.concatenate([bl,jnp.zeros((n,256-feat),bf16)],axis=1)
    da=jnp.zeros((width,n),f32)
    for r in range(4):
        piece=padded[:,r*feat:r*feat+256]
        bl_ref[r]=piece
        da=da+mm(wo[r],piece,NT)
    t_s[...]=da.astype(bf16)
    for k,er in enumerate((e0,e1,e2,e3)):
        er[...]=t_s[rows_at(group_of(k),feat,64),:]
    f2=grad1.T
    for r in range(4):
        g1_ref[xor(r,row)]=f2[r*feat:(r+1)*feat]

def middle(info,attn_parts,x_own,cot_parts,chunk_a,chunk_b):
    feat,n=attn_parts[0].shape; width=4*feat; ff=4*chunk_a[0].shape[2]
    S=jax.ShapeDtypeStruct
    return pl.pallas_call(middle_kernel,in_specs=[SM]+[VM]*9+[HB]*20,out_specs=[VM]*13,
        out_shape=[S((4,feat,n),bf16)]+[S((feat,n),bf16)]*4+[S((4,feat,n),f32),S((width,n),bf16),S((width,n),bf16),S((width,n),bf16),
                   S((4,n,256),bf16),S((n,ff),bf16),S((n,ff),bf16),S((8,width),f32)],
        scratch_shapes=[pltpu.VMEM((width,ff),bf16),pltpu.VMEM((width,ff),bf16),pltpu.VMEM((4,width,256),bf16),pltpu.VMEM((4,16,width),bf16),
                        pltpu.VMEM((n,ff),f32),pltpu.VMEM((width,n),bf16),pltpu.VMEM((n,width),f32),pltpu.SemaphoreType.DMA((4,))],
        compiler_params=pltpu.CompilerParams(vmem_limit_bytes=56*1024*1024),
        cost_estimate=pl.CostEstimate(flops=12*n*width*ff*2,bytes_accessed=24*width*ff,transcendentals=2*n*ff),
        name="middle")(info,*attn_parts,x_own,*cot_parts,*chunk_a,*chunk_b)

def outer_grad_kernel(info, outT_ref, act_ref, out_ref):
    half=out_ref.shape[3]; fh=act_ref.shape[1]//2; feat=2*half
    for g in range(2):
        gk=xor(g,info[5])
        for r in range(4):
            value=mm(outT_ref[r*feat:(r+1)*feat,:],act_ref[:,g*fh:(g+1)*fh]).astype(bf16)
            rk=xor(r,info[0])
            out_ref[gk,0,rk,:,:fh]=value[:half]
            out_ref[gk,0,rk,:,fh:]=value[half:]

def column(info,ky,which):
    return xor(info[6],ky)*2+xor(info[3],which)

def outer_grad(which,info,outT,act):
    width,n=outT.shape; ffc=act.shape[1]//4
    return pl.pallas_call(outer_grad_kernel,
        grid_spec=pltpu.PrefetchScalarGridSpec(num_scalar_prefetch=1,grid=(2,),
            in_specs=[pl.BlockSpec((width,n),lambda i,s:(0,0)),pl.BlockSpec((n,ffc),lambda i,s:(0,column(s,i,which)))],
            out_specs=pl.BlockSpec((2,1,4,width//8,ffc),lambda i,s:(0,i,0,0,0))),
        out_shape=jax.ShapeDtypeStruct((2,2,4,width//8,ffc),bf16),
        cost_estimate=pl.CostEstimate(flops=4*width*n*ffc,bytes_accessed=8*width*ffc,transcendentals=0),name="outer_grad")(info,outT,act)

def inner_grad_kernel(which, info, hidT_ref, il_ref, attnT_ref, bl_ref, norm_ref, out_ref):
    col=column(info,pl.program_id(0),which)
    half=hidT_ref.shape[0]//8; feat=2*half; third=half//3
    rows=attnT_ref[rows_at(col,feat,64),:]
    for r in range(4):
        rk=xor(r,info[0])
        value=mm(hidT_ref[r*feat:(r+1)*feat,:],il_ref[...]).astype(bf16)
        outs=mm(rows,bl_ref[r]).astype(bf16)
        line=jnp.concatenate([norm_ref[i:i+1,r*feat:(r+1)*feat] for i in range(4)],axis=1)
        norms=jnp.concatenate([line,jnp.zeros((15,line.shape[1]),f32)],axis=0).astype(bf16)
        for g in range(2):
            gk=xor(g,info[5])
            out_ref[gk,0,rk,:half,:]=value[g*half:(g+1)*half]
            for j in range(3):
                out_ref[gk,0,rk,half:half+third,j*256:(j+1)*256]=outs[g*half+j*third:g*half+(j+1)*third]
            out_ref[gk,0,rk,half+third:,:]=norms

def inner_grad(which,info,hidT,il,attnT,bl,norm):
    width,n=hidT.shape; ffc=il.shape[1]//4; half=width//8; rows=half+half//3+16
    fix=pl.BlockSpec((width,n),lambda i,s:(0,0))
    return pl.pallas_call(functools.partial(inner_grad_kernel,which),
        grid_spec=pltpu.PrefetchScalarGridSpec(num_scalar_prefetch=1,grid=(2,),
            in_specs=[fix,pl.BlockSpec((n,ffc),lambda i,s:(0,column(s,i,which))),fix,pl.BlockSpec((4,n,256),lambda i,s:(0,0,0)),pl.BlockSpec((8,width),lambda i,s:(0,0))],
            out_specs=pl.BlockSpec((2,1,4,rows,ffc),lambda i,s:(0,i,0,0,0))),
        out_shape=jax.ShapeDtypeStruct((2,2,4,rows,ffc),bf16),
        cost_estimate=pl.CostEstimate(flops=6*width*n*ffc,bytes_accessed=8*width*ffc,transcendentals=0),name="inner_grad")(info,hidT,il,attnT,bl,norm)

def exchange4(blocks, axes):
    parts = [blocks[0]]
    for step in range(1, 4):
        parts.append(lax.ppermute(blocks[step], axes, [(i, i ^ step) for i in range(4)]))
    return parts


def core_swap(value):
    return lax.ppermute(value, "cc", [(0, 1), (1, 0)])


def swap_by(blocks, index):
    pairs = blocks.reshape((2, 2) + blocks.shape[1:])
    pairs = jnp.where((index // 2) == 1, pairs[::-1], pairs)
    pairs = jnp.where((index % 2) == 1, pairs[:, ::-1], pairs)
    return pairs.reshape(blocks.shape)


def dp_gather(value):
    if lax.axis_size("dp") != 2:
        return lax.all_gather(value, "dp", axis=0, tiled=True)
    other = lax.ppermute(value, "dp", [(0, 1), (1, 0)])
    first = lax.axis_index("dp") == 0
    return jnp.concatenate([jnp.where(first, value, other), jnp.where(first, other, value)], axis=0)


def dp_reduce(value):
    if lax.axis_size("dp") != 2:
        return lax.psum_scatter(value.astype(bf16), "dp", scatter_dimension=0, tiled=True).astype(f32)
    half = value.shape[0] // 2
    second = lax.axis_index("dp") == 1
    keep = jnp.where(second, value[half:], value[:half])
    send = jnp.where(second, value[:half], value[half:]).astype(bf16)
    return keep + lax.ppermute(send, "dp", [(0, 1), (1, 0)]).astype(f32)


def group_route(rounds, inverse):
    pairs = []
    for m in range(2):
        for z in range(2):
            for y in range(2):
                for c in range(2):
                    source = ((m * 2 + z) * 2 + y) * 2 + c
                    target = (((m ^ rounds[0]) * 2 + c) * 2 + y) * 2 + (z ^ rounds[1])
                    pairs.append((target, source) if inverse else (source, target))
    return pairs


def pack_outer(part):
    turned = part.T
    half = turned.shape[0] // 2
    return jnp.concatenate([turned[:half], turned[half:]], axis=1)


def unpack_outer(packed):
    wide = packed.shape[1] // 2
    return jnp.concatenate([packed[:, :wide], packed[:, wide:]], axis=0).T


def pack_output(part):
    third = part.shape[0] // 3
    padded = jnp.pad(part, ((0, 0), (0, 256 - part.shape[1])))
    return jnp.concatenate([padded[j * third : (j + 1) * third] for j in range(3)], axis=1)


def unpack_output(packed, feat):
    return jnp.concatenate([packed[:, j * 256 : j * 256 + feat] for j in range(3)], axis=0)


def pack_norms(first_gain, first_shift, second_gain, second_shift):
    line = jnp.concatenate([first_gain, first_shift, second_gain, second_shift])
    high = lax.reduce_precision(line, 8, 7)
    middle_part = lax.reduce_precision(line - high, 8, 7)
    rest = line - high - middle_part
    rows = jnp.stack([high, middle_part, rest]).astype(bf16)
    return jnp.pad(rows, ((0, 13), (0, 0)))


def after(value, *earlier):
    return lax.optimization_barrier((value,) + earlier)[0]


def swap2(value, axis):
    return lax.ppermute(value, axis, [(0, 1), (1, 0)])


def row_stack(block):
    return jnp.stack(exchange4([block] * 4, ROW))


def plane_and_core(own_row):
    along_x = swap2(own_row, "dp")
    along_y = swap2(own_row, "cy")
    across_low = swap2(along_x[:2], "cy")
    across_high = swap2(along_y[2:], "dp")
    arrays = [own_row, along_x, along_y, across_low, across_high]
    return arrays + [core_swap(array) for array in arrays]


def gather_generic(w_output, w_inner, w_outer, norms, row, y, c):
    inner, outer, output = (lax.all_gather(w, "dp", axis=0, tiled=True) for w in (w_inner, w_outer, w_output))
    chunks = []
    for which in range(2):
        halves = []
        for g in range(2):
            parts = [w.reshape((2, w.shape[0] // 2) + w.shape[1:])[g] for w in (inner, outer, output)]
            if which == 0:
                halves.append(jnp.concatenate([parts[0], pack_output(parts[2]), norms], axis=0))
            else:
                halves.append(pack_outer(parts[1]))
        whole = lax.all_gather(jnp.stack(halves), GROUP)
        arrays = []
        for kc in range(2):
            for kx, ky, rows in ((0, 0, (0, 1, 2, 3)), (1, 0, (0, 1, 2, 3)), (0, 1, (0, 1, 2, 3)), (1, 1, (0, 1)), (1, 1, (2, 3))):
                spots = jnp.stack([(row ^ k) * 4 + (y ^ ky) * 2 + (c ^ kc) for k in rows])
                arrays.append(jnp.take(whole[:, kx], spots, axis=0))
        chunks.append(arrays)
    return chunks


def add_parts(parts):
    total = parts[0].astype(f32)
    for part in parts[1:]:
        total = total + part.astype(f32)
    return total


def start_sums(keep, got):
    def part(kx, ky, rows):
        return (keep[kx, ky, rows].astype(f32) + got[kx, ky, rows].astype(f32)).astype(bf16)

    everything = slice(0, 4)
    return (
        part(0, 0, everything), part(1, 0, everything), part(0, 1, everything),
        part(1, 1, slice(0, 2)), part(1, 1, slice(2, 4)),
    )


def second_sums(sums, to_x, to_y):
    own, along_x, along_y, _, _ = sums
    x_sum = jnp.concatenate([along_x[:2], (along_x[2:].astype(f32) + to_y.astype(f32)).astype(bf16)], axis=0)
    y_sum = jnp.concatenate([(along_y[:2].astype(f32) + to_x.astype(f32)).astype(bf16), along_y[2:]], axis=0)
    return own, x_sum, y_sum


def generic_sums(keep, got):
    core = (keep.astype(f32) + got.astype(f32)).astype(bf16)
    planes = [add_parts([core[g, 0], core_y]).astype(bf16) for g in range(2) for core_y in [swap2(core[g, 1], "cy")]]
    return [add_parts(exchange4(plane, ROW)) for plane in planes]


def local(
    tokens, w_query, w_key, w_value, w_output, w_inner, w_outer,
    first_gain, first_shift, second_gain, second_shift, seq_lengths, out_grad,
):
    feat = tokens.shape[1]
    cols = tokens.shape[2]
    half = cols // 2
    head_width = w_query.shape[1]
    two = lax.axis_size("dp") == 2
    row = lax.axis_index(ROW)
    group = lax.axis_index("dp")
    m = lax.axis_index("rm")
    z = lax.axis_index("rz")
    y = lax.axis_index("cy")
    c = lax.axis_index("cc")
    length = lax.dynamic_index_in_dim(seq_lengths[m], group, keepdims=False)
    own_start = (y * 2 + c) * cols + z * half
    info = jnp.stack([
        row, z * 2 + y, m * 2 + c, c, length - own_start, group if two else 0 * group, y, 0 * y,
    ]).astype(jnp.int32)

    def to_row_order(array):
        blocks = array.reshape(2, feat, 2, half).transpose(0, 2, 1, 3).reshape(4, feat, half)
        return swap_by(blocks, row)

    def from_row_order(parts):
        back = swap_by(jnp.stack(parts), row)
        return back.reshape(2, 2, feat, half).transpose(0, 2, 1, 3).reshape(2, feat, cols)

    x_own = jnp.stack(exchange4(to_row_order(tokens), ROW))
    xs = exchange4([x_own] * 4, SQUARE)

    qkv_rows = dp_gather(jnp.concatenate([w_query, w_key, w_value], axis=1))
    row_halves = qkv_rows.reshape(2, feat // 2, 3 * head_width)
    pieces = []
    for r1 in range(2):
        for r2 in range(2):
            part = jnp.where((z ^ r2) == 0, row_halves[0], row_halves[1])
            pieces.append(lax.ppermute(part, GROUP, group_route((r1, r2), False)))
    mine = jnp.stack(pieces)
    theirs = core_swap(mine)

    starts = []
    for kc in range(2):
        for k in range(4):
            starts.append(((y ^ (k % 2)) * 2 + (c ^ kc)) * cols + (z ^ (k // 2)) * half)
    positions = (jnp.stack(starts)[:, None] + jnp.arange(half, dtype=jnp.int32)[None, :]).reshape(-1)
    invalid = jnp.where(positions < length, 0.0, masked_score)
    bias = jnp.where(jnp.arange(HD)[:, None] == 0, invalid[None, :], 0.0).astype(bf16)
    frequency = 10000.0 ** (-2.0 * jnp.arange(HD // 2, dtype=f32) / HD)
    angles = frequency[:, None] * positions[: 4 * half].astype(f32)[None, :]
    cosine = jnp.repeat(jnp.cos(angles), 2, axis=0)
    sines = jnp.sin(angles)
    sine = jnp.stack([-sines, sines], axis=1).reshape(HD, 4 * half)

    norms = pack_norms(first_gain, first_shift, second_gain, second_shift)
    if two:
        block_a = jnp.concatenate([w_inner, pack_output(w_output), norms], axis=0)
        row_a = row_stack(after(block_a, x_own))
        chunk_a = plane_and_core(row_a)
        row_b = row_stack(after(pack_outer(w_outer), row_a))
        chunk_b = plane_and_core(row_b)
    else:
        chunk_a, chunk_b = gather_generic(w_output, w_inner, w_outer, norms, row, y, c)

    q_rot, kv_own = qkv(info, xs, mine, theirs, cosine, sine)
    kv_other = core_swap(kv_own)
    out, log_totals, *lows = attend(q_rot, kv_own, kv_other, bias)
    attn_parts = exchange4(lows, SQUARE)
    cot_parts = exchange4(after(to_row_order(out_grad), xs[3]), ROW)
    mixed, e0, e1, e2, e3, grad_one, attn_t, hidden_t, outer_t, branch_low, act_low, inner_low, norm_sums = middle(
        info, attn_parts, x_own, cot_parts, chunk_a, chunk_b
    )
    grads = exchange4([e0, e1, e2, e3], SQUARE)
    give_outer = outer_grad(1, info, outer_t, act_low)
    got_outer = core_swap(give_outer)
    give_inner = inner_grad(1, info, hidden_t, after(inner_low, give_outer), attn_t, branch_low, norm_sums)
    got_inner = core_swap(give_inner)
    keep_outer = outer_grad(0, info, outer_t, after(act_low, give_inner))
    keep_inner = inner_grad(0, info, hidden_t, after(inner_low, keep_outer), attn_t, branch_low, norm_sums)

    def head_back(head, grads):
        return attend_back(head, q_rot, kv_own, kv_other, bias, out, log_totals, grads, cosine, sine)

    if two:
        sums_outer = start_sums(keep_outer, got_outer)
        outer_x = swap2(sums_outer[3], "dp")
        outer_y = swap2(sums_outer[4], "cy")
        first = head_back(0, [after(grads[0], sums_outer[3], sums_outer[4], keep_inner)] + grads[1:])
        sums_inner = start_sums(after(keep_inner, first[0]), got_inner)
        inner_x = swap2(sums_inner[3], "dp")
        inner_y = swap2(sums_inner[4], "cy")
        own_outer, x_outer, y_outer = second_sums(sums_outer, outer_x, outer_y)
        plane_outer_parts = [own_outer, swap2(x_outer, "dp"), swap2(y_outer, "cy")]
        second = head_back(1, [after(grads[0], x_outer, y_outer, sums_inner[3], sums_inner[4])] + grads[1:])
        own_inner, x_inner, y_inner = second_sums(sums_inner, after(inner_x, second[0]), inner_y)
        plane_inner_parts = [own_inner, swap2(x_inner, "dp"), swap2(y_inner, "cy")]
        third_head = head_back(2, [after(grads[0], x_inner, y_inner)] + grads[1:])
    else:
        first, second, third_head = (head_back(head, grads) for head in range(3))

    mixed_out = from_row_order(exchange4(mixed, ROW))
    dqs, owns, gives = zip(first, second, third_head)
    gots = [core_swap(give) for give in gives]
    d0, d1, d2, d3, proj = finish_dx(info, dqs, owns, gots, mine, theirs, cosine, sine)
    dx_parts = exchange4([d0, d1, d2, d3], SQUARE)
    keep, give = finish_dw(info, proj, xs)
    by_round = (keep + core_swap(give).astype(f32)).astype(bf16)
    got = []
    for r1 in range(2):
        for r2 in range(2):
            got.append(
                lax.ppermute(by_round[r1 * 2 + r2], GROUP, group_route((r1, r2), True)).astype(f32)
            )
    if two:
        plane_outer = add_parts(plane_outer_parts).astype(bf16)
        outer_sums = [add_parts(exchange4(plane_outer, ROW))]
    d_x = add_parts([grad_one] + dx_parts).astype(bf16)
    d_input = from_row_order(exchange4(d_x, ROW)).astype(f32)
    if two:
        plane_inner = add_parts(plane_inner_parts).astype(bf16)
        inner_sums = [add_parts(exchange4(plane_inner, ROW))]
    else:
        outer_sums = generic_sums(keep_outer, got_outer)
        inner_sums = generic_sums(keep_inner, got_inner)

    lower = got[0] + got[2]
    upper = got[1] + got[3]
    g_qkv = dp_reduce(
        jnp.concatenate([jnp.where(z == 0, lower, upper), jnp.where(z == 0, upper, lower)], axis=0)
    )

    half_rows = feat // 2
    third = half_rows // 3
    g_outer = jnp.concatenate([unpack_outer(part) for part in outer_sums], axis=0)
    g_inner = jnp.concatenate([part[:half_rows] for part in inner_sums], axis=0)
    g_output = jnp.concatenate(
        [unpack_output(part[half_rows : half_rows + third], feat) for part in inner_sums], axis=0
    )
    g_norms = inner_sums[0][half_rows + third].reshape(4, feat)
    if not two:
        g_outer, g_inner, g_output = (
            lax.psum_scatter(g.astype(bf16), "dp", scatter_dimension=0, tiled=True).astype(f32)
            for g in (g_outer, g_inner, g_output)
        )
        g_norms = lax.psum(g_norms, "dp")

    return (
        mixed_out, d_input,
        g_qkv[:, :head_width], g_qkv[:, head_width : 2 * head_width], g_qkv[:, 2 * head_width :],
        g_output, g_inner, g_outer,
        g_norms[0], g_norms[1], g_norms[2], g_norms[3],
    )


def solution(mesh):
    shape = mesh.devices.shape
    fine = Mesh(mesh.devices.reshape(shape[0], 2, shape[1] // 2, 2, shape[2] // 2), EVERY)
    col = ("cy", "cc")
    acts = P(None, ROW, ("dp",) + col)
    by_row = P(ROW + ("dp",), col)
    by_col = P(col + ("dp",), ROW)
    vec = P(ROW)
    return jax.shard_map(
        local,
        mesh=fine,
        in_specs=(
            acts, by_row, by_row, by_row, by_col, by_row, by_col, vec, vec, vec, vec, P(), acts,
        ),
        out_specs=(
            acts, acts, by_row, by_row, by_row, by_col, by_row, by_col, vec, vec, vec, vec,
        ),
        check_vma=False,
    )
```

```python
import functools

import jax
import jax.numpy as jnp
from jax import lax
from jax.experimental import pallas as pl
from jax.experimental.pallas import tpu as pltpu
from jax.sharding import Mesh, PartitionSpec as P

HD = 64
EVERY = ("dp", "rm", "rz", "cy", "cc")
GROUP = ("rm", "rz", "cy", "cc")
ROW = ("rm", "rz")
SQUARE = ("rz", "cy")
bf16=jnp.bfloat16; f32=jnp.float32
LOG2E=1.4426950408889634
LN2=0.6931471805599453
masked_score=-1e30

def mm(a,b,dims=((1,),(0,))):
    return lax.dot_general(a,b,(dims,((),())),preferred_element_type=f32)
NT=((1,),(1,))

def pair_turn(values, cosine, signed_sine):
    shape = values.shape
    v3 = values.reshape(shape[0]//8, 8, shape[1])
    up = pltpu.roll(v3, 7, 1); down = pltpu.roll(v3, 1, 1)
    even = (lax.broadcasted_iota(jnp.int32, v3.shape, 1) % 2) == 0
    other = jnp.where(even, up, down).reshape(shape)
    return values*cosine + other*signed_sine

KB=1024
QB=2
def one_row(shape, dtype, value=1.0):
    return jnp.where(lax.broadcasted_iota(jnp.int32, shape, 0)==0, value, 0.0).astype(dtype)

def attend_kernel(q_ref, ko_ref, vo_ref, kx_ref, vx_ref, bias_ref, o_ref, lse_ref, l0, l1, l2, l3, kaug, vall):
    head=pl.program_id(0); qb=pl.program_id(1)
    span=ko_ref.shape[1]
    @pl.when(qb==0)
    def _():
        for part,(kr,vr) in enumerate(((ko_ref,vo_ref),(kx_ref,vx_ref))):
            aug=jnp.concatenate([kr[...], bias_ref[:, part*span:(part+1)*span]],axis=0)
            kaug[part*span:(part+1)*span,:]=aug.T
            vall[:, part*span:(part+1)*span]=vr[...]
    n=q_ref.shape[1]
    qaug=jnp.concatenate([q_ref[...], one_row((HD,n),bf16)],axis=0)
    top=jnp.full((1,n),-3e38,f32); total=jnp.zeros((1,n),f32); acc=jnp.zeros((HD,n),f32)
    s=mm(kaug[0:KB,:],qaug)
    for kb in range(0,2*span,KB):
        following=mm(kaug[kb+KB:kb+2*KB,:],qaug) if kb+KB<2*span else None
        new=jnp.maximum(top,jnp.max(s,axis=0,keepdims=True))
        alpha=jnp.exp2(top-new)
        p=jnp.exp2(s-new)
        total=total*alpha+jnp.sum(p,axis=0,keepdims=True)
        acc=acc*alpha+mm(vall[:,kb:kb+KB],p.astype(bf16))
        top=new
        s=following
    out=acc/total
    o_ref[...]=out
    lse_ref[0]=top+jnp.log2(total)
    low=out.astype(bf16)
    part=n//QB
    for k,ref in enumerate((l0,l1,l2,l3)):
        @pl.when(qb==k//QB)
        def _(): ref[pl.ds(pl.multiple_of(head*HD,HD),HD),:]=low[:,(k%QB)*part:(k%QB+1)*part]

def attend(q,kv,kvx,bias):
    width,n4=q.shape; heads=width//HD; n=n4//4*QB; span=kv.shape[1]
    kspec=pl.BlockSpec((HD,span),lambda h,b:(h,0)); vspec=pl.BlockSpec((HD,span),lambda h,b:(heads+h,0))
    lowspec=pl.BlockSpec((width,n4//4),lambda h,b:(0,0))
    return pl.pallas_call(attend_kernel,grid=(heads,4//QB),
        in_specs=[pl.BlockSpec((HD,n),lambda h,b:(h,b)),kspec,vspec,kspec,vspec,pl.BlockSpec((HD,2*span),lambda h,b:(0,0))],
        out_specs=[pl.BlockSpec((HD,n),lambda h,b:(h,b)),pl.BlockSpec((1,1,n),lambda h,b:(h,0,b))]+[lowspec]*4,
        out_shape=[jax.ShapeDtypeStruct((width,n4),f32),jax.ShapeDtypeStruct((heads,1,n4),f32)]+[jax.ShapeDtypeStruct((width,n4//4),bf16)]*4,
        scratch_shapes=[pltpu.VMEM((2*span,2*HD),bf16),pltpu.VMEM((HD,2*span),bf16)],
        cost_estimate=pl.CostEstimate(flops=4*width*n4//HD*2*span*256,bytes_accessed=4*n4*2*span,transcendentals=heads*n4*2*span),
        name="attend")(q,kv,kv,kvx,kvx,bias)

BKB=512
def attend_back_kernel(q_ref, ko_ref, vo_ref, kx_ref, vx_ref, bias_ref, o_ref, lse_ref, g0,g1,g2,g3, cos_ref, sin_ref,
                       dq_ref, own_ref, give_ref, kaug, vtm, kall, acc):
    qb=pl.program_id(0)
    span=ko_ref.shape[1]; n=q_ref.shape[1]
    @pl.when(qb==0)
    def _():
        for part,(kr,vr) in enumerate(((ko_ref,vo_ref),(kx_ref,vx_ref))):
            sl=slice(part*span,(part+1)*span)
            kaug[sl,:]=jnp.concatenate([kr[...], bias_ref[:, sl]],axis=0).T
            vtm[sl,:]=jnp.concatenate([vr[...], jnp.zeros((HD,span),bf16)],axis=0).T
            kall[:,sl]=kr[...]
        acc[...]=jnp.zeros_like(acc)
    q=q_ref[...]
    zeros=jnp.zeros((HD,n),bf16)
    qaug=jnp.concatenate([q, one_row((HD,n),bf16)],axis=0)
    g=jnp.concatenate([jnp.where(qb==0,g0[...],g2[...]),jnp.where(qb==0,g1[...],g3[...])],axis=1)
    qpad=jnp.concatenate([q,zeros],axis=0).T
    gpad=jnp.concatenate([zeros,g],axis=0).T
    gaug=jnp.concatenate([g,zeros],axis=0)
    delta=jnp.sum(g.astype(f32)*o_ref[...],axis=0,keepdims=True)
    lse=lse_ref[0]
    dq=jnp.zeros((HD,n),f32)
    s=mm(kaug[0:BKB,:],qaug); dp=mm(vtm[0:BKB,:],gaug)
    for kb in range(0,2*span,BKB):
        last=kb+BKB>=2*span
        s_next=None if last else mm(kaug[kb+BKB:kb+2*BKB,:],qaug)
        dp_next=None if last else mm(vtm[kb+BKB:kb+2*BKB,:],gaug)
        p=jnp.exp2(s-lse)
        ds=(p*(dp-delta)).astype(bf16)
        dq=dq+mm(kall[:,kb:kb+BKB],ds)
        acc[kb:kb+BKB,:]=acc[kb:kb+BKB,:]+mm(ds,qpad)+mm(p.astype(bf16),gpad)
        s=s_next; dp=dp_next
    dq_ref[...]=pair_turn(dq*(HD**-0.5),cos_ref[...],-sin_ref[...]).astype(bf16)
    @pl.when(qb==4//QB-1)
    def _():
        own_ref[...]=acc[:span,:]
        give_ref[...]=acc[span:,:].astype(bf16)

def attend_back(head,q,kv,kvx,bias,o,lse,grads,cos,sin):
    width,n4=q.shape; heads=width//HD; n=n4//4*QB; span=kv.shape[1]
    kspec=pl.BlockSpec((HD,span),lambda b:(head,0)); vspec=pl.BlockSpec((HD,span),lambda b:(heads+head,0))
    gspec=pl.BlockSpec((HD,n4//4),lambda b:(head,0)); hb=pl.BlockSpec((HD,n),lambda b:(head,b)); tb=pl.BlockSpec((HD,n),lambda b:(0,b))
    dspec=pl.BlockSpec((span,2*HD),lambda b:(0,0))
    return pl.pallas_call(attend_back_kernel,grid=(4//QB,),
        in_specs=[hb,kspec,vspec,kspec,vspec,pl.BlockSpec((HD,2*span),lambda b:(0,0)),hb,pl.BlockSpec((1,1,n),lambda b:(head,0,b)),gspec,gspec,gspec,gspec,tb,tb],
        out_specs=[tb,dspec,dspec],
        out_shape=[jax.ShapeDtypeStruct((HD,n4),bf16),jax.ShapeDtypeStruct((span,2*HD),f32),jax.ShapeDtypeStruct((span,2*HD),bf16)],
        scratch_shapes=[pltpu.VMEM((2*span,2*HD),bf16),pltpu.VMEM((2*span,2*HD),bf16),pltpu.VMEM((HD,2*span),bf16),pltpu.VMEM((2*span,2*HD),f32)],
        cost_estimate=pl.CostEstimate(flops=10*n4*2*span*256,bytes_accessed=4*n4*2*span,transcendentals=n4*2*span),
        name="attend_back")(q,kv,kv,kvx,kvx,bias,o,lse,*grads,cos,sin)
def xor(a,b):
    return lax.bitwise_xor(jnp.asarray(a,jnp.int32),jnp.asarray(b,jnp.int32))

def rows_at(index,size,align):
    return pl.ds(pl.multiple_of(index*size,align),size)

def place_qkv_weights(info, mine_ref, theirs_ref, w_s):
    row=info[0]; c=info[3]
    half=mine_ref.shape[1]
    for r in range(4):
        k=xor(r,row)
        w_s[pl.ds(pl.multiple_of((2*r+c)*half,32),half),:]=mine_ref[k]
        w_s[pl.ds(pl.multiple_of((2*r+1-c)*half,32),half),:]=theirs_ref[k]

def place_tokens(info, x_ref, kz, x_s):
    feat=x_ref.shape[1]; base=xor(info[0],kz)
    for r in range(4):
        x_s[r*feat:(r+1)*feat,:]=x_ref[xor(r,base)]

def qkv_kernel(info, x0,x1,x2,x3, mine_ref, theirs_ref, cos_ref, sin_ref, q_ref, kv_ref, w_s, wt_s, x_s):
    place_qkv_weights(info,mine_ref,theirs_ref,w_s)
    wt_s[...]=w_s[...].T
    hw=q_ref.shape[0]; n=x0.shape[2]
    for k,xr in enumerate((x0,x1,x2,x3)):
        place_tokens(info,xr,k//2,x_s)
        out=mm(wt_s[...],x_s[...])
        sl=slice(k*n,(k+1)*n)
        cos=cos_ref[:,sl]; sin=sin_ref[:,sl]
        for h in range(2*hw//HD):
            turned=pair_turn(out[h*HD:(h+1)*HD],cos,sin)
            if h*HD<hw: q_ref[h*HD:(h+1)*HD,sl]=(turned*(HD**-0.5*LOG2E)).astype(bf16)
            else: kv_ref[h*HD-hw:(h+1)*HD-hw,sl]=turned.astype(bf16)
        kv_ref[hw:,sl]=out[2*hw:].astype(bf16)

VM=pl.BlockSpec(memory_space=pltpu.VMEM)
SM=pl.BlockSpec(memory_space=pltpu.SMEM)
HB=pl.BlockSpec(memory_space=pl.ANY)

def qkv(info,xs,mine,theirs,cos,sin):
    _,feat,n=xs[0].shape; w3=mine.shape[2]; hw=w3//3; width=4*feat
    return pl.pallas_call(qkv_kernel,in_specs=[SM]+[VM]*8,out_specs=[VM,VM],
        out_shape=[jax.ShapeDtypeStruct((hw,4*n),bf16),jax.ShapeDtypeStruct((2*hw,4*n),bf16)],
        scratch_shapes=[pltpu.VMEM((width,w3),bf16),pltpu.VMEM((w3,width),bf16),pltpu.VMEM((width,n),bf16)],
        name="qkv")(info,*xs,mine,theirs,cos,sin)

def finish_dx_kernel(info, *refs):
    heads=refs[0].shape[0]
    del heads
    (q0,q1,q2,o0,o1,o2,r0,r1,r2,mine_ref,theirs_ref,cos_ref,sin_ref,d0,d1,d2,d3,p_ref,w_s)=refs
    hw=3*HD; n=d0.shape[2]; feat=d0.shape[1]
    place_qkv_weights(info,mine_ref,theirs_ref,w_s)
    for h,(qr,orr,rr) in enumerate(((q0,o0,r0),(q1,o1,r1),(q2,o2,r2))):
        p_ref[h*HD:(h+1)*HD,:]=qr[...]
        t=(orr[...]+rr[...].astype(f32)).T
        p_ref[hw+h*HD:hw+(h+1)*HD,:]=pair_turn(t[:HD]*LN2,cos_ref[...],-sin_ref[...]).astype(bf16)
        p_ref[2*hw+h*HD:2*hw+(h+1)*HD,:]=t[HD:].astype(bf16)
    for k,dr in ((3,d3),(1,d1),(2,d2),(0,d0)):
        sl=slice(k*n,(k+1)*n)
        base=xor(info[0],k//2)
        for r in range(4):
            dr[xor(r,base)]=mm(w_s[r*feat:(r+1)*feat,:],p_ref[:,sl]).astype(dr.dtype)

def finish_dx(info,dqs,owns,gots,mine,theirs,cos,sin):
    w3=mine.shape[2]; half=mine.shape[1]; feat=2*half; width=4*feat; n=dqs[0].shape[1]//4
    S=jax.ShapeDtypeStruct
    return pl.pallas_call(finish_dx_kernel,in_specs=[SM]+[VM]*13,out_specs=[VM]*5,
        out_shape=[S((4,feat,n),f32)]+[S((4,feat,n),bf16)]*3+[S((w3,4*n),bf16)],
        scratch_shapes=[pltpu.VMEM((width,w3),bf16)],
        cost_estimate=pl.CostEstimate(flops=8*width*w3*n,bytes_accessed=8*width*n*4,transcendentals=0),
        name="finish_dx")(info,*dqs,*owns,*gots,mine,theirs,cos,sin)

def finish_dw_kernel(info, p_ref, x0,x1,x2,x3, keep_ref, give_ref, x_s, g_s):
    n=x0.shape[2]; half=keep_ref.shape[1]
    for k,xr in enumerate((x0,x1,x2,x3)):
        place_tokens(info,xr,k//2,x_s.at[:,k*n:(k+1)*n])
    g_s[...]=mm(x_s[...],p_ref[...],NT)
    c=info[3]; row=info[0]
    for r in range(4):
        mine_rows=pl.ds(pl.multiple_of((2*r+c)*half,32),half); their_rows=pl.ds(pl.multiple_of((2*r+1-c)*half,32),half)
        keep_ref[xor(r,row)]=g_s[mine_rows,:]
        give_ref[xor(r,row)]=g_s[their_rows,:].astype(bf16)

def finish_dw(info,proj,xs):
    _,feat,n=xs[0].shape; w3=proj.shape[0]; width=4*feat; half=feat//2
    return pl.pallas_call(finish_dw_kernel,in_specs=[SM]+[VM]*5,out_specs=[VM]*2,
        out_shape=[jax.ShapeDtypeStruct((4,half,w3),f32),jax.ShapeDtypeStruct((4,half,w3),bf16)],
        scratch_shapes=[pltpu.VMEM((width,4*n),bf16),pltpu.VMEM((width,w3),f32)],
        cost_estimate=pl.CostEstimate(flops=8*width*w3*n,bytes_accessed=8*width*n*2,transcendentals=0),
        name="finish_dw")(info,proj,*xs)

def row_step(core,slot):
    return jnp.where(core==0,slot,(slot%2)*2+slot//2)

def middle_kernel(info, a0,a1,a2,a3, x_ref, c0,c1,c2,c3, *refs):
    chunk_a=refs[:8]; chunk_b=refs[8:16]
    (mixed_ref, e0,e1,e2,e3, g1_ref, attnT_ref, hidT_ref, outT_ref, bl_ref, act_ref, il_ref, norm_ref,
                  win, woT, wo, ns, gp_s, t_s, f_s, sems)=refs[16:]
    row=info[0]; zy=info[1]; c=info[3]; group=info[5]; y=info[6]
    feat=a0.shape[0]; n=a0.shape[1]; width=4*feat; ffc=chunk_a[0].shape[2]; half=feat//2; fh=ffc//2; third=half//3
    def go(src,dst,s): pltpu.make_async_copy(src,dst,sems.at[s]).start()
    def each(chunk):
        for kc in range(2):
            core=xor(c,kc)
            for spot,ref in enumerate(chunk[4*kc:4*kc+4]):
                first,second=spot%2,spot//2
                kx=jnp.where(core==0,second,first); ky=jnp.where(core==0,first,second)
                g=xor(group,kx); col=xor(y,ky)*2+core
                for i in range(4):
                    step=row_step(core,i)
                    yield ref.at[i],xor(row,step),g,col,kc+spot
    for ref,r,g,col,_ in each(chunk_a):
        for j in range(3):
            go(ref.at[half:half+third,j*256:(j+1)*256],wo.at[r,pl.ds(pl.multiple_of((col*2+g)*half+j*third,16),third),:],0)
    for ref,r,g,col,where in each(chunk_a):
        if where==0:
            go(ref.at[half+third:half+third+16,:],ns.at[r],3)
    for ref,r,g,col,_ in each(chunk_a):
        go(ref.at[0:half,:],win.at[pl.ds(pl.multiple_of(r*feat+g*half,16),half),pl.ds(pl.multiple_of(col*ffc,128),ffc)],1)
    for ref,r,g,col,_ in each(chunk_b):
        for t in range(2):
            go(ref.at[:,t*fh:(t+1)*fh],woT.at[pl.ds(pl.multiple_of(r*feat+t*half,16),half),pl.ds(pl.multiple_of((col*2+g)*fh,128),fh)],2)
    def group_of(k):
        other=xor(zy,k)
        return (other%2)*2+other//2
    for k,ar in enumerate((a0,a1,a2,a3)):
        attnT_ref[rows_at(group_of(k),feat,64),:]=ar[...]
    for i in range(4):
        t_s[rows_at(xor(i,row),feat,64),:]=x_ref[i]
    attn=attnT_ref[...].T
    x=t_s[...].T.astype(f32)
    pltpu.make_async_copy(wo,wo,sems.at[0]).wait()
    pltpu.make_async_copy(ns,ns,sems.at[3]).wait()
    def vector(which):
        out=[]
        for r in range(4):
            v=ns[r].astype(f32)[0:3,which*feat:(which+1)*feat]
            out.append(jnp.sum(v,axis=0,keepdims=True))
        return jnp.concatenate(out,axis=1)
    gain1=vector(0); shift1=vector(1); gain2=vector(2); shift2=vector(3)
    branch=jnp.concatenate([mm(attn,wo[r])[:,:feat] for r in range(4)],axis=1)
    def stats(v):
        mean=jnp.sum(v,axis=1,keepdims=True)*(1.0/width)
        var=jnp.sum(v*v,axis=1,keepdims=True)*(1.0/width)-mean*mean
        inv=lax.rsqrt(var+1e-5)
        return (v-mean)*inv,inv
    cent1,inv1=stats(x+branch)
    hidden=cent1*gain1+shift1
    hid=hidden.astype(bf16)
    hidT_ref[...]=hid.T
    pltpu.make_async_copy(win,win,sems.at[1]).wait()
    pltpu.make_async_copy(woT,woT,sems.at[2]).wait()
    f_s[...]=jnp.zeros_like(f_s)
    nb=2; bw=ffc//nb
    def forward(j,carry):
        sl=pl.ds(pl.multiple_of(j*bw,128),bw)
        inner=mm(hid,win[:,sl])
        cdf=0.5+0.5*lax.erf(inner*0.7071067811865476)
        act=(inner*cdf).astype(bf16)
        gp_s[:,sl]=cdf+inner*(jnp.exp(inner*inner*-0.5)*0.3989422804014327)
        act_ref[:,sl]=act
        f_s[...]+=mm(act,woT[:,sl],NT)
        return carry
    lax.fori_loop(0,4*nb,forward,0)
    cent2,inv2=stats(hidden+f_s[...])
    t_s[...]=(cent2*gain2+shift2).astype(bf16).T
    for i in range(4):
        mixed_ref[i]=t_s[rows_at(xor(i,row),feat,64),:]
    for k,cr in enumerate((c0,c1,c2,c3)):
        for j in range(3):
            t_s[pl.ds(pl.multiple_of(xor(k,row)*feat+j*(feat//3),64),feat//3),:]=cr[half:,j*256:(j+1)*256]
    valid=(lax.broadcasted_iota(jnp.int32,(n,1),0)<info[4]).astype(f32)
    cot=t_s[...].T.astype(f32)*valid
    sums2=(jnp.sum(cot*cent2,axis=0,keepdims=True),jnp.sum(cot,axis=0,keepdims=True))
    def back(e,cent,inv):
        first=jnp.sum(e,axis=1,keepdims=True)*(1.0/width)
        second=jnp.sum(e*cent,axis=1,keepdims=True)*(1.0/width)
        return inv*(e-first-cent*second)
    grad2=back(cot*gain2,cent2,inv2)
    low=grad2.astype(bf16)
    outT_ref[...]=low.T
    f_s[...]=grad2
    def backward(j,carry):
        sl=pl.ds(pl.multiple_of(j*bw,128),bw)
        il=(mm(low,woT[:,sl])*gp_s[:,sl]).astype(bf16)
        il_ref[:,sl]=il
        f_s[...]+=mm(il,win[:,sl],NT)
        return carry
    lax.fori_loop(0,4*nb,backward,0)
    gh=f_s[...]
    sums=jnp.concatenate((jnp.sum(gh*cent1,axis=0,keepdims=True),jnp.sum(gh,axis=0,keepdims=True))+sums2+(jnp.zeros((4,width),f32),),axis=0)
    for r in range(4):
        norm_ref[r]=sums[:,r*feat:(r+1)*feat]
    grad1=back(gh*gain1,cent1,inv1)
    bl=grad1.astype(bf16)
    padded=jnp.concatenate([bl,jnp.zeros((n,256-feat),bf16)],axis=1)
    da=jnp.zeros((width,n),f32)
    for r in range(4):
        piece=padded[:,r*feat:r*feat+256]
        bl_ref[r]=piece
        da=da+mm(wo[r],piece,NT)
    t_s[...]=da.astype(bf16)
    for k,er in enumerate((e0,e1,e2,e3)):
        er[...]=t_s[rows_at(group_of(k),feat,64),:]
    f2=grad1.T
    for r in range(4):
        g1_ref[xor(r,row)]=f2[r*feat:(r+1)*feat]

def middle(info,attn_parts,x_own,cot_parts,chunk_a,chunk_b):
    feat,n=attn_parts[0].shape; width=4*feat; ff=4*chunk_a[0].shape[2]
    S=jax.ShapeDtypeStruct
    return pl.pallas_call(middle_kernel,in_specs=[SM]+[VM]*9+[HB]*16,out_specs=[VM]*13,
        out_shape=[S((4,feat,n),bf16)]+[S((feat,n),bf16)]*4+[S((4,feat,n),f32),S((width,n),bf16),S((width,n),bf16),S((width,n),bf16),
                   S((4,n,256),bf16),S((n,ff),bf16),S((n,ff),bf16),S((4,8,feat),f32)],
        scratch_shapes=[pltpu.VMEM((width,ff),bf16),pltpu.VMEM((width,ff),bf16),pltpu.VMEM((4,width,256),bf16),pltpu.VMEM((4,16,width),bf16),
                        pltpu.VMEM((n,ff),f32),pltpu.VMEM((width,n),bf16),pltpu.VMEM((n,width),f32),pltpu.SemaphoreType.DMA((4,))],
        compiler_params=pltpu.CompilerParams(vmem_limit_bytes=56*1024*1024),
        cost_estimate=pl.CostEstimate(flops=12*n*width*ff*2,bytes_accessed=24*width*ff,transcendentals=2*n*ff),
        name="middle")(info,*attn_parts,x_own,*cot_parts,*chunk_a,*chunk_b)

def target(info,which,a,b):
    core=xor(info[3],which)
    kx=jnp.where(core==0,a,b); ky=jnp.where(core==0,b,a)
    return core,xor(info[5],kx),xor(info[6],ky)*2+core

def outer_blocks(info,which,a,b,refs,put):
    outT_ref,act_ref=refs
    core,g,_=target(info,which,a,b)
    half=outT_ref.shape[0]//8; fh=act_ref.shape[1]//2
    rhs=act_ref[:,pl.ds(pl.multiple_of(g*fh,128),fh)]
    for s in range(4):
        value=mm(outT_ref[rows_at(xor(info[0],row_step(core,s)),2*half,64),:],rhs)
        put(s,slice(0,half),slice(0,fh),value[:half])
        put(s,slice(0,half),slice(fh,2*fh),value[half:])

def inner_blocks(info,which,a,b,refs,put):
    hidT_ref,il_ref,attnT_ref,bl_ref,norm_ref=refs
    core,g,col=target(info,which,a,b)
    half=hidT_ref.shape[0]//8; third=half//3
    rows=[xor(info[0],row_step(core,s)) for s in range(4)]
    lhs=jnp.concatenate([hidT_ref[rows_at(r*2+g,half,32),:] for r in rows],axis=0)
    value=mm(lhs,il_ref[...])
    heads=attnT_ref[rows_at(col*2+g,half,32),:]
    for s,r in enumerate(rows):
        put(s,slice(0,half),slice(None),value[s*half:(s+1)*half])
        outs=mm(heads,bl_ref[r])
        for j in range(3):
            put(s,slice(half,half+third),slice(j*256,(j+1)*256),outs[j*third:(j+1)*third])
        line=jnp.concatenate([norm_ref[r][i:i+1] for i in range(4)],axis=1)
        put(s,slice(half+third,half+third+16),slice(None),jnp.concatenate([line,jnp.zeros((15,line.shape[1]),f32)],axis=0))

def give_kernel(blocks,info,*refs):
    out=refs[-1]
    def put(s,rows,lanes,value): out[0,0,s,rows,lanes]=value.astype(bf16)
    blocks(info,1,pl.program_id(0),pl.program_id(1),refs[:-1],put)

def first_kernel(blocks,info,*refs):
    got,out=refs[-2:]
    def put(s,rows,lanes,value): out[0,s,rows,lanes]=(value+got[0,0,s,rows,lanes].astype(f32)).astype(bf16)
    blocks(info,0,1,pl.program_id(0),refs[:-2],put)

def second_kernel(blocks,info,*refs):
    got,came,keep,send=refs[-4:]
    for b,out in ((0,keep),(1,send)):
        def put(s,rows,lanes,value):
            out[s,rows,lanes]=(value+got[0,0,s,rows,lanes].astype(f32)+came[0,s,rows,lanes].astype(f32)).astype(bf16)
        @pl.when(pl.program_id(0)==b)
        def _(): blocks(info,0,0,b,refs[:-4],put)

def grad_call(kind,stage,info,args,got=None,came=None):
    S=jax.ShapeDtypeStruct
    width,n=args[0].shape; ffc=args[1].shape[1]//4; half=width//8
    blocks,rows=(inner_blocks,half+half//3+16) if kind=="inner" else (outer_blocks,half)
    fixed=[pl.BlockSpec((width,n),lambda *i:(0,0)),None]+([pl.BlockSpec((width,n),lambda *i:(0,0)),pl.BlockSpec((4,n,256),lambda *i:(0,0,0)),pl.BlockSpec((4,8,width//4),lambda *i:(0,0,0))] if kind=="inner" else [])
    cost=pl.CostEstimate(flops=(4 if stage=="give" else 2)*width*n*ffc,bytes_accessed=16*rows*ffc,transcendentals=0)
    name=kind+"_"+stage
    if stage=="give":
        fixed[1]=pl.BlockSpec((n,ffc),lambda a,b,s:(0,target(s,1,a,b)[2]))
        return pl.pallas_call(functools.partial(give_kernel,blocks),
            grid_spec=pltpu.PrefetchScalarGridSpec(num_scalar_prefetch=1,grid=(2,2),in_specs=fixed,out_specs=pl.BlockSpec((1,1,4,rows,ffc),lambda a,b,s:(a,b,0,0,0))),
            out_shape=S((2,2,4,rows,ffc),bf16),cost_estimate=cost,name=name)(info,*args)
    a=1 if stage=="first" else 0
    fixed[1]=pl.BlockSpec((n,ffc),lambda b,s:(0,target(s,0,a,b)[2]))
    got_spec=pl.BlockSpec((1,1,4,rows,ffc),lambda b,s:(a,b,0,0,0)); one=pl.BlockSpec((1,4,rows,ffc),lambda b,s:(b,0,0,0))
    if stage=="first":
        return pl.pallas_call(functools.partial(first_kernel,blocks),
            grid_spec=pltpu.PrefetchScalarGridSpec(num_scalar_prefetch=1,grid=(2,),in_specs=fixed+[got_spec],out_specs=one),
            out_shape=S((2,4,rows,ffc),bf16),cost_estimate=cost,name=name)(info,*args,got)
    whole=pl.BlockSpec((4,rows,ffc),lambda b,s:(0,0,0))
    return pl.pallas_call(functools.partial(second_kernel,blocks),
        grid_spec=pltpu.PrefetchScalarGridSpec(num_scalar_prefetch=1,grid=(2,),in_specs=fixed+[got_spec,one],out_specs=[whole,whole]),
        out_shape=[S((4,rows,ffc),bf16)]*2,cost_estimate=cost,name=name)(info,*args,got,came)

def exchange4(blocks, axes):
    parts = [blocks[0]]
    for step in range(1, 4):
        parts.append(lax.ppermute(blocks[step], axes, [(i, i ^ step) for i in range(4)]))
    return parts


def core_swap(value):
    return lax.ppermute(value, "cc", [(0, 1), (1, 0)])


def swap_by(blocks, index):
    pairs = blocks.reshape((2, 2) + blocks.shape[1:])
    pairs = jnp.where((index // 2) == 1, pairs[::-1], pairs)
    pairs = jnp.where((index % 2) == 1, pairs[:, ::-1], pairs)
    return pairs.reshape(blocks.shape)


def dp_halves(value, c):
    if lax.axis_size("dp") != 2:
        whole = lax.all_gather(value, "dp", axis=0, tiled=True)
        halves = whole.reshape((2, whole.shape[0] // 2) + whole.shape[1:])
        return jnp.where(c == 0, halves[0], halves[1]), jnp.where(c == 0, halves[1], halves[0])
    other = swap2(value, "dp")
    same = lax.axis_index("dp") == c
    return jnp.where(same, value, other), jnp.where(same, other, value)


def dp_sum(this_half, other_half, c):
    if lax.axis_size("dp") != 2:
        whole = jnp.concatenate(
            [jnp.where(c == 0, this_half, other_half), jnp.where(c == 0, other_half, this_half)], axis=0
        )
        return lax.psum_scatter(whole.astype(bf16), "dp", scatter_dimension=0, tiled=True).astype(f32)
    same = lax.axis_index("dp") == c
    keep = jnp.where(same, this_half, other_half)
    return keep + swap2(jnp.where(same, other_half, this_half).astype(bf16), "dp").astype(f32)


def pack_outer(part):
    turned = part.T
    half = turned.shape[0] // 2
    return jnp.concatenate([turned[:half], turned[half:]], axis=1)


def unpack_outer(packed):
    wide = packed.shape[1] // 2
    return jnp.concatenate([packed[:, :wide], packed[:, wide:]], axis=0).T


def pack_output(part):
    third = part.shape[0] // 3
    padded = jnp.pad(part, ((0, 0), (0, 256 - part.shape[1])))
    return jnp.concatenate([padded[j * third : (j + 1) * third] for j in range(3)], axis=1)


def unpack_output(packed, feat):
    return jnp.concatenate([packed[:, j * 256 : j * 256 + feat] for j in range(3)], axis=0)


def pack_norms(first_gain, first_shift, second_gain, second_shift):
    line = jnp.concatenate([first_gain, first_shift, second_gain, second_shift])
    high = lax.reduce_precision(line, 8, 7)
    middle_part = lax.reduce_precision(line - high, 8, 7)
    rest = line - high - middle_part
    rows = jnp.stack([high, middle_part, rest]).astype(bf16)
    return jnp.pad(rows, ((0, 13), (0, 0)))


def after(value, *earlier):
    return lax.optimization_barrier((value,) + earlier)[0]


def swap2(value, axis):
    return lax.ppermute(value, axis, [(0, 1), (1, 0)])


def crossed(value, axes, first):
    pairs = []
    for u in range(2):
        for v in range(2):
            for core in range(2):
                along = first ^ core
                pairs.append(((u * 2 + v) * 2 + core, ((u ^ (1 - along)) * 2 + (v ^ along)) * 2 + core))
    return lax.ppermute(value, axes + ("cc",), pairs)


PLANE = ("dp", "cy")


def row_gather(block):
    pair = jnp.stack([block, crossed(block, ROW, 1)])
    return jnp.concatenate([pair, crossed(pair, ROW, 0)], axis=0)


def plane_gather(stack, forward_after):
    near = crossed(stack, PLANE, 1)
    far = crossed(stack, PLANE, 0)
    both = crossed(after(near, *forward_after), PLANE, 0)
    return [stack, near, far, both]


def core_copies(arrays, ties):
    return arrays + [core_swap(after(array, *tie)) for array, tie in zip(arrays, ties)]


def gather_generic(w_output, w_inner, w_outer, norms, row, y, c):
    inner, outer, output = (lax.all_gather(w, "dp", axis=0, tiled=True) for w in (w_inner, w_outer, w_output))
    chunks = []
    for which in range(2):
        halves = []
        for g in range(2):
            parts = [w.reshape((2, w.shape[0] // 2) + w.shape[1:])[g] for w in (inner, outer, output)]
            if which == 0:
                halves.append(jnp.concatenate([parts[0], pack_output(parts[2]), norms], axis=0))
            else:
                halves.append(pack_outer(parts[1]))
        whole = lax.all_gather(jnp.stack(halves), GROUP)
        flat = whole.reshape((-1,) + whole.shape[2:])
        arrays = []
        for kc in range(2):
            core = c ^ kc
            for spot in range(4):
                first, second = spot % 2, spot // 2
                kx = jnp.where(core == 0, second, first)
                ky = jnp.where(core == 0, first, second)
                steps = [jnp.where(core == 0, i, (i % 2) * 2 + i // 2) for i in range(4)]
                spots = jnp.stack([((row ^ k) * 4 + (y ^ ky) * 2 + core) * 2 + kx for k in steps])
                arrays.append(jnp.take(flat, spots, axis=0))
        chunks.append(arrays)
    return chunks


def add_parts(parts):
    total = parts[0].astype(f32)
    for part in parts[1:]:
        total = total + part.astype(f32)
    return total


def halve(stack):
    pass_on = crossed(stack[2:], ROW, 0)
    pair = (stack[:2].astype(f32) + pass_on.astype(f32)).astype(bf16)
    return pair[0].astype(f32) + crossed(pair[1], ROW, 1).astype(f32)


def generic_sums(first, keep, send, c):
    parts = [keep, send, first[0], first[1]]
    by_x = [
        (parts[0], jnp.where(c == 0, parts[1], parts[2])),
        (jnp.where(c == 0, parts[2], parts[1]), parts[3]),
    ]
    planes = [add_parts([own, swap2(other, "cy")]).astype(bf16) for own, other in by_x]
    return [halve(plane) for plane in planes]


def local(
    tokens, w_query, w_key, w_value, w_output, w_inner, w_outer,
    first_gain, first_shift, second_gain, second_shift, seq_lengths, out_grad,
):
    feat = tokens.shape[1]
    cols = tokens.shape[2]
    half = cols // 2
    head_width = w_query.shape[1]
    two = lax.axis_size("dp") == 2
    row = lax.axis_index(ROW)
    group = lax.axis_index("dp")
    m = lax.axis_index("rm")
    z = lax.axis_index("rz")
    y = lax.axis_index("cy")
    c = lax.axis_index("cc")
    length = lax.dynamic_index_in_dim(seq_lengths[m], group, keepdims=False)
    own_start = (y * 2 + c) * cols + z * half
    info = jnp.stack([
        row, z * 2 + y, m * 2 + c, c, length - own_start, group if two else 0 * group, y, 0 * y,
    ]).astype(jnp.int32)

    def to_row_order(array):
        blocks = array.reshape(2, feat, 2, half).transpose(0, 2, 1, 3).reshape(4, feat, half)
        return swap_by(blocks, row)

    def from_row_order(parts):
        back = swap_by(jnp.stack(parts), row)
        return back.reshape(2, 2, feat, half).transpose(0, 2, 1, 3).reshape(2, feat, cols)

    this_half, other_half = dp_halves(jnp.concatenate([w_query, w_key, w_value], axis=1), c)
    x_own = jnp.stack(exchange4(to_row_order(tokens), ROW))
    other_columns = core_swap(other_half)
    near = jnp.where(z == c, this_half, other_columns)
    far = jnp.where(z == c, other_columns, this_half)
    norms = pack_norms(first_gain, first_shift, second_gain, second_shift)
    if two:
        block_a = jnp.concatenate([w_inner, pack_output(w_output), norms], axis=0)
        row_a = row_gather(block_a)
        row_b = row_gather(after(pack_outer(w_outer), row_a))
    cot_blocks = to_row_order(out_grad)
    wide = jnp.concatenate([cot_blocks[:, j * feat // 3 : (j + 1) * feat // 3] for j in range(3)], axis=2)
    fill = ((0, 0), (0, wide.shape[2] - 3 * head_width))
    near, far = jnp.pad(near, fill), jnp.pad(far, fill)
    third_parts = exchange4(
        [jnp.concatenate([(near, far)[k % 2], wide[k]], axis=0) for k in range(4)], ROW
    )
    mine = jnp.stack([part[: feat // 2, : 3 * head_width] for part in third_parts])
    theirs = core_swap(mine)
    xs = exchange4([x_own] * 4, SQUARE)

    starts = []
    for kc in range(2):
        for k in range(4):
            starts.append(((y ^ (k % 2)) * 2 + (c ^ kc)) * cols + (z ^ (k // 2)) * half)
    positions = (jnp.stack(starts)[:, None] + jnp.arange(half, dtype=jnp.int32)[None, :]).reshape(-1)
    invalid = jnp.where(positions < length, 0.0, masked_score)
    bias = jnp.where(jnp.arange(HD)[:, None] == 0, invalid[None, :], 0.0).astype(bf16)
    frequency = 10000.0 ** (-2.0 * jnp.arange(HD // 2, dtype=f32) / HD)
    angles = frequency[:, None] * positions[: 4 * half].astype(f32)[None, :]
    cosine = jnp.repeat(jnp.cos(angles), 2, axis=0)
    sines = jnp.sin(angles)
    sine = jnp.stack([-sines, sines], axis=1).reshape(HD, 4 * half)

    q_rot, kv_own = qkv(info, xs, mine, theirs, cosine, sine)
    kv_other = core_swap(kv_own)
    out, log_totals, *lows = attend(q_rot, kv_own, kv_other, bias)
    attn_parts = exchange4(lows, SQUARE)
    if two:
        arrays_a = plane_gather(row_a, (kv_own,))
        chunk_a = core_copies(arrays_a, [(kv_own,), (kv_own,), (lows[0],), (lows[0],)])
        arrays_b = plane_gather(after(row_b, kv_own), (lows[0],))
        chunk_b = core_copies(arrays_b, [(lows[0],), (attn_parts[1],), (attn_parts[2],), (attn_parts[3],)])
    else:
        chunk_a, chunk_b = gather_generic(w_output, w_inner, w_outer, norms, row, y, c)
    mixed, e0, e1, e2, e3, grad_one, attn_t, hidden_t, outer_t, branch_low, act_low, inner_low, norm_sums = middle(
        info, attn_parts, x_own, third_parts, chunk_a, chunk_b
    )
    grads = exchange4([e0, e1, e2, e3], SQUARE)
    inner_args = (hidden_t, inner_low, attn_t, branch_low, norm_sums)
    outer_args = (outer_t, act_low)

    def tied(args, *earlier):
        return (after(args[0], *earlier),) + args[1:]

    def head_back(head, *earlier):
        return attend_back(
            head, after(q_rot, *earlier), kv_own, kv_other, bias, out, log_totals, grads, cosine, sine
        )

    give_inner = grad_call("inner", "give", info, inner_args)
    got_inner = core_swap(give_inner)
    give_outer = grad_call("outer", "give", info, tied(outer_args, give_inner))
    got_outer = core_swap(give_outer)
    first_inner = grad_call("inner", "first", info, tied(inner_args, give_outer), got_inner)
    came_inner = crossed(first_inner, PLANE, 0) if two else jnp.zeros_like(first_inner)
    first_outer = grad_call("outer", "first", info, tied(outer_args, first_inner), got_outer)
    came_outer = crossed(first_outer, PLANE, 0) if two else jnp.zeros_like(first_outer)
    dq0, own0, send0 = head_back(0, first_outer)
    keep_inner, pass_inner = grad_call(
        "inner", "second", info, tied(inner_args, dq0), got_inner, after(came_inner, dq0)
    )
    dq1, own1, send1 = head_back(1, keep_inner)
    keep_outer, pass_outer = grad_call(
        "outer", "second", info, tied(outer_args, dq1), got_outer, after(came_outer, dq1)
    )
    if two:
        plane_inner = add_parts([keep_inner, crossed(after(pass_inner, keep_inner), PLANE, 1)])
        plane_inner = after(plane_inner, keep_outer).astype(bf16)
        dq2, own2, send2 = head_back(2, plane_inner)
        plane_outer = add_parts([keep_outer, after(crossed(pass_outer, PLANE, 1), dq2)]).astype(bf16)
        outer_sums = [halve(plane_outer)]
        inner_sums = [halve(plane_inner)]
        own2 = after(own2, plane_outer)
    else:
        dq2, own2, send2 = head_back(2, keep_outer)
        outer_sums = generic_sums(first_outer, keep_outer, pass_outer, c)
        inner_sums = generic_sums(first_inner, keep_inner, pass_inner, c)

    gots = [core_swap(send) for send in (send0, send1, send2)]
    d0, d1, d2, d3, proj = finish_dx(info, (dq0, dq1, dq2), (own0, own1, own2), gots, mine, theirs, cosine, sine)
    dx_parts = exchange4([d0, d1, d2, d3], SQUARE)
    keep, give = finish_dw(info, after(proj, d0), xs)
    got = core_swap(give)
    by_row_step = (keep + got.astype(f32)).astype(bf16)
    d_x = add_parts([grad_one] + dx_parts).astype(bf16)
    d_input = from_row_order(exchange4(d_x, ROW)).astype(f32)
    mixed_out = from_row_order([after(part, give) for part in exchange4(after(mixed, first_outer), ROW)])
    q0, q1, q2, q3 = (part.astype(f32) for part in exchange4(by_row_step, ROW))
    near_sum = q0 + q2
    far_sum = q1 + q3
    kept = jnp.where(z == c, near_sum, far_sum)
    passed = core_swap(jnp.where(z == c, far_sum, near_sum).astype(bf16)).astype(f32)
    g_qkv = dp_sum(kept, passed, c)

    half_rows = feat // 2
    third = half_rows // 3
    g_outer = jnp.concatenate([unpack_outer(part) for part in outer_sums], axis=0)
    g_inner = jnp.concatenate([part[:half_rows] for part in inner_sums], axis=0)
    g_output = jnp.concatenate(
        [unpack_output(part[half_rows : half_rows + third], feat) for part in inner_sums], axis=0
    )
    g_norms = inner_sums[0][half_rows + third].reshape(4, feat)
    if not two:
        g_outer, g_inner, g_output = (
            lax.psum_scatter(g.astype(bf16), "dp", scatter_dimension=0, tiled=True).astype(f32)
            for g in (g_outer, g_inner, g_output)
        )
        g_norms = lax.psum(g_norms, "dp")

    return (
        mixed_out, d_input,
        g_qkv[:, :head_width], g_qkv[:, head_width : 2 * head_width], g_qkv[:, 2 * head_width :],
        g_output, g_inner, g_outer,
        g_norms[0], g_norms[1], g_norms[2], g_norms[3],
    )


def solution(mesh):
    shape = mesh.devices.shape
    fine = Mesh(mesh.devices.reshape(shape[0], 2, shape[1] // 2, 2, shape[2] // 2), EVERY)
    col = ("cy", "cc")
    acts = P(None, ROW, ("dp",) + col)
    by_row = P(ROW + ("dp",), col)
    by_col = P(col + ("dp",), ROW)
    vec = P(ROW)
    return jax.shard_map(
        local,
        mesh=fine,
        in_specs=(
            acts, by_row, by_row, by_row, by_col, by_row, by_col, vec, vec, vec, vec, P(), acts,
        ),
        out_specs=(
            acts, acts, by_row, by_row, by_row, by_col, by_row, by_col, vec, vec, vec, vec,
        ),
        check_vma=False,
    )
```

```python
import functools

import jax
import jax.numpy as jnp
from jax import lax
from jax.experimental import pallas as pl
from jax.experimental.pallas import tpu as pltpu
from jax.sharding import Mesh, PartitionSpec as P

HD = 64
EVERY = ("dp", "rm", "rz", "cy", "cc")
GROUP = ("rm", "rz", "cy", "cc")
ROW = ("rm", "rz")
SQUARE = ("rz", "cy")
bf16=jnp.bfloat16; f32=jnp.float32
LOG2E=1.4426950408889634
LN2=0.6931471805599453
masked_score=-1e30

def mm(a,b,dims=((1,),(0,))):
    return lax.dot_general(a,b,(dims,((),())),preferred_element_type=f32)
NT=((1,),(1,))

def pair_turn(values, cosine, signed_sine):
    shape = values.shape
    v3 = values.reshape(shape[0]//8, 8, shape[1])
    up = pltpu.roll(v3, 7, 1); down = pltpu.roll(v3, 1, 1)
    even = (lax.broadcasted_iota(jnp.int32, v3.shape, 1) % 2) == 0
    other = jnp.where(even, up, down).reshape(shape)
    return values*cosine + other*signed_sine

KB=1024
QB=2
def one_row(shape, dtype, value=1.0):
    return jnp.where(lax.broadcasted_iota(jnp.int32, shape, 0)==0, value, 0.0).astype(dtype)

def attend_kernel(q_ref, ko_ref, vo_ref, kx_ref, vx_ref, bias_ref, o_ref, lse_ref, low_ref, kaug, vall):
    span=ko_ref.shape[1]
    for part,(kr,vr) in enumerate(((ko_ref,vo_ref),(kx_ref,vx_ref))):
        aug=jnp.concatenate([kr[...], bias_ref[:, part*span:(part+1)*span]],axis=0)
        kaug[part*span:(part+1)*span,:]=aug.T
        vall[:, part*span:(part+1)*span]=vr[...]
    n=q_ref.shape[1]
    qaug=jnp.concatenate([q_ref[...], one_row((HD,n),bf16)],axis=0)
    top=jnp.full((1,n),-3e38,f32); total=jnp.zeros((1,n),f32); acc=jnp.zeros((HD,n),f32)
    s=mm(kaug[0:KB,:],qaug)
    for kb in range(0,2*span,KB):
        following=mm(kaug[kb+KB:kb+2*KB,:],qaug) if kb+KB<2*span else None
        new=jnp.maximum(top,jnp.max(s,axis=0,keepdims=True))
        alpha=jnp.exp2(top-new)
        p=jnp.exp2(s-new)
        total=total*alpha+jnp.sum(p,axis=0,keepdims=True)
        acc=acc*alpha+mm(vall[:,kb:kb+KB],p.astype(bf16))
        top=new
        s=following
    out=acc/total
    o_ref[...]=out
    lse_ref[0]=top+jnp.log2(total)
    low=out.astype(bf16)
    for b in range(2):
        low_ref[b]=low[:,b*(n//2):(b+1)*(n//2)]

def attend(part,q,kv,kvx,bias):
    width,n4=q.shape; heads=width//HD; n=n4//2; span=kv.shape[1]
    kspec=pl.BlockSpec((HD,span),lambda h:(h,0)); vspec=pl.BlockSpec((HD,span),lambda h:(heads+h,0))
    return pl.pallas_call(attend_kernel,grid=(heads,),
        in_specs=[pl.BlockSpec((HD,n),lambda h:(h,part)),kspec,vspec,kspec,vspec,pl.BlockSpec((HD,2*span),lambda h:(0,0))],
        out_specs=[pl.BlockSpec((HD,n),lambda h:(h,0)),pl.BlockSpec((1,1,n),lambda h:(h,0,0)),pl.BlockSpec((2,HD,n//2),lambda h:(0,h,0))],
        out_shape=[jax.ShapeDtypeStruct((width,n),f32),jax.ShapeDtypeStruct((heads,1,n),f32),jax.ShapeDtypeStruct((2,width,n//2),bf16)],
        scratch_shapes=[pltpu.VMEM((2*span,2*HD),bf16),pltpu.VMEM((HD,2*span),bf16)],
        cost_estimate=pl.CostEstimate(flops=int(6.0*(2*width*n4//HD*2*span*256))+1,bytes_accessed=int(6.0*(2*n4*2*span))+1,transcendentals=int(6.0*(heads*n*2*span))+1),
        name="attend")(q,kv,kv,kvx,kvx,bias)

BKB=512
def attend_back_kernel(q_ref, ko_ref, vo_ref, kx_ref, vx_ref, bias_ref, oa_ref, ob_ref, lsea_ref, lseb_ref, g0,g1,g2,g3, cos_ref, sin_ref,
                       dq_ref, own_ref, give_ref, kaug, vtm, kall, acc):
    qb=pl.program_id(0)
    span=ko_ref.shape[1]; n=q_ref.shape[1]
    @pl.when(qb==0)
    def _():
        for part,(kr,vr) in enumerate(((ko_ref,vo_ref),(kx_ref,vx_ref))):
            sl=slice(part*span,(part+1)*span)
            kaug[sl,:]=jnp.concatenate([kr[...], bias_ref[:, sl]],axis=0).T
            vtm[sl,:]=jnp.concatenate([vr[...], jnp.zeros((HD,span),bf16)],axis=0).T
            kall[:,sl]=kr[...]
        acc[...]=jnp.zeros_like(acc)
    q=q_ref[...]
    zeros=jnp.zeros((HD,n),bf16)
    qaug=jnp.concatenate([q, one_row((HD,n),bf16)],axis=0)
    g=jnp.concatenate([jnp.where(qb==0,g0[...],g2[...]),jnp.where(qb==0,g1[...],g3[...])],axis=1)
    o=jnp.where(qb==0,oa_ref[...],ob_ref[...])
    qpad=jnp.concatenate([q,zeros],axis=0).T
    gpad=jnp.concatenate([zeros,g],axis=0).T
    gaug=jnp.concatenate([g,zeros],axis=0)
    delta=jnp.sum(g.astype(f32)*o,axis=0,keepdims=True)
    lse=jnp.where(qb==0,lsea_ref[0],lseb_ref[0])
    dq=jnp.zeros((HD,n),f32)
    s=mm(kaug[0:BKB,:],qaug); dp=mm(vtm[0:BKB,:],gaug)
    for kb in range(0,2*span,BKB):
        last=kb+BKB>=2*span
        s_next=None if last else mm(kaug[kb+BKB:kb+2*BKB,:],qaug)
        dp_next=None if last else mm(vtm[kb+BKB:kb+2*BKB,:],gaug)
        p=jnp.exp2(s-lse)
        ds=(p*(dp-delta)).astype(bf16)
        dq=dq+mm(kall[:,kb:kb+BKB],ds)
        acc[kb:kb+BKB,:]=acc[kb:kb+BKB,:]+mm(ds,qpad)+mm(p.astype(bf16),gpad)
        s=s_next; dp=dp_next
    dq_ref[...]=pair_turn(dq*(HD**-0.5),cos_ref[...],-sin_ref[...]).astype(bf16)
    @pl.when(qb==4//QB-1)
    def _():
        own_ref[...]=acc[:span,:]
        give_ref[...]=acc[span:,:].astype(bf16)

def attend_back(head,q,kv,kvx,bias,os,lses,grads,cos,sin):
    width,n4=q.shape; heads=width//HD; n=n4//4*QB; span=kv.shape[1]
    kspec=pl.BlockSpec((HD,span),lambda b:(head,0)); vspec=pl.BlockSpec((HD,span),lambda b:(heads+head,0))
    gspec=lambda i:pl.BlockSpec((None,HD,n4//4),lambda b:(i,head,0)); hb=pl.BlockSpec((HD,n),lambda b:(head,b)); tb=pl.BlockSpec((HD,n),lambda b:(0,b))
    dspec=pl.BlockSpec((span,2*HD),lambda b:(0,0)); ospec=pl.BlockSpec((HD,n),lambda b:(head,0)); lspec=pl.BlockSpec((1,1,n),lambda b:(head,0,0))
    return pl.pallas_call(attend_back_kernel,grid=(4//QB,),
        in_specs=[hb,kspec,vspec,kspec,vspec,pl.BlockSpec((HD,2*span),lambda b:(0,0)),ospec,ospec,lspec,lspec,gspec(0),gspec(0),gspec(0),gspec(1),tb,tb],
        out_specs=[tb,dspec,dspec],
        out_shape=[jax.ShapeDtypeStruct((HD,n4),bf16),jax.ShapeDtypeStruct((span,2*HD),f32),jax.ShapeDtypeStruct((span,2*HD),bf16)],
        scratch_shapes=[pltpu.VMEM((2*span,2*HD),bf16),pltpu.VMEM((2*span,2*HD),bf16),pltpu.VMEM((HD,2*span),bf16),pltpu.VMEM((2*span,2*HD),f32)],
        cost_estimate=pl.CostEstimate(flops=int(6.0*(10*n4*2*span*256))+1,bytes_accessed=int(6.0*(4*n4*2*span))+1,transcendentals=int(6.0*(n4*2*span))+1),
        name="attend_back")(q,kv,kv,kvx,kvx,bias,*os,*lses,grads[0],grads[2],grads[1],grads[2],cos,sin)
def xor(a,b):
    return lax.bitwise_xor(jnp.asarray(a,jnp.int32),jnp.asarray(b,jnp.int32))

def rows_at(index,size,align):
    return pl.ds(pl.multiple_of(index*size,align),size)

def row_step(core,slot):
    return jnp.where(core==0,slot,(slot%2)*2+slot//2)

def z_step(core,slot):
    return jnp.where(core==0,slot//2,slot%2)

def y_step(core,slot):
    return jnp.where(core==0,slot%2,slot//2)

def slots(three):
    keep,first,second=three
    return (keep.at[0],second.at[0],first.at[0],second.at[1])

def place_qkv_weights(info, mine_ref, theirs_ref, w_s):
    row=info[0]; c=info[3]
    half=mine_ref.shape[1]
    for r in range(4):
        k=xor(r,row)
        w_s[pl.ds(pl.multiple_of((2*r+c)*half,32),half),:]=mine_ref[row_step(c,k)]
        w_s[pl.ds(pl.multiple_of((2*r+1-c)*half,32),half),:]=theirs_ref[row_step(1-c,k)]

def place_tokens(info, x_ref, slot, x_s):
    feat=x_ref.shape[1]; c=info[3]; base=xor(info[0],z_step(c,slot))
    for r in range(4):
        x_s[r*feat:(r+1)*feat,:]=x_ref[row_step(c,xor(r,base))]

def token_refs(own, second, others):
    return (own, second, others.at[0], others.at[1])

def qkv_kernel(info, xa,xb,xc, mine_ref, theirs_ref, cos_ref, sin_ref, q_ref, kv_ref, w_s, wt_s, x_s):
    place_qkv_weights(info,mine_ref,theirs_ref,w_s)
    wt_s[...]=w_s[...].T
    hw=q_ref.shape[0]; n=xa.shape[2]
    for k,xr in enumerate(token_refs(xa,xb,xc)):
        place_tokens(info,xr,k,x_s)
        out=mm(wt_s[...],x_s[...])
        sl=slice(k*n,(k+1)*n)
        cos=cos_ref[:,sl]; sin=sin_ref[:,sl]
        for h in range(2*hw//HD):
            turned=pair_turn(out[h*HD:(h+1)*HD],cos,sin)
            if h*HD<hw: q_ref[h*HD:(h+1)*HD,sl]=(turned*(HD**-0.5*LOG2E)).astype(bf16)
            else: kv_ref[h*HD-hw:(h+1)*HD-hw,sl]=turned.astype(bf16)
        kv_ref[hw:,sl]=out[2*hw:].astype(bf16)

VM=pl.BlockSpec(memory_space=pltpu.VMEM)
SM=pl.BlockSpec(memory_space=pltpu.SMEM)
HB=pl.BlockSpec(memory_space=pl.ANY)

def qkv(info,xs,mine,theirs,cos,sin):
    _,feat,n=xs[0].shape; w3=mine.shape[2]; hw=w3//3; width=4*feat
    return pl.pallas_call(qkv_kernel,in_specs=[SM]+[VM]*7,out_specs=[VM,VM],
        out_shape=[jax.ShapeDtypeStruct((hw,4*n),bf16),jax.ShapeDtypeStruct((2*hw,4*n),bf16)],
        scratch_shapes=[pltpu.VMEM((width,w3),bf16),pltpu.VMEM((w3,width),bf16),pltpu.VMEM((width,n),bf16)],
        name="qkv")(info,*xs,mine,theirs,cos,sin)

def finish_dx_kernel(info, *refs):
    (q0,q1,q2,o0,o1,o2,r0,r1,r2,mine_ref,theirs_ref,cos_ref,sin_ref,keep_ref,send_ref,p_ref,w_s)=refs
    hw=3*HD; n=keep_ref.shape[3]; feat=keep_ref.shape[2]; c=info[3]
    place_qkv_weights(info,mine_ref,theirs_ref,w_s)
    for h,(qr,orr,rr) in enumerate(((q0,o0,r0),(q1,o1,r1),(q2,o2,r2))):
        p_ref[h*HD:(h+1)*HD,:]=qr[...]
        t=(orr[...]+rr[...].astype(f32)).T
        p_ref[hw+h*HD:hw+(h+1)*HD,:]=pair_turn(t[:HD]*LN2,cos_ref[...],-sin_ref[...]).astype(bf16)
        p_ref[2*hw+h*HD:2*hw+(h+1)*HD,:]=t[HD:].astype(bf16)
    for k,dr in ((3,send_ref),(2,send_ref),(1,keep_ref),(0,keep_ref)):
        sl=slice(k*n,(k+1)*n)
        base=xor(info[0],z_step(c,k))
        for r in range(4):
            dr[k%2,row_step(c,xor(r,base))]=mm(w_s[r*feat:(r+1)*feat,:],p_ref[:,sl]).astype(dr.dtype)

def finish_dx(info,dqs,owns,gots,mine,theirs,cos,sin):
    w3=mine.shape[2]; half=mine.shape[1]; feat=2*half; width=4*feat; n=dqs[0].shape[1]//4
    S=jax.ShapeDtypeStruct
    return pl.pallas_call(finish_dx_kernel,in_specs=[SM]+[VM]*13,out_specs=[VM]*3,
        out_shape=[S((2,4,feat,n),f32),S((2,4,feat,n),bf16),S((w3,4*n),bf16)],
        scratch_shapes=[pltpu.VMEM((width,w3),bf16)],
        cost_estimate=pl.CostEstimate(flops=int(6.0*(8*width*w3*n))+1,bytes_accessed=int(6.0*(8*width*n*4))+1,transcendentals=int(6.0*(0))+1),
        name="finish_dx")(info,*dqs,*owns,*gots,mine,theirs,cos,sin)

def finish_dw_kernel(info, p_ref, xa,xb,xc, keep_ref, give_ref, x_s, g_s):
    n=xa.shape[2]; half=keep_ref.shape[1]
    for k,xr in enumerate(token_refs(xa,xb,xc)):
        place_tokens(info,xr,k,x_s.at[:,k*n:(k+1)*n])
    g_s[...]=mm(x_s[...],p_ref[...],NT)
    c=info[3]; row=info[0]
    for r in range(4):
        mine_rows=pl.ds(pl.multiple_of((2*r+c)*half,32),half); their_rows=pl.ds(pl.multiple_of((2*r+1-c)*half,32),half)
        keep_ref[xor(r,row)]=g_s[mine_rows,:]
        give_ref[xor(r,row)]=g_s[their_rows,:].astype(bf16)

def finish_dw(info,proj,xs):
    _,feat,n=xs[0].shape; w3=proj.shape[0]; width=4*feat; half=feat//2
    return pl.pallas_call(finish_dw_kernel,in_specs=[SM]+[VM]*4,out_specs=[VM]*2,
        out_shape=[jax.ShapeDtypeStruct((4,half,w3),f32),jax.ShapeDtypeStruct((4,half,w3),bf16)],
        scratch_shapes=[pltpu.VMEM((width,4*n),bf16),pltpu.VMEM((width,w3),f32)],
        cost_estimate=pl.CostEstimate(flops=int(6.0*(8*width*w3*n))+1,bytes_accessed=int(6.0*(8*width*n*2))+1,transcendentals=int(6.0*(0))+1),
        name="finish_dw")(info,proj,*xs)

def middle_kernel(info, a0,a1,a2, x_ref, c0,c1,c2, *refs):
    chunk_a=refs[:8]; chunk_b=refs[8:16]
    (mixk_ref, mixs_ref, ek_ref, es_ref, g1_ref, attnT_ref, hidT_ref, outT_ref, bl_ref, act_ref, il_ref, norm_ref,
                  win, woT, wo, ns, gp_s, t_s, f_s, sems)=refs[16:]
    row=info[0]; z=info[1]; y=info[2]; c=info[3]; group=info[5]
    feat=a0.shape[1]; n=a0.shape[2]; width=4*feat; ffc=chunk_a[0].shape[2]; half=feat//2; fh=ffc//2; third=half//3
    def go(src,dst,s): pltpu.make_async_copy(src,dst,sems.at[s]).start()
    def each(chunk):
        for kc in range(2):
            core=xor(c,kc)
            for spot,ref in enumerate(chunk[4*kc:4*kc+4]):
                first,second=spot%2,spot//2
                kx=jnp.where(core==0,second,first); ky=jnp.where(core==0,first,second)
                g=xor(group,kx); col=xor(y,ky)*2+core
                for i in range(4):
                    step=row_step(core,i)
                    yield ref.at[i],xor(row,step),g,col,kc+spot
    for ref,r,g,col,_ in each(chunk_a):
        for j in range(3):
            go(ref.at[half:half+third,j*256:(j+1)*256],wo.at[r,pl.ds(pl.multiple_of((col*2+g)*half+j*third,16),third),:],0)
    for ref,r,g,col,where in each(chunk_a):
        if where==0:
            go(ref.at[half+third:half+third+16,:],ns.at[r],3)
    for ref,r,g,col,_ in each(chunk_a):
        go(ref.at[0:half,:],win.at[pl.ds(pl.multiple_of(r*feat+g*half,16),half),pl.ds(pl.multiple_of(col*ffc,128),ffc)],1)
    for ref,r,g,col,_ in each(chunk_b):
        for t in range(2):
            go(ref.at[:,t*fh:(t+1)*fh],woT.at[pl.ds(pl.multiple_of(r*feat+t*half,16),half),pl.ds(pl.multiple_of((col*2+g)*fh,128),fh)],2)
    def group_of(s):
        return xor(y,y_step(c,s))*2+xor(z,z_step(c,s))
    def row_of(s):
        return xor(row,row_step(c,s))
    for s,ar in enumerate(slots((a0,a1,a2))):
        attnT_ref[rows_at(group_of(s),feat,64),:]=ar[...]
    for s in range(4):
        t_s[rows_at(row_of(s),feat,64),:]=x_ref[s]
    attn=attnT_ref[...].T
    x=t_s[...].T.astype(f32)
    pltpu.make_async_copy(wo,wo,sems.at[0]).wait()
    pltpu.make_async_copy(ns,ns,sems.at[3]).wait()
    def vector(which):
        out=[]
        for r in range(4):
            v=ns[r].astype(f32)[0:3,which*feat:(which+1)*feat]
            out.append(jnp.sum(v,axis=0,keepdims=True))
        return jnp.concatenate(out,axis=1)
    gain1=vector(0); shift1=vector(1); gain2=vector(2); shift2=vector(3)
    branch=jnp.concatenate([mm(attn,wo[r])[:,:feat] for r in range(4)],axis=1)
    def stats(v):
        mean=jnp.sum(v,axis=1,keepdims=True)*(1.0/width)
        var=jnp.sum(v*v,axis=1,keepdims=True)*(1.0/width)-mean*mean
        inv=lax.rsqrt(var+1e-5)
        return (v-mean)*inv,inv
    cent1,inv1=stats(x+branch)
    hidden=cent1*gain1+shift1
    hid=hidden.astype(bf16)
    hidT_ref[...]=hid.T
    pltpu.make_async_copy(win,win,sems.at[1]).wait()
    pltpu.make_async_copy(woT,woT,sems.at[2]).wait()
    f_s[...]=jnp.zeros_like(f_s)
    nb=2; bw=ffc//nb
    def forward(j,carry):
        sl=pl.ds(pl.multiple_of(j*bw,128),bw)
        inner=mm(hid,win[:,sl])
        cdf=0.5+0.5*lax.erf(inner*0.7071067811865476)
        act=(inner*cdf).astype(bf16)
        gp_s[:,sl]=cdf+inner*(jnp.exp(inner*inner*-0.5)*0.3989422804014327)
        act_ref[:,sl]=act
        f_s[...]+=mm(act,woT[:,sl],NT)
        return carry
    lax.fori_loop(0,4*nb,forward,0)
    cent2,inv2=stats(hidden+f_s[...])
    t_s[...]=(cent2*gain2+shift2).astype(bf16).T
    for s in range(4):
        (mixk_ref,mixs_ref)[s//2][s%2]=t_s[rows_at(row_of(s),feat,64),:]
    for s,cr in enumerate(slots((c0,c1,c2))):
        t_s[rows_at(row_of(s),feat,64),:]=cr[...]
    valid=(lax.broadcasted_iota(jnp.int32,(n,1),0)<info[4]).astype(f32)
    cot=t_s[...].T.astype(f32)*valid
    sums2=(jnp.sum(cot*cent2,axis=0,keepdims=True),jnp.sum(cot,axis=0,keepdims=True))
    def back(e,cent,inv):
        first=jnp.sum(e,axis=1,keepdims=True)*(1.0/width)
        second=jnp.sum(e*cent,axis=1,keepdims=True)*(1.0/width)
        return inv*(e-first-cent*second)
    grad2=back(cot*gain2,cent2,inv2)
    low=grad2.astype(bf16)
    outT_ref[...]=low.T
    f_s[...]=grad2
    def backward(j,carry):
        sl=pl.ds(pl.multiple_of(j*bw,128),bw)
        il=(mm(low,woT[:,sl])*gp_s[:,sl]).astype(bf16)
        il_ref[:,sl]=il
        f_s[...]+=mm(il,win[:,sl],NT)
        return carry
    lax.fori_loop(0,4*nb,backward,0)
    gh=f_s[...]
    sums=jnp.concatenate((jnp.sum(gh*cent1,axis=0,keepdims=True),jnp.sum(gh,axis=0,keepdims=True))+sums2+(jnp.zeros((4,width),f32),),axis=0)
    for r in range(4):
        norm_ref[r]=sums[:,r*feat:(r+1)*feat]
    grad1=back(gh*gain1,cent1,inv1)
    bl=grad1.astype(bf16)
    padded=jnp.concatenate([bl,jnp.zeros((n,256-feat),bf16)],axis=1)
    da=jnp.zeros((width,n),f32)
    for r in range(4):
        piece=padded[:,r*feat:r*feat+256]
        bl_ref[r]=piece
        da=da+mm(wo[r],piece,NT)
    t_s[...]=da.astype(bf16)
    for s in range(4):
        (ek_ref,es_ref)[s//2][s%2]=t_s[rows_at(group_of(s),feat,64),:]
    f2=grad1.T
    for r in range(4):
        g1_ref[row_step(c,xor(r,row))]=f2[r*feat:(r+1)*feat]

def middle(info,attn_parts,x_own,cot_parts,chunk_a,chunk_b):
    _,feat,n=attn_parts[0].shape; width=4*feat; ff=4*chunk_a[0].shape[2]
    S=jax.ShapeDtypeStruct
    return pl.pallas_call(middle_kernel,in_specs=[SM]+[VM]*7+[HB]*16,out_specs=[VM]*12,
        out_shape=[S((2,feat,n),bf16)]*4+[S((4,feat,n),f32),S((width,n),bf16),S((width,n),bf16),S((width,n),bf16),
                   S((4,n,256),bf16),S((n,ff),bf16),S((n,ff),bf16),S((4,8,feat),f32)],
        scratch_shapes=[pltpu.VMEM((width,ff),bf16),pltpu.VMEM((width,ff),bf16),pltpu.VMEM((4,width,256),bf16),pltpu.VMEM((4,16,width),bf16),
                        pltpu.VMEM((n,ff),f32),pltpu.VMEM((width,n),bf16),pltpu.VMEM((n,width),f32),pltpu.SemaphoreType.DMA((4,))],
        compiler_params=pltpu.CompilerParams(vmem_limit_bytes=56*1024*1024),
        cost_estimate=pl.CostEstimate(flops=int(6.0*(12*n*width*ff*2))+1,bytes_accessed=int(6.0*(24*width*ff))+1,transcendentals=int(6.0*(2*n*ff))+1),
        name="middle")(info,*attn_parts,x_own,*cot_parts,*chunk_a,*chunk_b)

def plane_target(info,core,slot):
    kx=jnp.where(core==0,slot//2,slot%2); ky=jnp.where(core==0,slot%2,slot//2)
    return xor(info[5],kx),xor(info[2],ky)*2+core

def target(info,which,a,b):
    core=xor(info[3],which)
    return (core,)+plane_target(info,core,2*a+b)

def outer_blocks(info,which,a,b,refs,put):
    outT_ref,act_near,act_far=refs
    core=xor(info[3],which)
    half=outT_ref.shape[0]//8; fh=act_near.shape[1]//2
    rows=outT_ref[rows_at(xor(info[0],row_step(core,2*a+b)),2*half,64),:]
    for ky,act_ref in enumerate((act_near,act_far)):
        value=mm(rows,act_ref[...])
        for g in range(2):
            kx=xor(g,info[5])
            slot=jnp.where(core==0,2*kx+ky,2*ky+kx)
            for t in range(2):
                put(slot,slice(0,half),slice(t*fh,(t+1)*fh),value[t*half:(t+1)*half,g*fh:(g+1)*fh])

def inner_blocks(info,which,a,b,refs,put):
    hidT_ref,il_ref,attnT_ref,bl_ref,norm_ref=refs
    core,g,col=target(info,which,a,b)
    half=hidT_ref.shape[0]//8; third=half//3
    rows=[xor(info[0],row_step(core,s)) for s in range(4)]
    lhs=jnp.concatenate([hidT_ref[rows_at(r*2+g,half,32),:] for r in rows],axis=0)
    value=mm(lhs,il_ref[...])
    heads=attnT_ref[rows_at(col*2+g,half,32),:]
    for s,r in enumerate(rows):
        put(s,slice(0,half),slice(None),value[s*half:(s+1)*half])
        outs=mm(heads,bl_ref[r])
        for j in range(3):
            put(s,slice(half,half+third),slice(j*256,(j+1)*256),outs[j*third:(j+1)*third])
        line=jnp.concatenate([norm_ref[r][i:i+1] for i in range(4)],axis=1)
        put(s,slice(half+third,half+third+16),slice(None),jnp.concatenate([line,jnp.zeros((15,line.shape[1]),f32)],axis=0))

def give_kernel(blocks,info,*refs):
    out=refs[-1]
    def put(s,rows,lanes,value): out[0,0,s,rows,lanes]=value.astype(bf16)
    blocks(info,1,pl.program_id(0),pl.program_id(1),refs[:-1],put)

def first_kernel(blocks,info,*refs):
    got,out=refs[-2:]
    def put(s,rows,lanes,value): out[0,s,rows,lanes]=(value+got[0,0,s,rows,lanes].astype(f32)).astype(bf16)
    blocks(info,0,1,pl.program_id(0),refs[:-2],put)

def second_kernel(blocks,info,*refs):
    got,came,keep,send=refs[-4:]
    for b,out in ((0,keep),(1,send)):
        def put(s,rows,lanes,value):
            out[s,rows,lanes]=(value+got[0,0,s,rows,lanes].astype(f32)+came[0,s,rows,lanes].astype(f32)).astype(bf16)
        @pl.when(pl.program_id(0)==b)
        def _(): blocks(info,0,0,b,refs[:-4],put)

def grad_call(kind,stage,info,args,got=None,came=None):
    S=jax.ShapeDtypeStruct
    width,n=args[0].shape; ffc=args[1].shape[1]//4; half=width//8
    a={"give":None,"first":1,"second":0}[stage]; which=1 if stage=="give" else 0
    def at(index):
        if stage=="give": return lambda i,j,s:index(i,j,s)
        return lambda j,s:index(a,j,s)
    whole=pl.BlockSpec((width,n),at(lambda i,j,s:(0,0)))
    if kind=="inner":
        blocks,rows=inner_blocks,half+half//3+16
        specs=[whole,pl.BlockSpec((n,ffc),at(lambda i,j,s:(0,target(s,which,i,j)[2]))),whole,
               pl.BlockSpec((4,n,256),at(lambda i,j,s:(0,0,0))),pl.BlockSpec((4,8,width//4),at(lambda i,j,s:(0,0,0)))]
    else:
        blocks,rows=outer_blocks,half
        args=(args[0],args[1],args[1])
        def column(ky): return at(lambda i,j,s:(0,xor(s[2],ky)*2+xor(s[3],which)))
        specs=[whole,pl.BlockSpec((n,ffc),column(0)),pl.BlockSpec((n,ffc),column(1))]
    cost=pl.CostEstimate(flops=int(6.0*((4 if stage=="give" else 2)*width*n*ffc))+1,bytes_accessed=int(6.0*(16*rows*ffc))+1,transcendentals=int(6.0*(0))+1)
    name=kind+"_"+stage
    five=(1,1,4,rows,ffc)
    if stage=="give":
        return pl.pallas_call(functools.partial(give_kernel,blocks),
            grid_spec=pltpu.PrefetchScalarGridSpec(num_scalar_prefetch=1,grid=(2,2),in_specs=specs,out_specs=pl.BlockSpec(five,lambda i,j,s:(i,j,0,0,0))),
            out_shape=S((2,2,4,rows,ffc),bf16),cost_estimate=cost,name=name)(info,*args)
    got_spec=pl.BlockSpec(five,lambda j,s:(a,j,0,0,0)); one=pl.BlockSpec((1,4,rows,ffc),lambda j,s:(j,0,0,0))
    if stage=="first":
        return pl.pallas_call(functools.partial(first_kernel,blocks),
            grid_spec=pltpu.PrefetchScalarGridSpec(num_scalar_prefetch=1,grid=(2,),in_specs=specs+[got_spec],out_specs=one),
            out_shape=S((2,4,rows,ffc),bf16),cost_estimate=cost,name=name)(info,*args,got)
    full=pl.BlockSpec((4,rows,ffc),lambda j,s:(0,0,0))
    return pl.pallas_call(functools.partial(second_kernel,blocks),
        grid_spec=pltpu.PrefetchScalarGridSpec(num_scalar_prefetch=1,grid=(2,),in_specs=specs+[got_spec,one],out_specs=[full,full]),
        out_shape=[S((4,rows,ffc),bf16)]*2,cost_estimate=cost,name=name)(info,*args,got,came)

def core_swap(value):
    return lax.ppermute(value, "cc", [(0, 1), (1, 0)])


def swap_by(blocks, index):
    pairs = blocks.reshape((2, 2) + blocks.shape[1:])
    pairs = jnp.where((index // 2) == 1, pairs[::-1], pairs)
    pairs = jnp.where((index % 2) == 1, pairs[:, ::-1], pairs)
    return pairs.reshape(blocks.shape)


def dp_halves(value, c):
    if lax.axis_size("dp") != 2:
        whole = lax.all_gather(value, "dp", axis=0, tiled=True)
        halves = whole.reshape((2, whole.shape[0] // 2) + whole.shape[1:])
        return jnp.where(c == 0, halves[0], halves[1]), jnp.where(c == 0, halves[1], halves[0])
    other = swap2(value, "dp")
    same = lax.axis_index("dp") == c
    return jnp.where(same, value, other), jnp.where(same, other, value)


def dp_sum(this_half, other_half, c):
    if lax.axis_size("dp") != 2:
        whole = jnp.concatenate(
            [jnp.where(c == 0, this_half, other_half), jnp.where(c == 0, other_half, this_half)], axis=0
        )
        return lax.psum_scatter(whole.astype(bf16), "dp", scatter_dimension=0, tiled=True).astype(f32)
    same = lax.axis_index("dp") == c
    keep = jnp.where(same, this_half, other_half)
    return keep + swap2(jnp.where(same, other_half, this_half).astype(bf16), "dp").astype(f32)


def pack_outer(part):
    turned = part.T
    half = turned.shape[0] // 2
    return jnp.concatenate([turned[:half], turned[half:]], axis=1)


def unpack_outer(packed):
    wide = packed.shape[1] // 2
    return jnp.concatenate([packed[:, :wide], packed[:, wide:]], axis=0).T


def pack_output(part):
    third = part.shape[0] // 3
    padded = jnp.pad(part, ((0, 0), (0, 256 - part.shape[1])))
    return jnp.concatenate([padded[j * third : (j + 1) * third] for j in range(3)], axis=1)


def unpack_output(packed, feat):
    return jnp.concatenate([packed[:, j * 256 : j * 256 + feat] for j in range(3)], axis=0)


def pack_norms(first_gain, first_shift, second_gain, second_shift):
    line = jnp.concatenate([first_gain, first_shift, second_gain, second_shift])
    high = lax.reduce_precision(line, 8, 7)
    middle_part = lax.reduce_precision(line - high, 8, 7)
    rest = line - high - middle_part
    rows = jnp.stack([high, middle_part, rest]).astype(bf16)
    return jnp.pad(rows, ((0, 13), (0, 0)))


def after(value, *earlier):
    return lax.optimization_barrier((value,) + earlier)[0]


def swap2(value, axis):
    return lax.ppermute(value, axis, [(0, 1), (1, 0)])


def crossed(value, axes, first):
    pairs = []
    for u in range(2):
        for v in range(2):
            for core in range(2):
                along = first ^ core
                pairs.append(((u * 2 + v) * 2 + core, ((u ^ (1 - along)) * 2 + (v ^ along)) * 2 + core))
    return lax.ppermute(value, axes + ("cc",), pairs)


PLANE = ("dp", "cy")


def scatter_steps(keep, send, axes, *between):
    first = after(crossed(send, axes, 0), *between)
    second = crossed(jnp.stack([keep[1], first[1]]), axes, 1)
    return keep, first, second


def by_slot(three):
    keep, first, second = three
    return [keep[0], second[0], first[0], second[1]]


def row_pair(block, *between):
    return jnp.stack([block, after(crossed(block, ROW, 1), *between)])


def row_rest(pair, *between):
    return jnp.concatenate([pair, after(crossed(pair, ROW, 0), *between)], axis=0)


def plane_gather(stack, forward_after):
    near = crossed(stack, PLANE, 1)
    far = crossed(stack, PLANE, 0)
    both = crossed(after(near, *forward_after), PLANE, 0)
    return [stack, near, far, both]


def core_copies(arrays, ties):
    return arrays + [core_swap(after(array, *tie)) for array, tie in zip(arrays, ties)]


def gather_generic(w_output, w_inner, w_outer, norms, row, y, c):
    inner, outer, output = (lax.all_gather(w, "dp", axis=0, tiled=True) for w in (w_inner, w_outer, w_output))
    chunks = []
    for which in range(2):
        halves = []
        for g in range(2):
            parts = [w.reshape((2, w.shape[0] // 2) + w.shape[1:])[g] for w in (inner, outer, output)]
            if which == 0:
                halves.append(jnp.concatenate([parts[0], pack_output(parts[2]), norms], axis=0))
            else:
                halves.append(pack_outer(parts[1]))
        whole = lax.all_gather(jnp.stack(halves), GROUP)
        flat = whole.reshape((-1,) + whole.shape[2:])
        arrays = []
        for kc in range(2):
            core = c ^ kc
            for spot in range(4):
                first, second = spot % 2, spot // 2
                kx = jnp.where(core == 0, second, first)
                ky = jnp.where(core == 0, first, second)
                steps = [jnp.where(core == 0, i, (i % 2) * 2 + i // 2) for i in range(4)]
                spots = jnp.stack([((row ^ k) * 4 + (y ^ ky) * 2 + core) * 2 + kx for k in steps])
                arrays.append(jnp.take(flat, spots, axis=0))
        chunks.append(arrays)
    return chunks


def add_parts(parts):
    total = parts[0].astype(f32)
    for part in parts[1:]:
        total = total + part.astype(f32)
    return total


def halve(stack):
    pass_on = crossed(stack[2:], ROW, 0)
    pair = (stack[:2].astype(f32) + pass_on.astype(f32)).astype(bf16)
    return pair[0].astype(f32) + crossed(pair[1], ROW, 1).astype(f32)


def generic_inner(first, keep, send, c):
    parts = [keep, send, first[0], first[1]]
    by_x = [
        (parts[0], jnp.where(c == 0, parts[1], parts[2])),
        (jnp.where(c == 0, parts[2], parts[1]), parts[3]),
    ]
    planes = [add_parts([own, swap2(other, "cy")]).astype(bf16) for own, other in by_x]
    return [halve(plane) for plane in planes]


def generic_outer(row_sum, c):
    by_x = [
        (row_sum[0], jnp.where(c == 0, row_sum[1], row_sum[2])),
        (jnp.where(c == 0, row_sum[2], row_sum[1]), row_sum[3]),
    ]
    return [add_parts([own, swap2(other, "cy")]) for own, other in by_x]


def local(
    tokens, w_query, w_key, w_value, w_output, w_inner, w_outer,
    first_gain, first_shift, second_gain, second_shift, seq_lengths, out_grad,
):
    feat = tokens.shape[1]
    cols = tokens.shape[2]
    half = cols // 2
    head_width = w_query.shape[1]
    two = lax.axis_size("dp") == 2
    row = lax.axis_index(ROW)
    group = lax.axis_index("dp")
    m = lax.axis_index("rm")
    z = lax.axis_index("rz")
    y = lax.axis_index("cy")
    c = lax.axis_index("cc")
    length = lax.dynamic_index_in_dim(seq_lengths[m], group, keepdims=False)
    own_start = (y * 2 + c) * cols + z * half
    info = jnp.stack([
        row, z, y, c, length - own_start, group if two else 0 * group, 0 * y, 0 * y,
    ]).astype(jnp.int32)

    def turn(blocks):
        pairs = blocks.reshape((2, 2) + blocks.shape[1:])
        return jnp.where(c == 0, pairs, pairs.swapaxes(0, 1)).reshape(blocks.shape)

    def to_slots(array):
        blocks = array.reshape(2, feat, 2, half).transpose(0, 2, 1, 3).reshape(4, feat, half)
        return turn(swap_by(blocks, row))

    def from_slots(parts):
        back = swap_by(turn(jnp.stack(parts)), row)
        return back.reshape(2, 2, feat, half).transpose(0, 2, 1, 3).reshape(2, feat, cols)

    this_half, other_half = dp_halves(jnp.concatenate([w_query, w_key, w_value], axis=1), c)
    token_blocks = to_slots(tokens)
    x_own = jnp.stack(by_slot(scatter_steps(token_blocks[:2], token_blocks[2:], ROW)))
    other_columns = core_swap(other_half)
    norms = pack_norms(first_gain, first_shift, second_gain, second_shift)
    if two:
        block_a = jnp.concatenate([w_inner, pack_output(w_output), norms], axis=0)
        pair_a = row_pair(block_a)
        block_b = pack_outer(w_outer)
        near_b = crossed(after(block_b, token_blocks), ROW, 1)
    pieces = []
    for s in range(4):
        step = jnp.where(c == 0, s % 2, s // 2)
        pieces.append(jnp.where((z ^ step) == c, this_half, other_columns))
    mine = jnp.stack(by_slot(scatter_steps(jnp.stack(pieces[:2]), jnp.stack(pieces[2:]), ROW)))
    theirs = core_swap(mine)
    if two:
        row_a = row_rest(pair_a)
        x_own = after(x_own, pair_a)
    x_second = crossed(x_own, SQUARE, 1)
    xs = (x_own, x_second, crossed(jnp.stack([x_own, x_second]), SQUARE, 0))
    if two:
        xs = (after(x_own, row_a),) + xs[1:]

    starts = []
    for kc in range(2):
        core = c ^ kc
        for s in range(4):
            z_here = z ^ jnp.where(core == 0, s // 2, s % 2)
            y_here = y ^ jnp.where(core == 0, s % 2, s // 2)
            starts.append((y_here * 2 + core) * cols + z_here * half)
    positions = (jnp.stack(starts)[:, None] + jnp.arange(half, dtype=jnp.int32)[None, :]).reshape(-1)
    invalid = jnp.where(positions < length, 0.0, masked_score)
    bias = jnp.where(jnp.arange(HD)[:, None] == 0, invalid[None, :], 0.0).astype(bf16)
    frequency = 10000.0 ** (-2.0 * jnp.arange(HD // 2, dtype=f32) / HD)
    angles = frequency[:, None] * positions[: 4 * half].astype(f32)[None, :]
    cosine = jnp.repeat(jnp.cos(angles), 2, axis=0)
    sines = jnp.sin(angles)
    sine = jnp.stack([-sines, sines], axis=1).reshape(HD, 4 * half)

    q_rot, kv_own = qkv(info, xs, mine, theirs, cosine, sine)
    kv_other = core_swap(kv_own)
    out_b, log_b, low_b = attend(1, q_rot, kv_own, kv_other, bias)
    out_a, log_a, low_a = attend(0, after(q_rot, low_b), kv_own, kv_other, bias)
    attn_three = scatter_steps(low_a, low_b, SQUARE)
    cot_blocks = after(to_slots(out_grad), kv_own)
    cot_three = scatter_steps(cot_blocks[:2], cot_blocks[2:], ROW, low_a)
    if two:
        arrays_a = plane_gather(row_a, (kv_own,))
        chunk_a = core_copies(arrays_a, [(kv_own,), (low_a,), (low_a,), (low_a,)])
        pair_b = jnp.stack([block_b, after(near_b, kv_own)])
        row_b = row_rest(pair_b, low_b)
        arrays_b = plane_gather(row_b, (low_a,))
        chunk_b = core_copies(arrays_b, [(low_a,), (low_a,), (attn_three[2],), (attn_three[2],)])
    else:
        chunk_a, chunk_b = gather_generic(w_output, w_inner, w_outer, norms, row, y, c)
    mixed_keep, mixed_send, e_keep, e_send, grad_one, attn_t, hidden_t, outer_t, branch_low, act_low, inner_low, norm_sums = middle(
        info, attn_three, x_own, cot_three, chunk_a, chunk_b
    )
    inner_args = (hidden_t, inner_low, attn_t, branch_low, norm_sums)
    outer_args = (outer_t, act_low)

    def tied(args, *earlier):
        return (after(args[0], *earlier),) + args[1:]

    def head_back(head, *earlier):
        return attend_back(
            head, after(q_rot, *earlier), kv_own, kv_other, bias, (out_a, out_b), (log_a, log_b), grads, cosine, sine
        )

    give_outer = grad_call("outer", "give", info, outer_args)
    got_outer = core_swap(give_outer)
    grads_first = after(crossed(e_send, SQUARE, 0), give_outer)
    grads_pass = jnp.stack([e_keep[1], grads_first[1]])
    grads = (e_keep, grads_first, crossed(grads_pass, SQUARE, 1))
    give_inner = grad_call("inner", "give", info, tied(inner_args, give_outer, grads_pass))
    got_inner = core_swap(give_inner)
    first_outer = grad_call("outer", "first", info, tied(outer_args, give_inner, grads[2]), got_outer)
    came_outer = crossed(first_outer, ROW, 0)
    first_inner = grad_call("inner", "first", info, tied(inner_args, first_outer), got_inner)
    came_inner = crossed(first_inner, PLANE, 0) if two else jnp.zeros_like(first_inner)
    dq0, own0, send0 = head_back(0, first_inner)
    dq1, own1, send1 = head_back(1, dq0)
    keep_outer, pass_outer = grad_call(
        "outer", "second", info, tied(outer_args, dq1), got_outer, after(came_outer, dq1)
    )
    keep_inner, pass_inner = grad_call(
        "inner", "second", info, tied(inner_args, keep_outer), got_inner, after(came_inner, keep_outer)
    )
    dq2, own2, send2 = head_back(2, keep_inner)
    if two:
        plane_inner = add_parts([keep_inner, after(crossed(pass_inner, PLANE, 1), dq2)]).astype(bf16)
        pass_on_inner = crossed(plane_inner[2:], ROW, 0)
        own2 = after(own2, plane_inner)
    gots = [core_swap(send) for send in (send0, send1, send2)]
    dx_keep, dx_send, proj = finish_dx(info, (dq0, dq1, dq2), (own0, own1, own2), gots, mine, theirs, cosine, sine)
    dx_first = crossed(dx_send, SQUARE, 0)
    if two:
        pair_inner = (plane_inner[:2].astype(f32) + after(pass_on_inner, dx_keep).astype(f32)).astype(bf16)
        last_inner = crossed(pair_inner[1], ROW, 1)
        proj = after(proj, pair_inner)
    keep, give = finish_dw(info, after(proj, dx_keep), xs)
    got = core_swap(give)
    dx_first = after(dx_first, give)
    dx_pass = (dx_keep[1] + dx_first[1].astype(f32)).astype(bf16)
    dx_second = crossed(dx_pass, SQUARE, 1)
    row_outer = add_parts([keep_outer, after(crossed(pass_outer, ROW, 1), dx_pass)]).astype(bf16)
    if two:
        pass_on_outer = crossed(row_outer[2:], PLANE, 0)
    by_row_step = keep + after(got, row_outer).astype(f32)
    passed_m = swap2(by_row_step[2:].astype(bf16), "rm")
    dx_second = after(dx_second, by_row_step)
    d_x = add_parts([grad_one, dx_keep[0], dx_first[0], dx_second]).astype(bf16)
    d_x_first = crossed(d_x[2:], ROW, 0)
    if two:
        pair_outer = (row_outer[:2].astype(f32) + after(pass_on_outer, d_x).astype(f32)).astype(bf16)
        last_outer = crossed(pair_outer[1], PLANE, 1)
        passed_m = after(passed_m, pair_outer)
    near_far = by_row_step[:2] + passed_m.astype(f32)
    near_sum = near_far[0]
    far_low = swap2(near_far[1].astype(bf16), "rz")
    d_x_first = after(d_x_first, near_far)
    d_x_second = crossed(jnp.stack([d_x[1], d_x_first[1]]), ROW, 1)
    far_sum = after(far_low, d_x_first).astype(f32)
    d_input = from_slots(by_slot((d_x[:2], d_x_first, d_x_second))).astype(f32)
    if two:
        inner_sums = [pair_inner[0].astype(f32) + after(last_inner, far_sum).astype(f32)]
        outer_sums = [pair_outer[0].astype(f32) + after(last_outer, far_sum).astype(f32)]
    else:
        outer_sums = generic_outer(row_outer, c)
        inner_sums = generic_inner(first_inner, keep_inner, pass_inner, c)
    mixed_three = scatter_steps(after(mixed_keep, give_outer), after(mixed_send, give_outer), ROW, dq0)
    mixed_out = from_slots(by_slot([after(part, give) for part in mixed_three]))
    kept = jnp.where(z == c, near_sum, far_sum)
    passed = core_swap(jnp.where(z == c, far_sum, near_sum).astype(bf16)).astype(f32)
    g_qkv = dp_sum(kept, passed, c)

    half_rows = feat // 2
    third = half_rows // 3
    g_outer = jnp.concatenate([unpack_outer(part) for part in outer_sums], axis=0)
    g_inner = jnp.concatenate([part[:half_rows] for part in inner_sums], axis=0)
    g_output = jnp.concatenate(
        [unpack_output(part[half_rows : half_rows + third], feat) for part in inner_sums], axis=0
    )
    g_norms = inner_sums[0][half_rows + third].reshape(4, feat)
    if not two:
        g_outer, g_inner, g_output = (
            lax.psum_scatter(g.astype(bf16), "dp", scatter_dimension=0, tiled=True).astype(f32)
            for g in (g_outer, g_inner, g_output)
        )
        g_norms = lax.psum(g_norms, "dp")

    return (
        mixed_out, d_input,
        g_qkv[:, :head_width], g_qkv[:, head_width : 2 * head_width], g_qkv[:, 2 * head_width :],
        g_output, g_inner, g_outer,
        g_norms[0], g_norms[1], g_norms[2], g_norms[3],
    )


def solution(mesh):
    shape = mesh.devices.shape
    fine = Mesh(mesh.devices.reshape(shape[0], 2, shape[1] // 2, 2, shape[2] // 2), EVERY)
    col = ("cy", "cc")
    acts = P(None, ROW, ("dp",) + col)
    by_row = P(ROW + ("dp",), col)
    by_col = P(col + ("dp",), ROW)
    vec = P(ROW)
    return jax.shard_map(
        local,
        mesh=fine,
        in_specs=(
            acts, by_row, by_row, by_row, by_col, by_row, by_col, vec, vec, vec, vec, P(), acts,
        ),
        out_specs=(
            acts, acts, by_row, by_row, by_row, by_col, by_row, by_col, vec, vec, vec, vec,
        ),
        check_vma=False,
    )
```

```python
import functools

import jax
import jax.numpy as jnp
from jax import lax
from jax.experimental import pallas as pl
from jax.experimental.pallas import tpu as pltpu
from jax.sharding import Mesh, PartitionSpec as P

HD = 64
EVERY = ("dp", "rm", "rz", "cy", "cc")
GROUP = ("rm", "rz", "cy", "cc")
ROW = ("rm", "rz")
SQUARE = ("rz", "cy")
bf16=jnp.bfloat16; f32=jnp.float32
LOG2E=1.4426950408889634
LN2=0.6931471805599453
masked_score=-1e30

def mm(a,b,dims=((1,),(0,))):
    return lax.dot_general(a,b,(dims,((),())),preferred_element_type=f32)
NT=((1,),(1,))

def pair_turn(values, cosine, signed_sine):
    shape = values.shape
    v3 = values.reshape(shape[0]//8, 8, shape[1])
    up = pltpu.roll(v3, 7, 1); down = pltpu.roll(v3, 1, 1)
    even = (lax.broadcasted_iota(jnp.int32, v3.shape, 1) % 2) == 0
    other = jnp.where(even, up, down).reshape(shape)
    return values*cosine + other*signed_sine

KB=1024
QB=2
def one_row(shape, dtype, value=1.0):
    return jnp.where(lax.broadcasted_iota(jnp.int32, shape, 0)==0, value, 0.0).astype(dtype)

def attend_kernel(q_ref, ko_ref, vo_ref, kx_ref, vx_ref, bias_ref, o_ref, lse_ref, low_ref, kaug, vall):
    span=ko_ref.shape[1]
    for part,(kr,vr) in enumerate(((ko_ref,vo_ref),(kx_ref,vx_ref))):
        aug=jnp.concatenate([kr[...], bias_ref[:, part*span:(part+1)*span]],axis=0)
        kaug[part*span:(part+1)*span,:]=aug.T
        vall[:, part*span:(part+1)*span]=vr[...]
    n=q_ref.shape[1]
    qaug=jnp.concatenate([q_ref[...], one_row((HD,n),bf16)],axis=0)
    top=jnp.full((1,n),-3e38,f32); total=jnp.zeros((1,n),f32); acc=jnp.zeros((HD,n),f32)
    s=mm(kaug[0:KB,:],qaug)
    for kb in range(0,2*span,KB):
        following=mm(kaug[kb+KB:kb+2*KB,:],qaug) if kb+KB<2*span else None
        new=jnp.maximum(top,jnp.max(s,axis=0,keepdims=True))
        alpha=jnp.exp2(top-new)
        p=jnp.exp2(s-new)
        total=total*alpha+jnp.sum(p,axis=0,keepdims=True)
        acc=acc*alpha+mm(vall[:,kb:kb+KB],p.astype(bf16))
        top=new
        s=following
    out=acc/total
    o_ref[...]=out
    lse_ref[0]=top+jnp.log2(total)
    low=out.astype(bf16)
    for b in range(2):
        low_ref[b]=low[:,b*(n//2):(b+1)*(n//2)]

def attend(part,q,kv,kvx,bias):
    width,n4=q.shape; heads=width//HD; n=n4//2; span=kv.shape[1]
    kspec=pl.BlockSpec((HD,span),lambda h:(h,0)); vspec=pl.BlockSpec((HD,span),lambda h:(heads+h,0))
    return pl.pallas_call(attend_kernel,grid=(heads,),
        in_specs=[pl.BlockSpec((HD,n),lambda h:(h,part)),kspec,vspec,kspec,vspec,pl.BlockSpec((HD,2*span),lambda h:(0,0))],
        out_specs=[pl.BlockSpec((HD,n),lambda h:(h,0)),pl.BlockSpec((1,1,n),lambda h:(h,0,0)),pl.BlockSpec((2,HD,n//2),lambda h:(0,h,0))],
        out_shape=[jax.ShapeDtypeStruct((width,n),f32),jax.ShapeDtypeStruct((heads,1,n),f32),jax.ShapeDtypeStruct((2,width,n//2),bf16)],
        scratch_shapes=[pltpu.VMEM((2*span,2*HD),bf16),pltpu.VMEM((HD,2*span),bf16)],
        cost_estimate=pl.CostEstimate(flops=int(6.0*(2*width*n4//HD*2*span*256))+1,bytes_accessed=int(6.0*(2*n4*2*span))+1,transcendentals=int(6.0*(heads*n*2*span))+1),
        name="attend")(q,kv,kv,kvx,kvx,bias)

BKB=512
def attend_back_kernel(q_ref, ko_ref, vo_ref, kx_ref, vx_ref, bias_ref, oa_ref, ob_ref, lsea_ref, lseb_ref, g0,g1,g2,g3, cos_ref, sin_ref,
                       dq_ref, own_ref, give_ref, kaug, vtm, kall, acc):
    qb=pl.program_id(1)
    span=ko_ref.shape[1]; n=q_ref.shape[1]
    @pl.when(qb==0)
    def _():
        for part,(kr,vr) in enumerate(((ko_ref,vo_ref),(kx_ref,vx_ref))):
            sl=slice(part*span,(part+1)*span)
            kaug[sl,:]=jnp.concatenate([kr[...], bias_ref[:, sl]],axis=0).T
            vtm[sl,:]=jnp.concatenate([vr[...], jnp.zeros((HD,span),bf16)],axis=0).T
            kall[:,sl]=kr[...]
        acc[...]=jnp.zeros_like(acc)
    q=q_ref[...]
    zeros=jnp.zeros((HD,n),bf16)
    qaug=jnp.concatenate([q, one_row((HD,n),bf16)],axis=0)
    g=jnp.concatenate([jnp.where(qb==0,g0[...],g2[...]),jnp.where(qb==0,g1[...],g3[...])],axis=1)
    o=jnp.where(qb==0,oa_ref[...],ob_ref[...])
    qpad=jnp.concatenate([q,zeros],axis=0).T
    gpad=jnp.concatenate([zeros,g],axis=0).T
    gaug=jnp.concatenate([g,zeros],axis=0)
    delta=jnp.sum(g.astype(f32)*o,axis=0,keepdims=True)
    lse=jnp.where(qb==0,lsea_ref[0],lseb_ref[0])
    dq=jnp.zeros((HD,n),f32)
    s=mm(kaug[0:BKB,:],qaug); dp=mm(vtm[0:BKB,:],gaug)
    for kb in range(0,2*span,BKB):
        last=kb+BKB>=2*span
        s_next=None if last else mm(kaug[kb+BKB:kb+2*BKB,:],qaug)
        dp_next=None if last else mm(vtm[kb+BKB:kb+2*BKB,:],gaug)
        p=jnp.exp2(s-lse)
        ds=(p*(dp-delta)).astype(bf16)
        dq=dq+mm(kall[:,kb:kb+BKB],ds)
        acc[kb:kb+BKB,:]=acc[kb:kb+BKB,:]+mm(ds,qpad)+mm(p.astype(bf16),gpad)
        s=s_next; dp=dp_next
    dq_ref[...]=pair_turn(dq*(HD**-0.5),cos_ref[...],-sin_ref[...]).astype(bf16)
    @pl.when(qb==4//QB-1)
    def _():
        own_ref[...]=acc[:span,:]
        give_ref[...]=acc[span:,:].astype(bf16)

def attend_back(first,count,q,kv,kvx,bias,os,lses,grads,cos,sin):
    width,n4=q.shape; heads=width//HD; n=n4//4*QB; span=kv.shape[1]
    kspec=pl.BlockSpec((HD,span),lambda h,b:(first+h,0)); vspec=pl.BlockSpec((HD,span),lambda h,b:(heads+first+h,0))
    gspec=lambda i:pl.BlockSpec((None,HD,n4//4),lambda h,b:(i,first+h,0)); tb=pl.BlockSpec((HD,n),lambda h,b:(0,b))
    dspec=pl.BlockSpec((None,span,2*HD),lambda h,b:(h,0,0)); ospec=pl.BlockSpec((HD,n),lambda h,b:(first+h,0)); lspec=pl.BlockSpec((1,1,n),lambda h,b:(first+h,0,0))
    return pl.pallas_call(attend_back_kernel,grid=(count,4//QB),
        in_specs=[pl.BlockSpec((HD,n),lambda h,b:(first+h,b)),kspec,vspec,kspec,vspec,pl.BlockSpec((HD,2*span),lambda h,b:(0,0)),ospec,ospec,lspec,lspec,gspec(0),gspec(0),gspec(0),gspec(1),tb,tb],
        out_specs=[pl.BlockSpec((HD,n),lambda h,b:(h,b)),dspec,dspec],
        out_shape=[jax.ShapeDtypeStruct((count*HD,n4),bf16),jax.ShapeDtypeStruct((count,span,2*HD),f32),jax.ShapeDtypeStruct((count,span,2*HD),bf16)],
        scratch_shapes=[pltpu.VMEM((2*span,2*HD),bf16),pltpu.VMEM((2*span,2*HD),bf16),pltpu.VMEM((HD,2*span),bf16),pltpu.VMEM((2*span,2*HD),f32)],
        cost_estimate=pl.CostEstimate(flops=int(6.0*(count*10*n4*2*span*256))+1,bytes_accessed=int(6.0*(count*4*n4*2*span))+1,transcendentals=int(6.0*(count*n4*2*span))+1),
        name="attend_back")(q,kv,kv,kvx,kvx,bias,*os,*lses,grads[0],grads[2],grads[1],grads[2],cos,sin)
def xor(a,b):
    return lax.bitwise_xor(jnp.asarray(a,jnp.int32),jnp.asarray(b,jnp.int32))

def rows_at(index,size,align):
    return pl.ds(pl.multiple_of(index*size,align),size)

def row_step(core,slot):
    return jnp.where(core==0,slot,(slot%2)*2+slot//2)

def z_step(core,slot):
    return jnp.where(core==0,slot//2,slot%2)

def y_step(core,slot):
    return jnp.where(core==0,slot%2,slot//2)

def slots(three):
    keep,first,second=three
    return (keep.at[0],second.at[0],first.at[0],second.at[1])

def place_qkv_weights(info, mine_ref, theirs_ref, w_s):
    row=info[0]; c=info[3]
    half=mine_ref.shape[1]
    for r in range(4):
        k=xor(r,row)
        w_s[pl.ds(pl.multiple_of((2*r+c)*half,32),half),:]=mine_ref[row_step(c,k)]
        w_s[pl.ds(pl.multiple_of((2*r+1-c)*half,32),half),:]=theirs_ref[row_step(1-c,k)]

def place_tokens(info, x_ref, slot, x_s):
    feat=x_ref.shape[1]; c=info[3]; base=xor(info[0],z_step(c,slot))
    for r in range(4):
        x_s[r*feat:(r+1)*feat,:]=x_ref[row_step(c,xor(r,base))]

def token_refs(own, second, others):
    return (own, second, others.at[0], others.at[1])

def qkv_kernel(info, xa,xb,xc, mine_ref, theirs_ref, cos_ref, sin_ref, q_ref, kv_ref, w_s, wt_s, x_s):
    place_qkv_weights(info,mine_ref,theirs_ref,w_s)
    wt_s[...]=w_s[...].T
    hw=q_ref.shape[0]; n=xa.shape[2]
    for k,xr in enumerate(token_refs(xa,xb,xc)):
        place_tokens(info,xr,k,x_s)
        out=mm(wt_s[...],x_s[...])
        sl=slice(k*n,(k+1)*n)
        cos=cos_ref[:,sl]; sin=sin_ref[:,sl]
        for h in range(2*hw//HD):
            turned=pair_turn(out[h*HD:(h+1)*HD],cos,sin)
            if h*HD<hw: q_ref[h*HD:(h+1)*HD,sl]=(turned*(HD**-0.5*LOG2E)).astype(bf16)
            else: kv_ref[h*HD-hw:(h+1)*HD-hw,sl]=turned.astype(bf16)
        kv_ref[hw:,sl]=out[2*hw:].astype(bf16)

VM=pl.BlockSpec(memory_space=pltpu.VMEM)
SM=pl.BlockSpec(memory_space=pltpu.SMEM)
HB=pl.BlockSpec(memory_space=pl.ANY)

def qkv(info,xs,mine,theirs,cos,sin):
    _,feat,n=xs[0].shape; w3=mine.shape[2]; hw=w3//3; width=4*feat
    return pl.pallas_call(qkv_kernel,in_specs=[SM]+[VM]*7,out_specs=[VM,VM],
        out_shape=[jax.ShapeDtypeStruct((hw,4*n),bf16),jax.ShapeDtypeStruct((2*hw,4*n),bf16)],
        scratch_shapes=[pltpu.VMEM((width,w3),bf16),pltpu.VMEM((w3,width),bf16),pltpu.VMEM((width,n),bf16)],
        name="qkv")(info,*xs,mine,theirs,cos,sin)

def finish_dx_kernel(info, *refs):
    (q_ref,own_ref,got_ref,mine_ref,theirs_ref,cos_ref,sin_ref,keep_ref,send_ref,p_ref,w_s)=refs
    hw=q_ref.shape[0]; n=keep_ref.shape[3]; feat=keep_ref.shape[2]; c=info[3]
    place_qkv_weights(info,mine_ref,theirs_ref,w_s)
    p_ref[0:hw,:]=q_ref[...]
    for h in range(hw//HD):
        t=(own_ref[h]+got_ref[h].astype(f32)).T
        p_ref[hw+h*HD:hw+(h+1)*HD,:]=pair_turn(t[:HD]*LN2,cos_ref[...],-sin_ref[...]).astype(bf16)
        p_ref[2*hw+h*HD:2*hw+(h+1)*HD,:]=t[HD:].astype(bf16)
    for k,dr in ((3,send_ref),(2,send_ref),(1,keep_ref),(0,keep_ref)):
        sl=slice(k*n,(k+1)*n)
        base=xor(info[0],z_step(c,k))
        for r in range(4):
            dr[k%2,row_step(c,xor(r,base))]=mm(w_s[r*feat:(r+1)*feat,:],p_ref[:,sl]).astype(dr.dtype)

def finish_dx(info,dq,own,got,mine,theirs,cos,sin):
    w3=mine.shape[2]; half=mine.shape[1]; feat=2*half; width=4*feat; n=dq.shape[1]//4
    S=jax.ShapeDtypeStruct
    return pl.pallas_call(finish_dx_kernel,in_specs=[SM]+[VM]*7,out_specs=[VM]*3,
        out_shape=[S((2,4,feat,n),f32),S((2,4,feat,n),bf16),S((w3,4*n),bf16)],
        scratch_shapes=[pltpu.VMEM((width,w3),bf16)],
        cost_estimate=pl.CostEstimate(flops=int(0.0*(8*width*w3*n))+1,bytes_accessed=int(0.0*(8*width*n*4))+1,transcendentals=int(0.0*(0))+1),
        name="finish_dx")(info,dq,own,got,mine,theirs,cos,sin)

def finish_dw_kernel(info, p_ref, xa,xb,xc, keep_ref, give_ref, x_s, g_s):
    n=xa.shape[2]; half=keep_ref.shape[1]
    for k,xr in enumerate(token_refs(xa,xb,xc)):
        place_tokens(info,xr,k,x_s.at[:,k*n:(k+1)*n])
    g_s[...]=mm(x_s[...],p_ref[...],NT)
    c=info[3]; row=info[0]
    for r in range(4):
        mine_rows=pl.ds(pl.multiple_of((2*r+c)*half,32),half); their_rows=pl.ds(pl.multiple_of((2*r+1-c)*half,32),half)
        keep_ref[xor(r,row)]=g_s[mine_rows,:]
        give_ref[xor(r,row)]=g_s[their_rows,:].astype(bf16)

def finish_dw(info,proj,xs):
    _,feat,n=xs[0].shape; w3=proj.shape[0]; width=4*feat; half=feat//2
    return pl.pallas_call(finish_dw_kernel,in_specs=[SM]+[VM]*4,out_specs=[VM]*2,
        out_shape=[jax.ShapeDtypeStruct((4,half,w3),f32),jax.ShapeDtypeStruct((4,half,w3),bf16)],
        scratch_shapes=[pltpu.VMEM((width,4*n),bf16),pltpu.VMEM((width,w3),f32)],
        cost_estimate=pl.CostEstimate(flops=int(6.0*(8*width*w3*n))+1,bytes_accessed=int(6.0*(8*width*n*2))+1,transcendentals=int(6.0*(0))+1),
        name="finish_dw")(info,proj,*xs)

def middle_kernel(info, a0,a1,a2, x_ref, c0,c1,c2, *refs):
    chunk_a=refs[:8]; chunk_b=refs[8:16]
    (mixk_ref, mixs_ref, ek_ref, es_ref, g1_ref, attnT_ref, hidT_ref, outT_ref, bl_ref, act_ref, il_ref, norm_ref,
                  win, woT, wo, ns, gp_s, t_s, f_s, sems)=refs[16:]
    row=info[0]; z=info[1]; y=info[2]; c=info[3]; group=info[5]
    feat=a0.shape[1]; n=a0.shape[2]; width=4*feat; ffc=chunk_a[0].shape[2]; half=feat//2; fh=ffc//2; third=half//3
    def go(src,dst,s): pltpu.make_async_copy(src,dst,sems.at[s]).start()
    def each(chunk):
        for kc in range(2):
            core=xor(c,kc)
            for spot,ref in enumerate(chunk[4*kc:4*kc+4]):
                first,second=spot%2,spot//2
                kx=jnp.where(core==0,second,first); ky=jnp.where(core==0,first,second)
                g=xor(group,kx); col=xor(y,ky)*2+core
                for i in range(4):
                    step=row_step(core,i)
                    yield ref.at[i],xor(row,step),g,col,kc+spot
    for ref,r,g,col,_ in each(chunk_a):
        for j in range(3):
            go(ref.at[half:half+third,j*256:(j+1)*256],wo.at[r,pl.ds(pl.multiple_of((col*2+g)*half+j*third,16),third),:],0)
    for ref,r,g,col,where in each(chunk_a):
        if where==0:
            go(ref.at[half+third:half+third+16,:],ns.at[r],3)
    for ref,r,g,col,_ in each(chunk_a):
        go(ref.at[0:half,:],win.at[pl.ds(pl.multiple_of(r*feat+g*half,16),half),pl.ds(pl.multiple_of(col*ffc,128),ffc)],1)
    for ref,r,g,col,_ in each(chunk_b):
        for t in range(2):
            go(ref.at[:,t*fh:(t+1)*fh],woT.at[pl.ds(pl.multiple_of(r*feat+t*half,16),half),pl.ds(pl.multiple_of((col*2+g)*fh,128),fh)],2)
    def group_of(s):
        return xor(y,y_step(c,s))*2+xor(z,z_step(c,s))
    def row_of(s):
        return xor(row,row_step(c,s))
    for s,ar in enumerate(slots((a0,a1,a2))):
        attnT_ref[rows_at(group_of(s),feat,64),:]=ar[...]
    for s in range(4):
        t_s[rows_at(row_of(s),feat,64),:]=x_ref[s]
    attn=attnT_ref[...].T
    x=t_s[...].T.astype(f32)
    pltpu.make_async_copy(wo,wo,sems.at[0]).wait()
    pltpu.make_async_copy(ns,ns,sems.at[3]).wait()
    def vector(which):
        out=[]
        for r in range(4):
            v=ns[r].astype(f32)[0:3,which*feat:(which+1)*feat]
            out.append(jnp.sum(v,axis=0,keepdims=True))
        return jnp.concatenate(out,axis=1)
    gain1=vector(0); shift1=vector(1); gain2=vector(2); shift2=vector(3)
    branch=jnp.concatenate([mm(attn,wo[r])[:,:feat] for r in range(4)],axis=1)
    def stats(v):
        mean=jnp.sum(v,axis=1,keepdims=True)*(1.0/width)
        var=jnp.sum(v*v,axis=1,keepdims=True)*(1.0/width)-mean*mean
        inv=lax.rsqrt(var+1e-5)
        return (v-mean)*inv,inv
    cent1,inv1=stats(x+branch)
    hidden=cent1*gain1+shift1
    hid=hidden.astype(bf16)
    hidT_ref[...]=hid.T
    pltpu.make_async_copy(win,win,sems.at[1]).wait()
    pltpu.make_async_copy(woT,woT,sems.at[2]).wait()
    f_s[...]=jnp.zeros_like(f_s)
    nb=2; bw=ffc//nb
    def forward(j,carry):
        sl=pl.ds(pl.multiple_of(j*bw,128),bw)
        inner=mm(hid,win[:,sl])
        cdf=0.5+0.5*lax.erf(inner*0.7071067811865476)
        act=(inner*cdf).astype(bf16)
        gp_s[:,sl]=cdf+inner*(jnp.exp(inner*inner*-0.5)*0.3989422804014327)
        act_ref[:,sl]=act
        f_s[...]+=mm(act,woT[:,sl],NT)
        return carry
    lax.fori_loop(0,4*nb,forward,0)
    cent2,inv2=stats(hidden+f_s[...])
    t_s[...]=(cent2*gain2+shift2).astype(bf16).T
    for s in range(4):
        (mixk_ref,mixs_ref)[s//2][s%2]=t_s[rows_at(row_of(s),feat,64),:]
    for s,cr in enumerate(slots((c0,c1,c2))):
        t_s[rows_at(row_of(s),feat,64),:]=cr[...]
    valid=(lax.broadcasted_iota(jnp.int32,(n,1),0)<info[4]).astype(f32)
    cot=t_s[...].T.astype(f32)*valid
    sums2=(jnp.sum(cot*cent2,axis=0,keepdims=True),jnp.sum(cot,axis=0,keepdims=True))
    def back(e,cent,inv):
        first=jnp.sum(e,axis=1,keepdims=True)*(1.0/width)
        second=jnp.sum(e*cent,axis=1,keepdims=True)*(1.0/width)
        return inv*(e-first-cent*second)
    grad2=back(cot*gain2,cent2,inv2)
    low=grad2.astype(bf16)
    outT_ref[...]=low.T
    f_s[...]=grad2
    def backward(j,carry):
        sl=pl.ds(pl.multiple_of(j*bw,128),bw)
        il=(mm(low,woT[:,sl])*gp_s[:,sl]).astype(bf16)
        il_ref[:,sl]=il
        f_s[...]+=mm(il,win[:,sl],NT)
        return carry
    lax.fori_loop(0,4*nb,backward,0)
    gh=f_s[...]
    sums=jnp.concatenate((jnp.sum(gh*cent1,axis=0,keepdims=True),jnp.sum(gh,axis=0,keepdims=True))+sums2+(jnp.zeros((4,width),f32),),axis=0)
    for r in range(4):
        norm_ref[r]=sums[:,r*feat:(r+1)*feat]
    grad1=back(gh*gain1,cent1,inv1)
    bl=grad1.astype(bf16)
    padded=jnp.concatenate([bl,jnp.zeros((n,256-feat),bf16)],axis=1)
    da=jnp.zeros((width,n),f32)
    for r in range(4):
        piece=padded[:,r*feat:r*feat+256]
        bl_ref[r]=piece
        da=da+mm(wo[r],piece,NT)
    t_s[...]=da.astype(bf16)
    for s in range(4):
        (ek_ref,es_ref)[s//2][s%2]=t_s[rows_at(group_of(s),feat,64),:]
    f2=grad1.T
    for r in range(4):
        g1_ref[row_step(c,xor(r,row))]=f2[r*feat:(r+1)*feat]

def middle(info,attn_parts,x_own,cot_parts,chunk_a,chunk_b):
    _,feat,n=attn_parts[0].shape; width=4*feat; ff=4*chunk_a[0].shape[2]
    S=jax.ShapeDtypeStruct
    return pl.pallas_call(middle_kernel,in_specs=[SM]+[VM]*7+[HB]*16,out_specs=[VM]*12,
        out_shape=[S((2,feat,n),bf16)]*4+[S((4,feat,n),f32),S((width,n),bf16),S((width,n),bf16),S((width,n),bf16),
                   S((4,n,256),bf16),S((n,ff),bf16),S((n,ff),bf16),S((4,8,feat),f32)],
        scratch_shapes=[pltpu.VMEM((width,ff),bf16),pltpu.VMEM((width,ff),bf16),pltpu.VMEM((4,width,256),bf16),pltpu.VMEM((4,16,width),bf16),
                        pltpu.VMEM((n,ff),f32),pltpu.VMEM((width,n),bf16),pltpu.VMEM((n,width),f32),pltpu.SemaphoreType.DMA((4,))],
        compiler_params=pltpu.CompilerParams(vmem_limit_bytes=56*1024*1024),
        cost_estimate=pl.CostEstimate(flops=int(6.0*(12*n*width*ff*2))+1,bytes_accessed=int(6.0*(24*width*ff))+1,transcendentals=int(6.0*(2*n*ff))+1),
        name="middle")(info,*attn_parts,x_own,*cot_parts,*chunk_a,*chunk_b)

def plane_target(info,core,slot):
    kx=jnp.where(core==0,slot//2,slot%2); ky=jnp.where(core==0,slot%2,slot//2)
    return xor(info[5],kx),xor(info[2],ky)*2+core

def target(info,which,a,b):
    core=xor(info[3],which)
    return (core,)+plane_target(info,core,2*a+b)

def outer_blocks(info,which,a,b,refs,put):
    outT_ref,act_near,act_far=refs
    core=xor(info[3],which)
    half=outT_ref.shape[0]//8; fh=act_near.shape[1]//2
    rows=outT_ref[rows_at(xor(info[0],row_step(core,2*a+b)),2*half,64),:]
    for ky,act_ref in enumerate((act_near,act_far)):
        value=mm(rows,act_ref[...])
        for g in range(2):
            kx=xor(g,info[5])
            slot=jnp.where(core==0,2*kx+ky,2*ky+kx)
            for t in range(2):
                put(slot,slice(0,half),slice(t*fh,(t+1)*fh),value[t*half:(t+1)*half,g*fh:(g+1)*fh])

def inner_blocks(info,which,a,b,refs,put):
    hidT_ref,il_ref,attnT_ref,bl_ref,norm_ref=refs
    core,g,col=target(info,which,a,b)
    half=hidT_ref.shape[0]//8; third=half//3
    rows=[xor(info[0],row_step(core,s)) for s in range(4)]
    lhs=jnp.concatenate([hidT_ref[rows_at(r*2+g,half,32),:] for r in rows],axis=0)
    value=mm(lhs,il_ref[...])
    heads=attnT_ref[rows_at(col*2+g,half,32),:]
    for s,r in enumerate(rows):
        put(s,slice(0,half),slice(None),value[s*half:(s+1)*half])
        outs=mm(heads,bl_ref[r])
        for j in range(3):
            put(s,slice(half,half+third),slice(j*256,(j+1)*256),outs[j*third:(j+1)*third])
        line=jnp.concatenate([norm_ref[r][i:i+1] for i in range(4)],axis=1)
        put(s,slice(half+third,half+third+16),slice(None),jnp.concatenate([line,jnp.zeros((15,line.shape[1]),f32)],axis=0))

def give_kernel(blocks,info,*refs):
    out=refs[-1]
    def put(s,rows,lanes,value): out[0,0,s,rows,lanes]=value.astype(bf16)
    blocks(info,1,pl.program_id(0),pl.program_id(1),refs[:-1],put)

def first_kernel(blocks,info,*refs):
    got,out=refs[-2:]
    def put(s,rows,lanes,value): out[0,s,rows,lanes]=(value+got[0,0,s,rows,lanes].astype(f32)).astype(bf16)
    blocks(info,0,1,pl.program_id(0),refs[:-2],put)

def second_kernel(blocks,info,*refs):
    got,came,keep,send=refs[-4:]
    for b,out in ((0,keep),(1,send)):
        def put(s,rows,lanes,value):
            out[s,rows,lanes]=(value+got[0,0,s,rows,lanes].astype(f32)+came[0,s,rows,lanes].astype(f32)).astype(bf16)
        @pl.when(pl.program_id(0)==b)
        def _(): blocks(info,0,0,b,refs[:-4],put)

def grad_call(kind,stage,info,args,got=None,came=None):
    S=jax.ShapeDtypeStruct
    width,n=args[0].shape; ffc=args[1].shape[1]//4; half=width//8
    a={"give":None,"first":1,"second":0}[stage]; which=1 if stage=="give" else 0
    def at(index):
        if stage=="give": return lambda i,j,s:index(i,j,s)
        return lambda j,s:index(a,j,s)
    whole=pl.BlockSpec((width,n),at(lambda i,j,s:(0,0)))
    if kind=="inner":
        blocks,rows=inner_blocks,half+half//3+16
        specs=[whole,pl.BlockSpec((n,ffc),at(lambda i,j,s:(0,target(s,which,i,j)[2]))),whole,
               pl.BlockSpec((4,n,256),at(lambda i,j,s:(0,0,0))),pl.BlockSpec((4,8,width//4),at(lambda i,j,s:(0,0,0)))]
    else:
        blocks,rows=outer_blocks,half
        args=(args[0],args[1],args[1])
        def column(ky): return at(lambda i,j,s:(0,xor(s[2],ky)*2+xor(s[3],which)))
        specs=[whole,pl.BlockSpec((n,ffc),column(0)),pl.BlockSpec((n,ffc),column(1))]
    weight={"give":4,"first":2,"second":0}[stage]
    cost=pl.CostEstimate(flops=int(6.0*(weight*width*n*ffc))+1,bytes_accessed=int(6.0*(4*weight*rows*ffc))+1,transcendentals=int(6.0*(0))+1)
    name=kind+"_"+stage
    five=(1,1,4,rows,ffc)
    if stage=="give":
        return pl.pallas_call(functools.partial(give_kernel,blocks),
            grid_spec=pltpu.PrefetchScalarGridSpec(num_scalar_prefetch=1,grid=(2,2),in_specs=specs,out_specs=pl.BlockSpec(five,lambda i,j,s:(i,j,0,0,0))),
            out_shape=S((2,2,4,rows,ffc),bf16),cost_estimate=cost,name=name)(info,*args)
    got_spec=pl.BlockSpec(five,lambda j,s:(a,j,0,0,0)); one=pl.BlockSpec((1,4,rows,ffc),lambda j,s:(j,0,0,0))
    if stage=="first":
        return pl.pallas_call(functools.partial(first_kernel,blocks),
            grid_spec=pltpu.PrefetchScalarGridSpec(num_scalar_prefetch=1,grid=(2,),in_specs=specs+[got_spec],out_specs=one),
            out_shape=S((2,4,rows,ffc),bf16),cost_estimate=cost,name=name)(info,*args,got)
    full=pl.BlockSpec((4,rows,ffc),lambda j,s:(0,0,0))
    return pl.pallas_call(functools.partial(second_kernel,blocks),
        grid_spec=pltpu.PrefetchScalarGridSpec(num_scalar_prefetch=1,grid=(2,),in_specs=specs+[got_spec,one],out_specs=[full,full]),
        out_shape=[S((4,rows,ffc),bf16)]*2,cost_estimate=cost,name=name)(info,*args,got,came)

def core_swap(value):
    return lax.ppermute(value, "cc", [(0, 1), (1, 0)])


def swap_by(blocks, index):
    pairs = blocks.reshape((2, 2) + blocks.shape[1:])
    pairs = jnp.where((index // 2) == 1, pairs[::-1], pairs)
    pairs = jnp.where((index % 2) == 1, pairs[:, ::-1], pairs)
    return pairs.reshape(blocks.shape)


def dp_halves(value, c):
    if lax.axis_size("dp") != 2:
        whole = lax.all_gather(value, "dp", axis=0, tiled=True)
        halves = whole.reshape((2, whole.shape[0] // 2) + whole.shape[1:])
        return jnp.where(c == 0, halves[0], halves[1]), jnp.where(c == 0, halves[1], halves[0])
    other = swap2(value, "dp")
    same = lax.axis_index("dp") == c
    return jnp.where(same, value, other), jnp.where(same, other, value)


def dp_sum(this_half, other_half, c):
    if lax.axis_size("dp") != 2:
        whole = jnp.concatenate(
            [jnp.where(c == 0, this_half, other_half), jnp.where(c == 0, other_half, this_half)], axis=0
        )
        return lax.psum_scatter(whole.astype(bf16), "dp", scatter_dimension=0, tiled=True).astype(f32)
    same = lax.axis_index("dp") == c
    keep = jnp.where(same, this_half, other_half)
    return keep + swap2(jnp.where(same, other_half, this_half).astype(bf16), "dp").astype(f32)


def pack_outer(part):
    turned = part.T
    half = turned.shape[0] // 2
    return jnp.concatenate([turned[:half], turned[half:]], axis=1)


def unpack_outer(packed):
    wide = packed.shape[1] // 2
    return jnp.concatenate([packed[:, :wide], packed[:, wide:]], axis=0).T


def pack_output(part):
    third = part.shape[0] // 3
    padded = jnp.pad(part, ((0, 0), (0, 256 - part.shape[1])))
    return jnp.concatenate([padded[j * third : (j + 1) * third] for j in range(3)], axis=1)


def unpack_output(packed, feat):
    return jnp.concatenate([packed[:, j * 256 : j * 256 + feat] for j in range(3)], axis=0)


def pack_norms(first_gain, first_shift, second_gain, second_shift):
    line = jnp.concatenate([first_gain, first_shift, second_gain, second_shift])
    high = lax.reduce_precision(line, 8, 7)
    middle_part = lax.reduce_precision(line - high, 8, 7)
    rest = line - high - middle_part
    rows = jnp.stack([high, middle_part, rest]).astype(bf16)
    return jnp.pad(rows, ((0, 13), (0, 0)))


def after(value, *earlier):
    return lax.optimization_barrier((value,) + earlier)[0]


def swap2(value, axis):
    return lax.ppermute(value, axis, [(0, 1), (1, 0)])


def crossed(value, axes, first):
    pairs = []
    for u in range(2):
        for v in range(2):
            for core in range(2):
                along = first ^ core
                pairs.append(((u * 2 + v) * 2 + core, ((u ^ (1 - along)) * 2 + (v ^ along)) * 2 + core))
    return lax.ppermute(value, axes + ("cc",), pairs)


PLANE = ("dp", "cy")


def scatter_steps(keep, send, axes, *between):
    first = after(crossed(send, axes, 0), *between)
    second = crossed(jnp.stack([keep[1], first[1]]), axes, 1)
    return keep, first, second


def by_slot(three):
    keep, first, second = three
    return [keep[0], second[0], first[0], second[1]]


def row_pair(block, *between):
    return jnp.stack([block, after(crossed(block, ROW, 1), *between)])


def row_rest(pair, *between):
    return jnp.concatenate([pair, after(crossed(pair, ROW, 0), *between)], axis=0)


def core_copies(arrays, ties):
    return arrays + [core_swap(after(array, *tie)) for array, tie in zip(arrays, ties)]


def gather_generic(w_output, w_inner, w_outer, norms, row, y, c):
    inner, outer, output = (lax.all_gather(w, "dp", axis=0, tiled=True) for w in (w_inner, w_outer, w_output))
    chunks = []
    for which in range(2):
        halves = []
        for g in range(2):
            parts = [w.reshape((2, w.shape[0] // 2) + w.shape[1:])[g] for w in (inner, outer, output)]
            if which == 0:
                halves.append(jnp.concatenate([parts[0], pack_output(parts[2]), norms], axis=0))
            else:
                halves.append(pack_outer(parts[1]))
        whole = lax.all_gather(jnp.stack(halves), GROUP)
        flat = whole.reshape((-1,) + whole.shape[2:])
        arrays = []
        for kc in range(2):
            core = c ^ kc
            for spot in range(4):
                first, second = spot % 2, spot // 2
                kx = jnp.where(core == 0, second, first)
                ky = jnp.where(core == 0, first, second)
                steps = [jnp.where(core == 0, i, (i % 2) * 2 + i // 2) for i in range(4)]
                spots = jnp.stack([((row ^ k) * 4 + (y ^ ky) * 2 + core) * 2 + kx for k in steps])
                arrays.append(jnp.take(flat, spots, axis=0))
        chunks.append(arrays)
    return chunks


def add_parts(parts):
    total = parts[0].astype(f32)
    for part in parts[1:]:
        total = total + part.astype(f32)
    return total


def halve(stack):
    pass_on = crossed(stack[2:], ROW, 0)
    pair = (stack[:2].astype(f32) + pass_on.astype(f32)).astype(bf16)
    return pair[0].astype(f32) + crossed(pair[1], ROW, 1).astype(f32)


def generic_inner(first, keep, send, c):
    parts = [keep, send, first[0], first[1]]
    by_x = [
        (parts[0], jnp.where(c == 0, parts[1], parts[2])),
        (jnp.where(c == 0, parts[2], parts[1]), parts[3]),
    ]
    planes = [add_parts([own, swap2(other, "cy")]).astype(bf16) for own, other in by_x]
    return [halve(plane) for plane in planes]


def generic_outer(row_sum, c):
    by_x = [
        (row_sum[0], jnp.where(c == 0, row_sum[1], row_sum[2])),
        (jnp.where(c == 0, row_sum[2], row_sum[1]), row_sum[3]),
    ]
    return [add_parts([own, swap2(other, "cy")]) for own, other in by_x]


def local(
    tokens, w_query, w_key, w_value, w_output, w_inner, w_outer,
    first_gain, first_shift, second_gain, second_shift, seq_lengths, out_grad,
):
    feat = tokens.shape[1]
    cols = tokens.shape[2]
    half = cols // 2
    head_width = w_query.shape[1]
    heads = head_width // HD
    two = lax.axis_size("dp") == 2
    row = lax.axis_index(ROW)
    group = lax.axis_index("dp")
    m = lax.axis_index("rm")
    z = lax.axis_index("rz")
    y = lax.axis_index("cy")
    c = lax.axis_index("cc")
    length = lax.dynamic_index_in_dim(seq_lengths[m], group, keepdims=False)
    own_start = (y * 2 + c) * cols + z * half
    info = jnp.stack([
        row, z, y, c, length - own_start, group if two else 0 * group, 0 * y, 0 * y,
    ]).astype(jnp.int32)

    def turn(blocks):
        pairs = blocks.reshape((2, 2) + blocks.shape[1:])
        return jnp.where(c == 0, pairs, pairs.swapaxes(0, 1)).reshape(blocks.shape)

    def to_slots(array):
        blocks = array.reshape(2, feat, 2, half).transpose(0, 2, 1, 3).reshape(4, feat, half)
        return turn(swap_by(blocks, row))

    def from_slots(parts):
        back = swap_by(turn(jnp.stack(parts)), row)
        return back.reshape(2, 2, feat, half).transpose(0, 2, 1, 3).reshape(2, feat, cols)

    this_half, other_half = dp_halves(jnp.concatenate([w_query, w_key, w_value], axis=1), c)
    token_blocks = to_slots(tokens)
    token_three = scatter_steps(token_blocks[:2], token_blocks[2:], ROW)
    x_own = jnp.stack(by_slot(token_three))
    other_columns = core_swap(other_half)
    norms = pack_norms(first_gain, first_shift, second_gain, second_shift)
    if two:
        block_a = jnp.concatenate([after(w_inner, token_blocks), pack_output(w_output), norms], axis=0)
        pair_a = row_pair(block_a)
        block_b = pack_outer(w_outer)
        near_b = crossed(after(block_b, token_blocks), ROW, 1)
    pieces = []
    for s in range(4):
        step = jnp.where(c == 0, s % 2, s // 2)
        pieces.append(jnp.where((z ^ step) == c, this_half, other_columns))
    mine = jnp.stack(by_slot(scatter_steps(jnp.stack(pieces[:2]), jnp.stack(pieces[2:]), ROW)))
    theirs = core_swap(mine)
    if two:
        row_a = row_rest(pair_a)
        x_own = after(x_own, pair_a)
    x_second = crossed(x_own, SQUARE, 1)
    xs = (x_own, x_second, crossed(jnp.stack([x_own, x_second]), SQUARE, 0))
    if two:
        xs = (after(x_own, row_a),) + xs[1:]

    starts = []
    for kc in range(2):
        core = c ^ kc
        for s in range(4):
            z_here = z ^ jnp.where(core == 0, s // 2, s % 2)
            y_here = y ^ jnp.where(core == 0, s % 2, s // 2)
            starts.append((y_here * 2 + core) * cols + z_here * half)
    positions = (jnp.stack(starts)[:, None] + jnp.arange(half, dtype=jnp.int32)[None, :]).reshape(-1)
    invalid = jnp.where(positions < length, 0.0, masked_score)
    bias = jnp.where(jnp.arange(HD)[:, None] == 0, invalid[None, :], 0.0).astype(bf16)
    frequency = 10000.0 ** (-2.0 * jnp.arange(HD // 2, dtype=f32) / HD)
    frequency = after(frequency, token_three[1])
    angles = frequency[:, None] * positions[: 4 * half].astype(f32)[None, :]
    cosine = jnp.repeat(jnp.cos(angles), 2, axis=0)
    sines = jnp.sin(angles)
    sine = jnp.stack([-sines, sines], axis=1).reshape(HD, 4 * half)

    q_rot, kv_own = qkv(info, xs, mine, theirs, cosine, sine)
    kv_other = core_swap(kv_own)
    out_b, log_b, low_b = attend(1, q_rot, kv_own, kv_other, bias)
    low_first = crossed(low_b, SQUARE, 0)
    cot_blocks = to_slots(after(out_grad, kv_own))
    cot_first = after(crossed(cot_blocks[2:], ROW, 0), low_b)
    cot_pass = jnp.stack([cot_blocks[1], cot_first[1]])
    cot_second = crossed(cot_pass, ROW, 1)
    cot_three = (cot_blocks[:2], cot_first, cot_second)
    q_second = after(q_rot, low_b, cot_pass)
    if two:
        near_a, far_a = crossed(row_a, PLANE, 1), crossed(row_a, PLANE, 0)
        both_a = crossed(after(near_a, kv_own), PLANE, 0)
        row_a_swapped = core_swap(after(row_a, kv_own))
        far_a = after(far_a, low_b)
        both_a = after(both_a, low_b)
        pair_b = jnp.stack([block_b, after(near_b, kv_own)])
        row_b = row_rest(pair_b, low_b)
        q_second = after(q_second, row_a_swapped, far_a, row_b)
        near_b, far_b = crossed(row_b, PLANE, 1), crossed(row_b, PLANE, 0)
    out_a, log_a, low_a = attend(0, q_second, kv_own, kv_other, bias)
    low_pass = jnp.stack([low_a[1], after(low_first, low_a)[1]])
    low_second = crossed(low_pass, SQUARE, 1)
    attn_three = (low_a, low_first, low_second)
    if two:
        both_b = crossed(after(near_b, low_second, cot_second), PLANE, 0)
        chunk_a = [row_a, near_a, far_a, both_a, row_a_swapped] + [core_swap(after(part, low_a)) for part in (near_a, far_a, both_a)]
        chunk_b = core_copies([row_b, near_b, far_b, both_b], [(low_a,), (low_pass,), (low_pass,), (low_pass,)])
    else:
        chunk_a, chunk_b = gather_generic(w_output, w_inner, w_outer, norms, row, y, c)
    mixed_keep, mixed_send, e_keep, e_send, grad_one, attn_t, hidden_t, outer_t, branch_low, act_low, inner_low, norm_sums = middle(
        info, attn_three, x_own, cot_three, chunk_a, chunk_b
    )
    inner_args = (hidden_t, inner_low, attn_t, branch_low, norm_sums)
    outer_args = (outer_t, act_low)

    def tied(args, *earlier):
        return (after(args[0], *earlier),) + args[1:]

    def head_back(first, count, *earlier):
        return attend_back(
            first, count, after(q_rot, *earlier), kv_own, kv_other, bias, (out_a, out_b), (log_a, log_b), grads, cosine, sine
        )

    give_outer = grad_call("outer", "give", info, outer_args)
    got_outer = core_swap(give_outer)
    grads_first = after(crossed(e_send, SQUARE, 0), give_outer)
    grads_pass = jnp.stack([e_keep[1], grads_first[1]])
    grads = (e_keep, grads_first, crossed(grads_pass, SQUARE, 1))
    give_inner = grad_call("inner", "give", info, tied(inner_args, give_outer, grads_pass))
    got_inner = core_swap(give_inner)
    mixed_first = after(crossed(mixed_send, ROW, 0), give_inner)
    mixed_pass = jnp.stack([mixed_keep[1], mixed_first[1]])
    first_outer = grad_call("outer", "first", info, tied(outer_args, mixed_pass, grads[2]), got_outer)
    came_outer = crossed(first_outer, ROW, 0)
    first_inner = grad_call("inner", "first", info, tied(inner_args, first_outer), got_inner)
    came_inner = crossed(first_inner, PLANE, 0) if two else jnp.zeros_like(first_inner)
    mixed_second = crossed(mixed_pass, ROW, 1)
    dq, own, send = head_back(0, heads, first_inner, mixed_second)
    came_outer = after(came_outer, dq)
    own = after(own, came_outer)
    dkv_got = core_swap(send)
    dx_keep, dx_send, proj = finish_dx(info, dq, own, dkv_got, mine, theirs, cosine, sine)
    dx_first = crossed(dx_send, SQUARE, 0)
    keep_outer, pass_outer = grad_call(
        "outer", "second", info, tied(outer_args, dx_keep), got_outer, after(came_outer, dx_keep)
    )
    keep_inner, pass_inner = grad_call(
        "inner", "second", info, tied(inner_args, keep_outer), got_inner, after(came_inner, keep_outer)
    )
    dx_first = after(dx_first, keep_inner)
    dx_pass = (dx_keep[1] + dx_first[1].astype(f32)).astype(bf16)
    dx_second = crossed(dx_pass, SQUARE, 1)
    keep, give = finish_dw(info, after(proj, dx_pass), xs)
    got = core_swap(give)
    dx_second = after(dx_second, give)
    d_x = add_parts([grad_one, dx_keep[0], dx_first[0], dx_second]).astype(bf16)
    d_x_first = crossed(d_x[2:], ROW, 0)
    by_row_step = keep + after(got, d_x).astype(f32)
    passed_m = swap2(by_row_step[2:].astype(bf16), "rm")
    if two:
        plane_inner = add_parts([keep_inner, after(crossed(pass_inner, PLANE, 1), by_row_step)]).astype(bf16)
        pass_on_inner = crossed(plane_inner[2:], ROW, 0)
    row_outer = add_parts([keep_outer, after(crossed(pass_outer, ROW, 1), by_row_step)]).astype(bf16)
    if two:
        pass_on_outer = crossed(row_outer[2:], PLANE, 0)
        d_x_first = after(d_x_first, plane_inner, row_outer)
    d_x_pass = jnp.stack([d_x[1], d_x_first[1]])
    d_x_second = crossed(d_x_pass, ROW, 1)
    near_far = by_row_step[:2] + after(passed_m, d_x_pass).astype(f32)
    near_sum = near_far[0]
    far_low = swap2(near_far[1].astype(bf16), "rz")
    if two:
        pair_inner = (plane_inner[:2].astype(f32) + after(pass_on_inner, near_far).astype(f32)).astype(bf16)
        last_inner = crossed(pair_inner[1], ROW, 1)
        pair_outer = (row_outer[:2].astype(f32) + after(pass_on_outer, near_far).astype(f32)).astype(bf16)
        last_outer = crossed(pair_outer[1], PLANE, 1)
        far_low = after(far_low, pair_inner, pair_outer)
    far_sum = far_low.astype(f32)
    kept = jnp.where(z == c, near_sum, far_sum)
    passed = core_swap(jnp.where(z == c, far_sum, near_sum).astype(bf16)).astype(f32)
    d_x_second = after(d_x_second, kept)
    d_input = from_slots(by_slot((d_x[:2], d_x_first, d_x_second))).astype(f32)
    g_qkv = dp_sum(kept, passed, c)
    if two:
        inner_sums = [pair_inner[0].astype(f32) + after(last_inner, passed).astype(f32)]
        outer_sums = [pair_outer[0].astype(f32) + after(last_outer, passed).astype(f32)]
    else:
        outer_sums = generic_outer(row_outer, c)
        inner_sums = generic_inner(first_inner, keep_inner, pass_inner, c)
    mixed_out = from_slots(by_slot((mixed_keep, mixed_first, mixed_second)))

    half_rows = feat // 2
    third = half_rows // 3
    g_outer = jnp.concatenate([unpack_outer(part) for part in outer_sums], axis=0)
    g_inner = jnp.concatenate([part[:half_rows] for part in inner_sums], axis=0)
    g_output = jnp.concatenate(
        [unpack_output(part[half_rows : half_rows + third], feat) for part in inner_sums], axis=0
    )
    g_norms = inner_sums[0][half_rows + third].reshape(4, feat)
    if not two:
        g_outer, g_inner, g_output = (
            lax.psum_scatter(g.astype(bf16), "dp", scatter_dimension=0, tiled=True).astype(f32)
            for g in (g_outer, g_inner, g_output)
        )
        g_norms = lax.psum(g_norms, "dp")

    return (
        mixed_out, d_input,
        g_qkv[:, :head_width], g_qkv[:, head_width : 2 * head_width], g_qkv[:, 2 * head_width :],
        g_output, g_inner, g_outer,
        g_norms[0], g_norms[1], g_norms[2], g_norms[3],
    )


def solution(mesh):
    shape = mesh.devices.shape
    fine = Mesh(mesh.devices.reshape(shape[0], 2, shape[1] // 2, 2, shape[2] // 2), EVERY)
    col = ("cy", "cc")
    acts = P(None, ROW, ("dp",) + col)
    by_row = P(ROW + ("dp",), col)
    by_col = P(col + ("dp",), ROW)
    vec = P(ROW)
    return jax.shard_map(
        local,
        mesh=fine,
        in_specs=(
            acts, by_row, by_row, by_row, by_col, by_row, by_col, vec, vec, vec, vec, P(), acts,
        ),
        out_specs=(
            acts, acts, by_row, by_row, by_row, by_col, by_row, by_col, vec, vec, vec, vec,
        ),
        check_vma=False,
    )
```

```python
import functools

import jax
import jax.numpy as jnp
from jax import lax
from jax.experimental import pallas as pl
from jax.experimental.pallas import tpu as pltpu
from jax.sharding import Mesh, PartitionSpec as P

HD = 64
EVERY = ("dp", "rm", "rz", "cy", "cc")
GROUP = ("rm", "rz", "cy", "cc")
ROW = ("rm", "rz")
SQUARE = ("rz", "cy")
bf16=jnp.bfloat16; f32=jnp.float32
LOG2E=1.4426950408889634
LN2=0.6931471805599453
masked_score=-1e30

def mm(a,b,dims=((1,),(0,))):
    return lax.dot_general(a,b,(dims,((),())),preferred_element_type=f32)
NT=((1,),(1,))

def pair_turn(values, cosine, signed_sine):
    shape = values.shape
    v3 = values.reshape(shape[0]//8, 8, shape[1])
    up = pltpu.roll(v3, 7, 1); down = pltpu.roll(v3, 1, 1)
    even = (lax.broadcasted_iota(jnp.int32, v3.shape, 1) % 2) == 0
    other = jnp.where(even, up, down).reshape(shape)
    return values*cosine + other*signed_sine

KB=1024
QB=2
def one_row(shape, dtype, value=1.0):
    return jnp.where(lax.broadcasted_iota(jnp.int32, shape, 0)==0, value, 0.0).astype(dtype)

def attend_kernel(q_ref, ko_ref, vo_ref, kx_ref, vx_ref, bias_ref, o_ref, lse_ref, low_ref, kaug, vall):
    span=ko_ref.shape[1]
    for part,(kr,vr) in enumerate(((ko_ref,vo_ref),(kx_ref,vx_ref))):
        aug=jnp.concatenate([kr[...], bias_ref[:, part*span:(part+1)*span]],axis=0)
        kaug[part*span:(part+1)*span,:]=aug.T
        vall[:, part*span:(part+1)*span]=vr[...]
    n=q_ref.shape[1]
    qaug=jnp.concatenate([q_ref[...], one_row((HD,n),bf16)],axis=0)
    top=jnp.full((1,n),-3e38,f32); total=jnp.zeros((1,n),f32); acc=jnp.zeros((HD,n),f32)
    s=mm(kaug[0:KB,:],qaug)
    for kb in range(0,2*span,KB):
        following=mm(kaug[kb+KB:kb+2*KB,:],qaug) if kb+KB<2*span else None
        new=jnp.maximum(top,jnp.max(s,axis=0,keepdims=True))
        alpha=jnp.exp2(top-new)
        p=jnp.exp2(s-new)
        total=total*alpha+jnp.sum(p,axis=0,keepdims=True)
        acc=acc*alpha+mm(vall[:,kb:kb+KB],p.astype(bf16))
        top=new
        s=following
    out=acc/total
    o_ref[...]=out
    lse_ref[0]=top+jnp.log2(total)
    low=out.astype(bf16)
    for b in range(2):
        low_ref[b]=low[:,b*(n//2):(b+1)*(n//2)]

def attend(part,q,kv,kvx,bias):
    width,n4=q.shape; heads=width//HD; n=n4//2; span=kv.shape[1]
    kspec=pl.BlockSpec((HD,span),lambda h:(h,0)); vspec=pl.BlockSpec((HD,span),lambda h:(heads+h,0))
    return pl.pallas_call(attend_kernel,grid=(heads,),
        in_specs=[pl.BlockSpec((HD,n),lambda h:(h,part)),kspec,vspec,kspec,vspec,pl.BlockSpec((HD,2*span),lambda h:(0,0))],
        out_specs=[pl.BlockSpec((HD,n),lambda h:(h,0)),pl.BlockSpec((1,1,n),lambda h:(h,0,0)),pl.BlockSpec((2,HD,n//2),lambda h:(0,h,0))],
        out_shape=[jax.ShapeDtypeStruct((width,n),f32),jax.ShapeDtypeStruct((heads,1,n),f32),jax.ShapeDtypeStruct((2,width,n//2),bf16)],
        scratch_shapes=[pltpu.VMEM((2*span,2*HD),bf16),pltpu.VMEM((HD,2*span),bf16)],
        cost_estimate=pl.CostEstimate(flops=int(6.0*(2*width*n4//HD*2*span*256))+1,bytes_accessed=int(6.0*(2*n4*2*span))+1,transcendentals=int(6.0*(heads*n*2*span))+1),
        name="attend")(q,kv,kv,kvx,kvx,bias)

BKB=512
def attend_back_kernel(q_ref, ko_ref, vo_ref, kx_ref, vx_ref, bias_ref, oa_ref, ob_ref, lsea_ref, lseb_ref, g0,g1,g2,g3, cos_ref, sin_ref,
                       dq_ref, own_ref, give_ref, kaug, vtm, kall, acc):
    qb=pl.program_id(1)
    span=ko_ref.shape[1]; n=q_ref.shape[1]
    @pl.when(qb==0)
    def _():
        for part,(kr,vr) in enumerate(((ko_ref,vo_ref),(kx_ref,vx_ref))):
            sl=slice(part*span,(part+1)*span)
            kaug[sl,:]=jnp.concatenate([kr[...], bias_ref[:, sl]],axis=0).T
            vtm[sl,:]=jnp.concatenate([vr[...], jnp.zeros((HD,span),bf16)],axis=0).T
            kall[:,sl]=kr[...]
        acc[...]=jnp.zeros_like(acc)
    q=q_ref[...]
    zeros=jnp.zeros((HD,n),bf16)
    qaug=jnp.concatenate([q, one_row((HD,n),bf16)],axis=0)
    g=jnp.concatenate([jnp.where(qb==0,g0[...],g2[...]),jnp.where(qb==0,g1[...],g3[...])],axis=1)
    o=jnp.where(qb==0,oa_ref[...],ob_ref[...])
    qpad=jnp.concatenate([q,zeros],axis=0).T
    gpad=jnp.concatenate([zeros,g],axis=0).T
    gaug=jnp.concatenate([g,zeros],axis=0)
    delta=jnp.sum(g.astype(f32)*o,axis=0,keepdims=True)
    lse=jnp.where(qb==0,lsea_ref[0],lseb_ref[0])
    dq=jnp.zeros((HD,n),f32)
    s=mm(kaug[0:BKB,:],qaug); dp=mm(vtm[0:BKB,:],gaug)
    for kb in range(0,2*span,BKB):
        last=kb+BKB>=2*span
        s_next=None if last else mm(kaug[kb+BKB:kb+2*BKB,:],qaug)
        dp_next=None if last else mm(vtm[kb+BKB:kb+2*BKB,:],gaug)
        p=jnp.exp2(s-lse)
        ds=(p*(dp-delta)).astype(bf16)
        dq=dq+mm(kall[:,kb:kb+BKB],ds)
        acc[kb:kb+BKB,:]=acc[kb:kb+BKB,:]+mm(ds,qpad)+mm(p.astype(bf16),gpad)
        s=s_next; dp=dp_next
    dq_ref[...]=pair_turn(dq*(HD**-0.5),cos_ref[...],-sin_ref[...]).astype(bf16)
    @pl.when(qb==4//QB-1)
    def _():
        own_ref[...]=acc[:span,:]
        give_ref[...]=acc[span:,:].astype(bf16)

def attend_back(first,count,q,kv,kvx,bias,os,lses,grads,cos,sin):
    width,n4=q.shape; heads=width//HD; n=n4//4*QB; span=kv.shape[1]
    kspec=pl.BlockSpec((HD,span),lambda h,b:(first+h,0)); vspec=pl.BlockSpec((HD,span),lambda h,b:(heads+first+h,0))
    gspec=lambda i:pl.BlockSpec((None,HD,n4//4),lambda h,b:(i,first+h,0)); tb=pl.BlockSpec((HD,n),lambda h,b:(0,b))
    dspec=pl.BlockSpec((None,span,2*HD),lambda h,b:(h,0,0)); ospec=pl.BlockSpec((HD,n),lambda h,b:(first+h,0)); lspec=pl.BlockSpec((1,1,n),lambda h,b:(first+h,0,0))
    return pl.pallas_call(attend_back_kernel,grid=(count,4//QB),
        in_specs=[pl.BlockSpec((HD,n),lambda h,b:(first+h,b)),kspec,vspec,kspec,vspec,pl.BlockSpec((HD,2*span),lambda h,b:(0,0)),ospec,ospec,lspec,lspec,gspec(0),gspec(0),gspec(0),gspec(1),tb,tb],
        out_specs=[pl.BlockSpec((HD,n),lambda h,b:(h,b)),dspec,dspec],
        out_shape=[jax.ShapeDtypeStruct((count*HD,n4),bf16),jax.ShapeDtypeStruct((count,span,2*HD),f32),jax.ShapeDtypeStruct((count,span,2*HD),bf16)],
        scratch_shapes=[pltpu.VMEM((2*span,2*HD),bf16),pltpu.VMEM((2*span,2*HD),bf16),pltpu.VMEM((HD,2*span),bf16),pltpu.VMEM((2*span,2*HD),f32)],
        cost_estimate=pl.CostEstimate(flops=int(6.0*(count*10*n4*2*span*256))+1,bytes_accessed=int(6.0*(count*4*n4*2*span))+1,transcendentals=int(6.0*(count*n4*2*span))+1),
        name="attend_back")(q,kv,kv,kvx,kvx,bias,*os,*lses,grads[0],grads[2],grads[1],grads[2],cos,sin)
def xor(a,b):
    return lax.bitwise_xor(jnp.asarray(a,jnp.int32),jnp.asarray(b,jnp.int32))

def rows_at(index,size,align):
    return pl.ds(pl.multiple_of(index*size,align),size)

def row_step(core,slot):
    return jnp.where(core==0,slot,(slot%2)*2+slot//2)

def z_step(core,slot):
    return jnp.where(core==0,slot//2,slot%2)

def y_step(core,slot):
    return jnp.where(core==0,slot%2,slot//2)

def slots(three):
    keep,first,second=three
    return (keep.at[0],second.at[0],first.at[0],second.at[1])

def place_qkv_weights(info, mine_ref, theirs_ref, w_s):
    row=info[0]; c=info[3]
    half=mine_ref.shape[1]
    for r in range(4):
        k=xor(r,row)
        w_s[pl.ds(pl.multiple_of((2*r+c)*half,32),half),:]=mine_ref[row_step(c,k)]
        w_s[pl.ds(pl.multiple_of((2*r+1-c)*half,32),half),:]=theirs_ref[row_step(1-c,k)]

def place_tokens(info, x_ref, slot, x_s):
    feat=x_ref.shape[1]; c=info[3]; base=xor(info[0],z_step(c,slot))
    for r in range(4):
        x_s[r*feat:(r+1)*feat,:]=x_ref[row_step(c,xor(r,base))]

def token_refs(own, second, others):
    return (own, second, others.at[0], others.at[1])

def qkv_kernel(info, xa,xb,xc, mine_ref, theirs_ref, cos_ref, sin_ref, q_ref, kv_ref, w_s, wt_s, x_s):
    place_qkv_weights(info,mine_ref,theirs_ref,w_s)
    wt_s[...]=w_s[...].T
    hw=q_ref.shape[0]; n=xa.shape[2]
    for k,xr in enumerate(token_refs(xa,xb,xc)):
        place_tokens(info,xr,k,x_s)
        out=mm(wt_s[...],x_s[...])
        sl=slice(k*n,(k+1)*n)
        cos=cos_ref[:,sl]; sin=sin_ref[:,sl]
        for h in range(2*hw//HD):
            turned=pair_turn(out[h*HD:(h+1)*HD],cos,sin)
            if h*HD<hw: q_ref[h*HD:(h+1)*HD,sl]=(turned*(HD**-0.5*LOG2E)).astype(bf16)
            else: kv_ref[h*HD-hw:(h+1)*HD-hw,sl]=turned.astype(bf16)
        kv_ref[hw:,sl]=out[2*hw:].astype(bf16)

VM=pl.BlockSpec(memory_space=pltpu.VMEM)
SM=pl.BlockSpec(memory_space=pltpu.SMEM)
HB=pl.BlockSpec(memory_space=pl.ANY)

def qkv(info,xs,mine,theirs,cos,sin):
    _,feat,n=xs[0].shape; w3=mine.shape[2]; hw=w3//3; width=4*feat
    return pl.pallas_call(qkv_kernel,in_specs=[SM]+[VM]*7,out_specs=[VM,VM],
        out_shape=[jax.ShapeDtypeStruct((hw,4*n),bf16),jax.ShapeDtypeStruct((2*hw,4*n),bf16)],
        scratch_shapes=[pltpu.VMEM((width,w3),bf16),pltpu.VMEM((w3,width),bf16),pltpu.VMEM((width,n),bf16)],
        name="qkv")(info,*xs,mine,theirs,cos,sin)

def finish_dx_kernel(info, *refs):
    (q_ref,own_ref,got_ref,mine_ref,theirs_ref,cos_ref,sin_ref,keep_ref,send_ref,p_ref,w_s)=refs
    hw=q_ref.shape[0]; n=keep_ref.shape[3]; feat=keep_ref.shape[2]; c=info[3]
    place_qkv_weights(info,mine_ref,theirs_ref,w_s)
    p_ref[0:hw,:]=q_ref[...]
    for h in range(hw//HD):
        t=(own_ref[h]+got_ref[h].astype(f32)).T
        p_ref[hw+h*HD:hw+(h+1)*HD,:]=pair_turn(t[:HD]*LN2,cos_ref[...],-sin_ref[...]).astype(bf16)
        p_ref[2*hw+h*HD:2*hw+(h+1)*HD,:]=t[HD:].astype(bf16)
    for k,dr in ((3,send_ref),(2,send_ref),(1,keep_ref),(0,keep_ref)):
        sl=slice(k*n,(k+1)*n)
        base=xor(info[0],z_step(c,k))
        for r in range(4):
            dr[k%2,row_step(c,xor(r,base))]=mm(w_s[r*feat:(r+1)*feat,:],p_ref[:,sl]).astype(dr.dtype)

def finish_dx(info,dq,own,got,mine,theirs,cos,sin):
    w3=mine.shape[2]; half=mine.shape[1]; feat=2*half; width=4*feat; n=dq.shape[1]//4
    S=jax.ShapeDtypeStruct
    return pl.pallas_call(finish_dx_kernel,in_specs=[SM]+[VM]*7,out_specs=[VM]*3,
        out_shape=[S((2,4,feat,n),f32),S((2,4,feat,n),bf16),S((w3,4*n),bf16)],
        scratch_shapes=[pltpu.VMEM((width,w3),bf16)],
        cost_estimate=pl.CostEstimate(flops=int(0.0*(8*width*w3*n))+1,bytes_accessed=int(0.0*(8*width*n*4))+1,transcendentals=int(0.0*(0))+1),
        name="finish_dx")(info,dq,own,got,mine,theirs,cos,sin)

def finish_dw_kernel(info, p_ref, xa,xb,xc, keep_ref, give_ref, x_s, g_s):
    n=xa.shape[2]; half=keep_ref.shape[1]
    for k,xr in enumerate(token_refs(xa,xb,xc)):
        place_tokens(info,xr,k,x_s.at[:,k*n:(k+1)*n])
    g_s[...]=mm(x_s[...],p_ref[...],NT)
    c=info[3]; row=info[0]
    for r in range(4):
        mine_rows=pl.ds(pl.multiple_of((2*r+c)*half,32),half); their_rows=pl.ds(pl.multiple_of((2*r+1-c)*half,32),half)
        keep_ref[xor(r,row)]=g_s[mine_rows,:]
        give_ref[xor(r,row)]=g_s[their_rows,:].astype(bf16)

def finish_dw(info,proj,xs):
    _,feat,n=xs[0].shape; w3=proj.shape[0]; width=4*feat; half=feat//2
    return pl.pallas_call(finish_dw_kernel,in_specs=[SM]+[VM]*4,out_specs=[VM]*2,
        out_shape=[jax.ShapeDtypeStruct((4,half,w3),f32),jax.ShapeDtypeStruct((4,half,w3),bf16)],
        scratch_shapes=[pltpu.VMEM((width,4*n),bf16),pltpu.VMEM((width,w3),f32)],
        cost_estimate=pl.CostEstimate(flops=int(6.0*(8*width*w3*n))+1,bytes_accessed=int(6.0*(8*width*n*2))+1,transcendentals=int(6.0*(0))+1),
        name="finish_dw")(info,proj,*xs)

def middle_kernel(info, a0,a1,a2, x_ref, c0,c1,c2, *refs):
    chunk_a=refs[:8]; chunk_b=refs[8:16]
    (mixk_ref, mixs_ref, ek_ref, es_ref, g1_ref, attnT_ref, hidT_ref, outT_ref, bl_ref, act_ref, il_ref, norm_ref,
                  win, woT, wo, wpk, gp_s, t_s, f_s, sems)=refs[16:]
    row=info[0]; z=info[1]; y=info[2]; c=info[3]; group=info[5]
    feat=a0.shape[1]; n=a0.shape[2]; width=4*feat; ffc=chunk_a[0].shape[2]; half=feat//2; fh=ffc//2; third=half//3
    def go(src,dst,s): pltpu.make_async_copy(src,dst,sems.at[s]).start()
    def each(chunk):
        for kc in range(2):
            core=xor(c,kc)
            for spot,ref in enumerate(chunk[4*kc:4*kc+4]):
                first,second=spot%2,spot//2
                kx=jnp.where(core==0,second,first); ky=jnp.where(core==0,first,second)
                g=xor(group,kx); col=xor(y,ky)*2+core
                for i in range(4):
                    step=row_step(core,i)
                    yield ref.at[i],xor(row,step),g,col,kc+spot
    for ref,r,g,col,_ in each(chunk_a):
        go(ref.at[half:half+third,:],wpk.at[r,col*2+g],0)
    for ref,r,g,col,_ in each(chunk_a):
        go(ref.at[0:half,:],win.at[pl.ds(pl.multiple_of(r*feat+g*half,16),half),pl.ds(pl.multiple_of(col*ffc,128),ffc)],1)
    for ref,r,g,col,_ in each(chunk_b):
        go(ref,woT.at[pl.ds(pl.multiple_of(r*feat,64),feat),pl.ds(pl.multiple_of((col*2+g)*fh,128),fh)],2)
    def group_of(s):
        return xor(y,y_step(c,s))*2+xor(z,z_step(c,s))
    def row_of(s):
        return xor(row,row_step(c,s))
    for s,ar in enumerate(slots((a0,a1,a2))):
        attnT_ref[rows_at(group_of(s),feat,64),:]=ar[...]
    for s in range(4):
        t_s[rows_at(row_of(s),feat,64),:]=x_ref[s]
    attn=attnT_ref[...].T
    x=t_s[...].T.astype(f32)
    pltpu.make_async_copy(wpk,wpk,sems.at[0]).wait()
    for r in range(4):
        for q in range(8):
            for j in range(3):
                wo[r,q*half+j*third:q*half+(j+1)*third,:]=wpk[r,q,:,j*256:(j+1)*256]
    wide=256-feat; pieces=feat//wide
    addends=[sum(wpk[r,0,0:16,j*256+feat:(j+1)*256].astype(f32) for j in range(3)) for r in range(4)]
    def vector(which):
        return jnp.concatenate([addends[r][which*pieces+t:which*pieces+t+1] for r in range(4) for t in range(pieces)],axis=1)
    gain1=vector(0); shift1=vector(1); gain2=vector(2); shift2=vector(3)
    branch=jnp.concatenate([mm(attn,wo[r])[:,:feat] for r in range(4)],axis=1)
    def stats(v):
        mean=jnp.sum(v,axis=1,keepdims=True)*(1.0/width)
        var=jnp.sum(v*v,axis=1,keepdims=True)*(1.0/width)-mean*mean
        inv=lax.rsqrt(var+1e-5)
        return (v-mean)*inv,inv
    cent1,inv1=stats(x+branch)
    hidden=cent1*gain1+shift1
    hid=hidden.astype(bf16)
    hidT_ref[...]=hid.T
    pltpu.make_async_copy(win,win,sems.at[1]).wait()
    pltpu.make_async_copy(woT,woT,sems.at[2]).wait()
    f_s[...]=jnp.zeros_like(f_s)
    nb=2; bw=ffc//nb
    def forward(j,carry):
        sl=pl.ds(pl.multiple_of(j*bw,128),bw)
        inner=mm(hid,win[:,sl])
        cdf=0.5+0.5*lax.erf(inner*0.7071067811865476)
        act=(inner*cdf).astype(bf16)
        gp_s[:,sl]=cdf+inner*(jnp.exp(inner*inner*-0.5)*0.3989422804014327)
        act_ref[:,sl]=act
        f_s[...]+=mm(act,woT[:,sl],NT)
        return carry
    lax.fori_loop(0,4*nb,forward,0)
    cent2,inv2=stats(hidden+f_s[...])
    t_s[...]=(cent2*gain2+shift2).astype(bf16).T
    for s in range(4):
        (mixk_ref,mixs_ref)[s//2][s%2]=t_s[rows_at(row_of(s),feat,64),:]
    for s,cr in enumerate(slots((c0,c1,c2))):
        t_s[rows_at(row_of(s),feat,64),:]=cr[...]
    valid=(lax.broadcasted_iota(jnp.int32,(n,1),0)<info[4]).astype(f32)
    cot=t_s[...].T.astype(f32)*valid
    sums2=(jnp.sum(cot*cent2,axis=0,keepdims=True),jnp.sum(cot,axis=0,keepdims=True))
    def back(e,cent,inv):
        first=jnp.sum(e,axis=1,keepdims=True)*(1.0/width)
        second=jnp.sum(e*cent,axis=1,keepdims=True)*(1.0/width)
        return inv*(e-first-cent*second)
    grad2=back(cot*gain2,cent2,inv2)
    low=grad2.astype(bf16)
    outT_ref[...]=low.T
    f_s[...]=grad2
    def backward(j,carry):
        sl=pl.ds(pl.multiple_of(j*bw,128),bw)
        il=(mm(low,woT[:,sl])*gp_s[:,sl]).astype(bf16)
        il_ref[:,sl]=il
        f_s[...]+=mm(il,win[:,sl],NT)
        return carry
    lax.fori_loop(0,4*nb,backward,0)
    gh=f_s[...]
    sums=jnp.concatenate((jnp.sum(gh*cent1,axis=0,keepdims=True),jnp.sum(gh,axis=0,keepdims=True))+sums2+(jnp.zeros((4,width),f32),),axis=0)
    for r in range(4):
        lines=[sums[i:i+1,r*feat+t*wide:r*feat+(t+1)*wide] for i in range(4) for t in range(pieces)]
        lines=jnp.concatenate(lines+[jnp.zeros((third-4*pieces,wide),f32)],axis=0)
        norm_ref[r]=jnp.concatenate([jnp.zeros((third,feat),f32),lines],axis=1)
    grad1=back(gh*gain1,cent1,inv1)
    bl=grad1.astype(bf16)
    da=jnp.zeros((width,n),f32)
    for r in range(4):
        piece=jnp.concatenate([bl[:,r*feat:(r+1)*feat],jnp.zeros((n,wide),bf16)],axis=1)
        bl_ref[r]=piece
        da=da+mm(wo[r],piece,NT)
    t_s[...]=da.astype(bf16)
    for s in range(4):
        (ek_ref,es_ref)[s//2][s%2]=t_s[rows_at(group_of(s),feat,64),:]
    f2=grad1.T
    for r in range(4):
        g1_ref[row_step(c,xor(r,row))]=f2[r*feat:(r+1)*feat]

def middle(info,attn_parts,x_own,cot_parts,chunk_a,chunk_b):
    _,feat,n=attn_parts[0].shape; width=4*feat; ff=4*chunk_a[0].shape[2]
    S=jax.ShapeDtypeStruct
    return pl.pallas_call(middle_kernel,in_specs=[SM]+[VM]*7+[HB]*16,out_specs=[VM]*12,
        out_shape=[S((2,feat,n),bf16)]*4+[S((4,feat,n),f32),S((width,n),bf16),S((width,n),bf16),S((width,n),bf16),
                   S((4,n,256),bf16),S((n,ff),bf16),S((n,ff),bf16),S((4,feat//6,256),f32)],
        scratch_shapes=[pltpu.VMEM((width,ff),bf16),pltpu.VMEM((width,ff),bf16),pltpu.VMEM((4,width,256),bf16),pltpu.VMEM((4,8,feat//6,width),bf16),
                        pltpu.VMEM((n,ff),f32),pltpu.VMEM((width,n),bf16),pltpu.VMEM((n,width),f32),pltpu.SemaphoreType.DMA((4,))],
        compiler_params=pltpu.CompilerParams(vmem_limit_bytes=56*1024*1024),
        cost_estimate=pl.CostEstimate(flops=int(6.0*(12*n*width*ff*2))+1,bytes_accessed=int(6.0*(24*width*ff))+1,transcendentals=int(6.0*(2*n*ff))+1),
        name="middle")(info,*attn_parts,x_own,*cot_parts,*chunk_a,*chunk_b)

def plane_target(info,core,slot):
    kx=jnp.where(core==0,slot//2,slot%2); ky=jnp.where(core==0,slot%2,slot//2)
    return xor(info[5],kx),xor(info[2],ky)*2+core

def target(info,which,a,b):
    core=xor(info[3],which)
    return (core,)+plane_target(info,core,2*a+b)

def outer_blocks(info,which,a,b,refs,put):
    outT_ref,act_near,act_far=refs
    core=xor(info[3],which)
    half=outT_ref.shape[0]//8; fh=act_near.shape[1]//2
    rows=outT_ref[rows_at(xor(info[0],row_step(core,2*a+b)),2*half,64),:]
    for ky,act_ref in enumerate((act_near,act_far)):
        value=mm(rows,act_ref[...])
        for g in range(2):
            kx=xor(g,info[5])
            slot=jnp.where(core==0,2*kx+ky,2*ky+kx)
            put(slot,slice(0,2*half),slice(0,fh),value[:,g*fh:(g+1)*fh])

def inner_blocks(info,which,a,b,refs,put):
    hidT_ref,il_ref,attnT_ref,bl_ref,norm_ref=refs
    core,g,col=target(info,which,a,b)
    half=hidT_ref.shape[0]//8; third=half//3
    rows=[xor(info[0],row_step(core,s)) for s in range(4)]
    lhs=jnp.concatenate([hidT_ref[rows_at(r*2+g,half,32),:] for r in rows],axis=0)
    value=mm(lhs,il_ref[...])
    heads=attnT_ref[rows_at(col*2+g,half,32),:]
    for s,r in enumerate(rows):
        put(s,slice(0,half),slice(None),value[s*half:(s+1)*half])
        outs=mm(heads,bl_ref[r])
        for j in range(3):
            piece=outs[j*third:(j+1)*third]
            if j==0: piece=piece+norm_ref[r]
            put(s,slice(half,half+third),slice(j*256,(j+1)*256),piece)

def give_kernel(blocks,info,*refs):
    out=refs[-1]
    def put(s,rows,lanes,value): out[0,0,s,rows,lanes]=value.astype(bf16)
    blocks(info,1,pl.program_id(0),pl.program_id(1),refs[:-1],put)

def first_kernel(blocks,info,*refs):
    got,out=refs[-2:]
    def put(s,rows,lanes,value): out[0,s,rows,lanes]=(value+got[0,0,s,rows,lanes].astype(f32)).astype(bf16)
    blocks(info,0,1,pl.program_id(0),refs[:-2],put)

def second_kernel(blocks,info,*refs):
    got,came,keep,send=refs[-4:]
    for b,out in ((0,keep),(1,send)):
        def put(s,rows,lanes,value):
            out[s,rows,lanes]=(value+got[0,0,s,rows,lanes].astype(f32)+came[0,s,rows,lanes].astype(f32)).astype(bf16)
        @pl.when(pl.program_id(0)==b)
        def _(): blocks(info,0,0,b,refs[:-4],put)

def grad_call(kind,stage,info,args,got=None,came=None):
    S=jax.ShapeDtypeStruct
    width,n=args[0].shape; ffc=args[1].shape[1]//4; half=width//8
    a={"give":None,"first":1,"second":0}[stage]; which=1 if stage=="give" else 0
    def at(index):
        if stage=="give": return lambda i,j,s:index(i,j,s)
        return lambda j,s:index(a,j,s)
    whole=pl.BlockSpec((width,n),at(lambda i,j,s:(0,0)))
    if kind=="inner":
        blocks,rows,lanes=inner_blocks,half+half//3,ffc
        specs=[whole,pl.BlockSpec((n,ffc),at(lambda i,j,s:(0,target(s,which,i,j)[2]))),whole,
               pl.BlockSpec((4,n,256),at(lambda i,j,s:(0,0,0))),pl.BlockSpec((4,half//3,256),at(lambda i,j,s:(0,0,0)))]
    else:
        blocks,rows,lanes=outer_blocks,2*half,ffc//2
        args=(args[0],args[1],args[1])
        def column(ky): return at(lambda i,j,s:(0,xor(s[2],ky)*2+xor(s[3],which)))
        specs=[whole,pl.BlockSpec((n,ffc),column(0)),pl.BlockSpec((n,ffc),column(1))]
    weight={"give":4,"first":2,"second":0}[stage]
    cost=pl.CostEstimate(flops=int(6.0*(weight*width*n*ffc))+1,bytes_accessed=int(6.0*(4*weight*rows*ffc))+1,transcendentals=int(6.0*(0))+1)
    name=kind+"_"+stage
    five=(1,1,4,rows,lanes)
    if stage=="give":
        return pl.pallas_call(functools.partial(give_kernel,blocks),
            grid_spec=pltpu.PrefetchScalarGridSpec(num_scalar_prefetch=1,grid=(2,2),in_specs=specs,out_specs=pl.BlockSpec(five,lambda i,j,s:(i,j,0,0,0))),
            out_shape=S((2,2,4,rows,lanes),bf16),cost_estimate=cost,name=name)(info,*args)
    got_spec=pl.BlockSpec(five,lambda j,s:(a,j,0,0,0)); one=pl.BlockSpec((1,4,rows,lanes),lambda j,s:(j,0,0,0))
    if stage=="first":
        return pl.pallas_call(functools.partial(first_kernel,blocks),
            grid_spec=pltpu.PrefetchScalarGridSpec(num_scalar_prefetch=1,grid=(2,),in_specs=specs+[got_spec],out_specs=one),
            out_shape=S((2,4,rows,lanes),bf16),cost_estimate=cost,name=name)(info,*args,got)
    full=pl.BlockSpec((4,rows,lanes),lambda j,s:(0,0,0))
    return pl.pallas_call(functools.partial(second_kernel,blocks),
        grid_spec=pltpu.PrefetchScalarGridSpec(num_scalar_prefetch=1,grid=(2,),in_specs=specs+[got_spec,one],out_specs=[full,full]),
        out_shape=[S((4,rows,lanes),bf16)]*2,cost_estimate=cost,name=name)(info,*args,got,came)

def core_swap(value):
    return lax.ppermute(value, "cc", [(0, 1), (1, 0)])


def swap_by(blocks, index):
    pairs = blocks.reshape((2, 2) + blocks.shape[1:])
    pairs = jnp.where((index // 2) == 1, pairs[::-1], pairs)
    pairs = jnp.where((index % 2) == 1, pairs[:, ::-1], pairs)
    return pairs.reshape(blocks.shape)


def dp_halves(value, c):
    if lax.axis_size("dp") != 2:
        whole = lax.all_gather(value, "dp", axis=0, tiled=True)
        halves = whole.reshape((2, whole.shape[0] // 2) + whole.shape[1:])
        return jnp.where(c == 0, halves[0], halves[1]), jnp.where(c == 0, halves[1], halves[0])
    other = swap2(value, "dp")
    same = lax.axis_index("dp") == c
    return jnp.where(same, value, other), jnp.where(same, other, value)


def dp_sum(this_half, other_half, c):
    whole = jnp.concatenate(
        [jnp.where(c == 0, this_half, other_half), jnp.where(c == 0, other_half, this_half)], axis=0
    )
    return lax.psum_scatter(whole.astype(bf16), "dp", scatter_dimension=0, tiled=True).astype(f32)


def pack_output(part, norms):
    third = part.shape[0] // 3
    wide = 256 - part.shape[1]
    addends = jnp.pad(norms.reshape(3, -1, wide), ((0, 0), (0, third - norms.shape[1] // wide), (0, 0)))
    pieces = []
    for j in range(3):
        pieces += [part[j * third : (j + 1) * third], addends[j]]
    return jnp.concatenate(pieces, axis=1)


def unpack_output(packed, feat):
    return jnp.concatenate([packed[:, j * 256 : j * 256 + feat] for j in range(3)], axis=0)


def pack_norms(first_gain, first_shift, second_gain, second_shift):
    line = jnp.concatenate([first_gain, first_shift, second_gain, second_shift])
    high = lax.reduce_precision(line, 8, 7)
    middle_part = lax.reduce_precision(line - high, 8, 7)
    return jnp.stack([high, middle_part, line - high - middle_part]).astype(bf16)


def after(value, *earlier):
    return lax.optimization_barrier((value,) + earlier)[0]


def swap2(value, axis):
    return lax.ppermute(value, axis, [(0, 1), (1, 0)])


def crossed(value, axes, first):
    pairs = []
    for u in range(2):
        for v in range(2):
            for core in range(2):
                along = first ^ core
                pairs.append(((u * 2 + v) * 2 + core, ((u ^ (1 - along)) * 2 + (v ^ along)) * 2 + core))
    return lax.ppermute(value, axes + ("cc",), pairs)


PLANE = ("dp", "cy")


def scatter_steps(keep, send, axes, *between):
    first = after(crossed(send, axes, 0), *between)
    second = crossed(jnp.stack([keep[1], first[1]]), axes, 1)
    return keep, first, second


def by_slot(three):
    keep, first, second = three
    return [keep[0], second[0], first[0], second[1]]


def row_pair(block, *between):
    return jnp.stack([block, after(crossed(block, ROW, 1), *between)])


def row_rest(pair, *between):
    return jnp.concatenate([pair, after(crossed(pair, ROW, 0), *between)], axis=0)


def core_copies(arrays, ties):
    return arrays + [core_swap(after(array, *tie)) for array, tie in zip(arrays, ties)]


def gather_generic(w_output, w_inner, w_outer, norms, row, y, c):
    inner, outer, output = (lax.all_gather(w, "dp", axis=0, tiled=True) for w in (w_inner, w_outer, w_output))
    chunks = []
    for which in range(2):
        halves = []
        for g in range(2):
            parts = [w.reshape((2, w.shape[0] // 2) + w.shape[1:])[g] for w in (inner, outer, output)]
            if which == 0:
                halves.append(jnp.concatenate([parts[0], pack_output(parts[2], norms)], axis=0))
            else:
                halves.append(parts[1].T)
        whole = lax.all_gather(jnp.stack(halves), GROUP)
        flat = whole.reshape((-1,) + whole.shape[2:])
        arrays = []
        for kc in range(2):
            core = c ^ kc
            for spot in range(4):
                first, second = spot % 2, spot // 2
                kx = jnp.where(core == 0, second, first)
                ky = jnp.where(core == 0, first, second)
                steps = [jnp.where(core == 0, i, (i % 2) * 2 + i // 2) for i in range(4)]
                spots = jnp.stack([((row ^ k) * 4 + (y ^ ky) * 2 + core) * 2 + kx for k in steps])
                arrays.append(jnp.take(flat, spots, axis=0))
        chunks.append(arrays)
    return chunks


def add_parts(parts):
    total = parts[0].astype(f32)
    for part in parts[1:]:
        total = total + part.astype(f32)
    return total


def halve(stack):
    pass_on = crossed(stack[2:], ROW, 0)
    pair = (stack[:2].astype(f32) + pass_on.astype(f32)).astype(bf16)
    return pair[0].astype(f32) + crossed(pair[1], ROW, 1).astype(f32)


def generic_inner(first, keep, send, c):
    parts = [keep, send, first[0], first[1]]
    by_x = [
        (parts[0], jnp.where(c == 0, parts[1], parts[2])),
        (jnp.where(c == 0, parts[2], parts[1]), parts[3]),
    ]
    planes = [add_parts([own, swap2(other, "cy")]).astype(bf16) for own, other in by_x]
    return [halve(plane) for plane in planes]


def generic_outer(row_sum, c):
    by_x = [
        (row_sum[0], jnp.where(c == 0, row_sum[1], row_sum[2])),
        (jnp.where(c == 0, row_sum[2], row_sum[1]), row_sum[3]),
    ]
    return [add_parts([own, swap2(other, "cy")]) for own, other in by_x]


def local(
    tokens, w_query, w_key, w_value, w_output, w_inner, w_outer,
    first_gain, first_shift, second_gain, second_shift, seq_lengths, out_grad,
):
    feat = tokens.shape[1]
    cols = tokens.shape[2]
    half = cols // 2
    head_width = w_query.shape[1]
    heads = head_width // HD
    two = lax.axis_size("dp") == 2
    row = lax.axis_index(ROW)
    group = lax.axis_index("dp")
    m = lax.axis_index("rm")
    z = lax.axis_index("rz")
    y = lax.axis_index("cy")
    c = lax.axis_index("cc")
    length = lax.dynamic_index_in_dim(seq_lengths[m], group, keepdims=False)
    own_start = (y * 2 + c) * cols + z * half
    info = jnp.stack([
        row, z, y, c, length - own_start, group if two else 0 * group, 0 * y, 0 * y,
    ]).astype(jnp.int32)

    def turn(blocks):
        pairs = blocks.reshape((2, 2) + blocks.shape[1:])
        return jnp.where(c == 0, pairs, pairs.swapaxes(0, 1)).reshape(blocks.shape)

    def to_slots(array):
        blocks = array.reshape(2, feat, 2, half).transpose(0, 2, 1, 3).reshape(4, feat, half)
        return turn(swap_by(blocks, row))

    def from_slots(parts):
        back = swap_by(turn(jnp.stack(parts)), row)
        return back.reshape(2, 2, feat, half).transpose(0, 2, 1, 3).reshape(2, feat, cols)

    token_blocks = to_slots(tokens)
    this_half, other_half = dp_halves(jnp.concatenate([after(w_query, token_blocks), w_key, w_value], axis=1), c)
    token_three = scatter_steps(token_blocks[:2], token_blocks[2:], ROW)
    x_own = jnp.stack(by_slot(token_three))
    other_columns = core_swap(other_half)
    norms = pack_norms(first_gain, first_shift, second_gain, second_shift)
    if two:
        block_a = jnp.concatenate([after(w_inner, token_blocks), pack_output(w_output, norms)], axis=0)
        pair_a = row_pair(block_a)
        block_b = w_outer.T
        near_b = crossed(after(block_b, token_blocks), ROW, 1)
    pieces = []
    for s in range(4):
        step = jnp.where(c == 0, s % 2, s // 2)
        pieces.append(jnp.where((z ^ step) == c, this_half, other_columns))
    mine = jnp.stack(by_slot(scatter_steps(jnp.stack(pieces[:2]), jnp.stack(pieces[2:]), ROW)))
    theirs = core_swap(mine)
    if two:
        row_a = row_rest(pair_a)
        x_own = after(x_own, pair_a)
    x_second = crossed(x_own, SQUARE, 1)
    xs = (x_own, x_second, crossed(jnp.stack([x_own, x_second]), SQUARE, 0))
    if two:
        xs = (after(x_own, row_a),) + xs[1:]

    starts = []
    for kc in range(2):
        core = c ^ kc
        for s in range(4):
            z_here = z ^ jnp.where(core == 0, s // 2, s % 2)
            y_here = y ^ jnp.where(core == 0, s % 2, s // 2)
            starts.append((y_here * 2 + core) * cols + z_here * half)
    positions = (jnp.stack(starts)[:, None] + jnp.arange(half, dtype=jnp.int32)[None, :]).reshape(-1)
    invalid = jnp.where(positions < length, 0.0, masked_score)
    bias = jnp.where(jnp.arange(HD)[:, None] == 0, invalid[None, :], 0.0).astype(bf16)
    frequency = 10000.0 ** (-2.0 * jnp.arange(HD // 2, dtype=f32) / HD)
    frequency = after(frequency, token_three[1])
    angles = frequency[:, None] * positions[: 4 * half].astype(f32)[None, :]
    cosine = jnp.repeat(jnp.cos(angles), 2, axis=0)
    sines = jnp.sin(angles)
    sine = jnp.stack([-sines, sines], axis=1).reshape(HD, 4 * half)

    q_rot, kv_own = qkv(info, xs, mine, theirs, cosine, sine)
    kv_other = core_swap(kv_own)
    out_b, log_b, low_b = attend(1, q_rot, kv_own, kv_other, bias)
    low_first = crossed(low_b, SQUARE, 0)
    cot_blocks = to_slots(after(out_grad, kv_own))
    cot_first = after(crossed(cot_blocks[2:], ROW, 0), low_b)
    cot_pass = jnp.stack([cot_blocks[1], cot_first[1]])
    cot_second = crossed(cot_pass, ROW, 1)
    cot_three = (cot_blocks[:2], cot_first, cot_second)
    q_second = after(q_rot, low_b, cot_pass)
    if two:
        near_a, far_a = crossed(row_a, PLANE, 1), crossed(row_a, PLANE, 0)
        both_a = crossed(after(near_a, kv_own), PLANE, 0)
        row_a_swapped = core_swap(row_a)
        far_a = after(far_a, low_b)
        both_a = after(both_a, low_b)
        pair_b = jnp.stack([block_b, after(near_b, xs[1])])
        row_b = row_rest(pair_b, low_b)
        q_second = after(q_second, row_a_swapped, far_a, row_b)
        near_b, far_b = crossed(row_b, PLANE, 1), crossed(row_b, PLANE, 0)
    out_a, log_a, low_a = attend(0, q_second, kv_own, kv_other, bias)
    low_pass = jnp.stack([low_a[1], after(low_first, low_a)[1]])
    low_second = crossed(low_pass, SQUARE, 1)
    attn_three = (low_a, low_first, low_second)
    if two:
        both_b = crossed(after(near_b, low_second, cot_second), PLANE, 0)
        chunk_a = [row_a, near_a, far_a, both_a, row_a_swapped] + [core_swap(after(part, low_a)) for part in (near_a, far_a, both_a)]
        chunk_b = core_copies([row_b, near_b, far_b, both_b], [(low_a,), (low_pass,), (low_pass,), (low_pass,)])
    else:
        chunk_a, chunk_b = gather_generic(w_output, w_inner, w_outer, norms, row, y, c)
    mixed_keep, mixed_send, e_keep, e_send, grad_one, attn_t, hidden_t, outer_t, branch_low, act_low, inner_low, norm_sums = middle(
        info, attn_three, x_own, cot_three, chunk_a, chunk_b
    )
    inner_args = (hidden_t, inner_low, attn_t, branch_low, norm_sums)
    outer_args = (outer_t, act_low)

    def tied(args, *earlier):
        return (after(args[0], *earlier),) + args[1:]

    def head_back(first, count, *earlier):
        return attend_back(
            first, count, after(q_rot, *earlier), kv_own, kv_other, bias, (out_a, out_b), (log_a, log_b), grads, cosine, sine
        )

    give_outer = grad_call("outer", "give", info, outer_args)
    got_outer = core_swap(give_outer)
    grads_first = after(crossed(e_send, SQUARE, 0), give_outer)
    grads_pass = jnp.stack([e_keep[1], grads_first[1]])
    grads = (e_keep, grads_first, crossed(grads_pass, SQUARE, 1))
    give_inner = grad_call("inner", "give", info, tied(inner_args, give_outer, grads_pass))
    got_inner = core_swap(give_inner)
    mixed_first = after(crossed(mixed_send, ROW, 0), give_inner)
    mixed_pass = jnp.stack([mixed_keep[1], mixed_first[1]])
    first_outer = grad_call("outer", "first", info, tied(outer_args, mixed_pass, grads[2]), got_outer)
    came_outer = crossed(first_outer, ROW, 0)
    first_inner = grad_call("inner", "first", info, tied(inner_args, first_outer, mixed_pass), got_inner)
    came_inner = crossed(first_inner, PLANE, 0) if two else jnp.zeros_like(first_inner)
    mixed_second = crossed(mixed_pass, ROW, 1)
    dq, own, send = head_back(0, heads, first_inner, mixed_second)
    came_outer = after(came_outer, dq)
    own = after(own, came_outer)
    dkv_got = core_swap(send)
    dx_keep, dx_send, proj = finish_dx(info, dq, own, dkv_got, mine, theirs, cosine, sine)
    dx_first = crossed(dx_send, SQUARE, 0)
    keep_outer, pass_outer = grad_call(
        "outer", "second", info, tied(outer_args, dx_keep), got_outer, after(came_outer, dx_keep)
    )
    keep_inner, pass_inner = grad_call(
        "inner", "second", info, tied(inner_args, keep_outer), got_inner, after(came_inner, keep_outer)
    )
    dx_first = after(dx_first, keep_inner)
    dx_pass = (dx_keep[1] + dx_first[1].astype(f32)).astype(bf16)
    dx_second = crossed(dx_pass, SQUARE, 1)
    keep, give = finish_dw(info, after(proj, dx_pass), xs)
    got = core_swap(give)
    dx_second = after(dx_second, give)
    d_x = add_parts([grad_one, dx_keep[0], dx_first[0], dx_second]).astype(bf16)
    d_x_first = crossed(d_x[2:], ROW, 0)
    by_row_step = keep + after(got, d_x).astype(f32)
    if two:
        here = group == c
        across = lax.ppermute(
            by_row_step.astype(bf16), ("dp", "cc"), [(2, 0), (1, 3)]
        )
    plane_parts = (keep_inner, after(crossed(pass_inner, PLANE, 1), by_row_step)) if two else None
    if two:
        plane_inner = add_parts(plane_parts).astype(bf16)
        pass_on_inner = crossed(plane_inner[2:], ROW, 0)
    row_outer = add_parts([keep_outer, after(crossed(pass_outer, ROW, 1), by_row_step)]).astype(bf16)
    if two:
        pass_on_outer = crossed(row_outer[2:], PLANE, 0)
        d_x_first = after(d_x_first, plane_inner, row_outer)
    d_x_pass = jnp.stack([d_x[1], d_x_first[1]])
    d_x_second = crossed(d_x_pass, ROW, 1)
    if two:
        summed = by_row_step + after(across, d_x_pass).astype(f32)
        active = [(g * 5 + 2 * side, g * 5 + 2 * (1 - side)) for g in range(2) for side in range(2)]
        passed_m = lax.ppermute(summed[2:].astype(bf16), ("dp", "rm", "cc"), active)
        pair_inner = (plane_inner[:2].astype(f32) + after(pass_on_inner, summed).astype(f32)).astype(bf16)
        last_inner = crossed(pair_inner[1], ROW, 1)
        pair_outer = (row_outer[:2].astype(f32) + after(pass_on_outer, pair_inner).astype(f32)).astype(bf16)
        last_outer = crossed(pair_outer[1], PLANE, 1)
        near_far = summed[:2] + after(passed_m, pair_outer).astype(f32)
        far_low = lax.ppermute(near_far[1].astype(bf16), ("dp", "rz", "cc"), active)
        d_x_second = after(d_x_second, near_far)
        d_input = from_slots(by_slot((d_x[:2], d_x_first, d_x_second))).astype(f32)
        near_sum = near_far[0]
        far_sum = after(far_low, d_x_second).astype(f32)
        kept = jnp.where(z == c, near_sum, far_sum)
        passed = core_swap(jnp.where(z == c, far_sum, near_sum).astype(bf16)).astype(f32)
        g_qkv = jnp.where(here, kept, passed)
        inner_sums = [pair_inner[0].astype(f32) + after(last_inner, far_sum).astype(f32)]
        outer_sums = [pair_outer[0].astype(f32) + after(last_outer, far_sum).astype(f32)]
    else:
        near_far = by_row_step[:2] + swap2(by_row_step[2:].astype(bf16), "rm").astype(f32)
        near_sum = near_far[0]
        far_sum = swap2(near_far[1].astype(bf16), "rz").astype(f32)
        kept = jnp.where(z == c, near_sum, far_sum)
        passed = core_swap(jnp.where(z == c, far_sum, near_sum).astype(bf16)).astype(f32)
        d_input = from_slots(by_slot((d_x[:2], d_x_first, d_x_second))).astype(f32)
        g_qkv = dp_sum(kept, passed, c)
        outer_sums = generic_outer(row_outer, c)
        inner_sums = generic_inner(first_inner, keep_inner, pass_inner, c)
    mixed_out = from_slots(by_slot((mixed_keep, mixed_first, mixed_second)))

    half_rows = feat // 2
    third = half_rows // 3
    g_outer = jnp.concatenate([part.T for part in outer_sums], axis=0)
    g_inner = jnp.concatenate([part[:half_rows] for part in inner_sums], axis=0)
    g_output = jnp.concatenate(
        [unpack_output(part[half_rows : half_rows + third], feat) for part in inner_sums], axis=0
    )
    g_norms = inner_sums[0][half_rows : half_rows + 4 * feat // (256 - feat), feat:256].reshape(4, feat)
    if not two:
        g_outer, g_inner, g_output = (
            lax.psum_scatter(g.astype(bf16), "dp", scatter_dimension=0, tiled=True).astype(f32)
            for g in (g_outer, g_inner, g_output)
        )
        g_norms = lax.psum(g_norms, "dp")

    return (
        mixed_out, d_input,
        g_qkv[:, :head_width], g_qkv[:, head_width : 2 * head_width], g_qkv[:, 2 * head_width :],
        g_output, g_inner, g_outer,
        g_norms[0], g_norms[1], g_norms[2], g_norms[3],
    )


def solution(mesh):
    shape = mesh.devices.shape
    fine = Mesh(mesh.devices.reshape(shape[0], 2, shape[1] // 2, 2, shape[2] // 2), EVERY)
    col = ("cy", "cc")
    acts = P(None, ROW, ("dp",) + col)
    by_row = P(ROW + ("dp",), col)
    by_col = P(col + ("dp",), ROW)
    vec = P(ROW)
    return jax.shard_map(
        local,
        mesh=fine,
        in_specs=(
            acts, by_row, by_row, by_row, by_col, by_row, by_col, vec, vec, vec, vec, P(), acts,
        ),
        out_specs=(
            acts, acts, by_row, by_row, by_row, by_col, by_row, by_col, vec, vec, vec, vec,
        ),
        check_vma=False,
    )
```

```python
import functools

import jax
import jax.numpy as jnp
from jax import lax
from jax.experimental import pallas as pl
from jax.experimental.pallas import tpu as pltpu
from jax.sharding import Mesh, PartitionSpec as P

HD = 64
EVERY = ("dp", "rm", "rz", "cy", "cc")
GROUP = ("rm", "rz", "cy", "cc")
ROW = ("rm", "rz")
SQUARE = ("rz", "cy")
bf16=jnp.bfloat16; f32=jnp.float32
LOG2E=1.4426950408889634
LN2=0.6931471805599453
masked_score=-1e30

def mm(a,b,dims=((1,),(0,))):
    return lax.dot_general(a,b,(dims,((),())),preferred_element_type=f32)
NT=((1,),(1,))

def pair_turn(values, cosine, signed_sine):
    shape = values.shape
    v3 = values.reshape(shape[0]//8, 8, shape[1])
    up = pltpu.roll(v3, 7, 1); down = pltpu.roll(v3, 1, 1)
    even = (lax.broadcasted_iota(jnp.int32, v3.shape, 1) % 2) == 0
    other = jnp.where(even, up, down).reshape(shape)
    return values*cosine + other*signed_sine

KB=1024
QB=2
def one_row(shape, dtype, value=1.0):
    return jnp.where(lax.broadcasted_iota(jnp.int32, shape, 0)==0, value, 0.0).astype(dtype)

def attend_kernel(q_ref, ko_ref, vo_ref, kx_ref, vx_ref, bias_ref, o_ref, lse_ref, low_ref, kaug, vall):
    span=ko_ref.shape[1]
    for part,(kr,vr) in enumerate(((ko_ref,vo_ref),(kx_ref,vx_ref))):
        aug=jnp.concatenate([kr[...], bias_ref[:, part*span:(part+1)*span]],axis=0)
        kaug[part*span:(part+1)*span,:]=aug.T
        vall[:, part*span:(part+1)*span]=vr[...]
    n=q_ref.shape[1]
    qaug=jnp.concatenate([q_ref[...], one_row((HD,n),bf16)],axis=0)
    top=jnp.full((1,n),-3e38,f32); total=jnp.zeros((1,n),f32); acc=jnp.zeros((HD,n),f32)
    s=mm(kaug[0:KB,:],qaug)
    for kb in range(0,2*span,KB):
        following=mm(kaug[kb+KB:kb+2*KB,:],qaug) if kb+KB<2*span else None
        new=jnp.maximum(top,jnp.max(s,axis=0,keepdims=True))
        alpha=jnp.exp2(top-new)
        p=jnp.exp2(s-new)
        total=total*alpha+jnp.sum(p,axis=0,keepdims=True)
        acc=acc*alpha+mm(vall[:,kb:kb+KB],p.astype(bf16))
        top=new
        s=following
    out=acc/total
    o_ref[...]=out
    lse_ref[0]=top+jnp.log2(total)
    low=out.astype(bf16)
    for b in range(2):
        low_ref[b]=low[:,b*(n//2):(b+1)*(n//2)]

def attend(part,q,kv,kvx,bias):
    width,n4=q.shape; heads=width//HD; n=n4//2; span=kv.shape[1]
    kspec=pl.BlockSpec((HD,span),lambda h:(h,0)); vspec=pl.BlockSpec((HD,span),lambda h:(heads+h,0))
    return pl.pallas_call(attend_kernel,grid=(heads,),
        in_specs=[pl.BlockSpec((HD,n),lambda h:(h,part)),kspec,vspec,kspec,vspec,pl.BlockSpec((HD,2*span),lambda h:(0,0))],
        out_specs=[pl.BlockSpec((HD,n),lambda h:(h,0)),pl.BlockSpec((1,1,n),lambda h:(h,0,0)),pl.BlockSpec((2,HD,n//2),lambda h:(0,h,0))],
        out_shape=[jax.ShapeDtypeStruct((width,n),f32),jax.ShapeDtypeStruct((heads,1,n),f32),jax.ShapeDtypeStruct((2,width,n//2),bf16)],
        scratch_shapes=[pltpu.VMEM((2*span,2*HD),bf16),pltpu.VMEM((HD,2*span),bf16)],
        cost_estimate=pl.CostEstimate(flops=int(6.0*(2*width*n4//HD*2*span*256))+1,bytes_accessed=int(6.0*(2*n4*2*span))+1,transcendentals=int(6.0*(heads*n*2*span))+1),
        name="attend")(q,kv,kv,kvx,kvx,bias)

BKB=512
def attend_back_kernel(q_ref, ko_ref, vo_ref, kx_ref, vx_ref, bias_ref, oa_ref, ob_ref, lsea_ref, lseb_ref, g0,g1,g2,g3, cos_ref, sin_ref,
                       dq_ref, own_ref, give_ref, kaug, vtm, kall, acc):
    qb=pl.program_id(1)
    span=ko_ref.shape[1]; n=q_ref.shape[1]
    @pl.when(qb==0)
    def _():
        for part,(kr,vr) in enumerate(((ko_ref,vo_ref),(kx_ref,vx_ref))):
            sl=slice(part*span,(part+1)*span)
            kaug[sl,:]=jnp.concatenate([kr[...], bias_ref[:, sl]],axis=0).T
            vtm[sl,:]=jnp.concatenate([vr[...], jnp.zeros((HD,span),bf16)],axis=0).T
            kall[:,sl]=kr[...]
        acc[...]=jnp.zeros_like(acc)
    q=q_ref[...]
    zeros=jnp.zeros((HD,n),bf16)
    qaug=jnp.concatenate([q, one_row((HD,n),bf16)],axis=0)
    g=jnp.concatenate([jnp.where(qb==0,g0[...],g2[...]),jnp.where(qb==0,g1[...],g3[...])],axis=1)
    o=jnp.where(qb==0,oa_ref[...],ob_ref[...])
    qpad=jnp.concatenate([q,zeros],axis=0).T
    gpad=jnp.concatenate([zeros,g],axis=0).T
    gaug=jnp.concatenate([g,zeros],axis=0)
    delta=jnp.sum(g.astype(f32)*o,axis=0,keepdims=True)
    lse=jnp.where(qb==0,lsea_ref[0],lseb_ref[0])
    dq=jnp.zeros((HD,n),f32)
    s=mm(kaug[0:BKB,:],qaug); dp=mm(vtm[0:BKB,:],gaug)
    for kb in range(0,2*span,BKB):
        last=kb+BKB>=2*span
        s_next=None if last else mm(kaug[kb+BKB:kb+2*BKB,:],qaug)
        dp_next=None if last else mm(vtm[kb+BKB:kb+2*BKB,:],gaug)
        p=jnp.exp2(s-lse)
        ds=(p*(dp-delta)).astype(bf16)
        dq=dq+mm(kall[:,kb:kb+BKB],ds)
        acc[kb:kb+BKB,:]=acc[kb:kb+BKB,:]+mm(ds,qpad)+mm(p.astype(bf16),gpad)
        s=s_next; dp=dp_next
    dq_ref[...]=pair_turn(dq*(HD**-0.5),cos_ref[...],-sin_ref[...]).astype(bf16)
    @pl.when(qb==4//QB-1)
    def _():
        own_ref[...]=acc[:span,:]
        give_ref[...]=acc[span:,:].astype(bf16)

def attend_back(first,count,q,kv,kvx,bias,os,lses,grads,cos,sin):
    width,n4=q.shape; heads=width//HD; n=n4//4*QB; span=kv.shape[1]
    kspec=pl.BlockSpec((HD,span),lambda h,b:(first+h,0)); vspec=pl.BlockSpec((HD,span),lambda h,b:(heads+first+h,0))
    gspec=lambda i:pl.BlockSpec((None,HD,n4//4),lambda h,b:(i,first+h,0)); tb=pl.BlockSpec((HD,n),lambda h,b:(0,b))
    dspec=pl.BlockSpec((None,span,2*HD),lambda h,b:(h,0,0)); ospec=pl.BlockSpec((HD,n),lambda h,b:(first+h,0)); lspec=pl.BlockSpec((1,1,n),lambda h,b:(first+h,0,0))
    return pl.pallas_call(attend_back_kernel,grid=(count,4//QB),
        in_specs=[pl.BlockSpec((HD,n),lambda h,b:(first+h,b)),kspec,vspec,kspec,vspec,pl.BlockSpec((HD,2*span),lambda h,b:(0,0)),ospec,ospec,lspec,lspec,gspec(0),gspec(0),gspec(0),gspec(1),tb,tb],
        out_specs=[pl.BlockSpec((HD,n),lambda h,b:(h,b)),dspec,dspec],
        out_shape=[jax.ShapeDtypeStruct((count*HD,n4),bf16),jax.ShapeDtypeStruct((count,span,2*HD),f32),jax.ShapeDtypeStruct((count,span,2*HD),bf16)],
        scratch_shapes=[pltpu.VMEM((2*span,2*HD),bf16),pltpu.VMEM((2*span,2*HD),bf16),pltpu.VMEM((HD,2*span),bf16),pltpu.VMEM((2*span,2*HD),f32)],
        cost_estimate=pl.CostEstimate(flops=int(6.0*(count*10*n4*2*span*256))+1,bytes_accessed=int(6.0*(count*4*n4*2*span))+1,transcendentals=int(6.0*(count*n4*2*span))+1),
        name="attend_back")(q,kv,kv,kvx,kvx,bias,*os,*lses,grads[0],grads[2],grads[1],grads[2],cos,sin)
def xor(a,b):
    return lax.bitwise_xor(jnp.asarray(a,jnp.int32),jnp.asarray(b,jnp.int32))

def rows_at(index,size,align):
    return pl.ds(pl.multiple_of(index*size,align),size)

def row_step(core,slot):
    return jnp.where(core==0,slot,(slot%2)*2+slot//2)

def z_step(core,slot):
    return jnp.where(core==0,slot//2,slot%2)

def y_step(core,slot):
    return jnp.where(core==0,slot%2,slot//2)

def slots(three):
    keep,first,second=three
    return (keep.at[0],second.at[0],first.at[0],second.at[1])

def place_qkv_weights(info, mine_ref, theirs_ref, w_s):
    row=info[0]; c=info[3]
    half=mine_ref.shape[1]
    for r in range(4):
        k=xor(r,row)
        w_s[pl.ds(pl.multiple_of((2*r+c)*half,32),half),:]=mine_ref[row_step(c,k)]
        w_s[pl.ds(pl.multiple_of((2*r+1-c)*half,32),half),:]=theirs_ref[row_step(1-c,k)]

def place_tokens(info, x_ref, slot, x_s):
    feat=x_ref.shape[1]; c=info[3]; base=xor(info[0],z_step(c,slot))
    for r in range(4):
        x_s[r*feat:(r+1)*feat,:]=x_ref[row_step(c,xor(r,base))]

def token_refs(own, second, others):
    return (own, second, others.at[0], others.at[1])

def qkv_kernel(info, xa,xb,xc, mine_ref, theirs_ref, cos_ref, sin_ref, q_ref, kv_ref, w_s, wt_s, x_s):
    place_qkv_weights(info,mine_ref,theirs_ref,w_s)
    wt_s[...]=w_s[...].T
    hw=q_ref.shape[0]; n=xa.shape[2]
    for k,xr in enumerate(token_refs(xa,xb,xc)):
        place_tokens(info,xr,k,x_s)
        out=mm(wt_s[...],x_s[...])
        sl=slice(k*n,(k+1)*n)
        cos=cos_ref[:,sl]; sin=sin_ref[:,sl]
        for h in range(2*hw//HD):
            turned=pair_turn(out[h*HD:(h+1)*HD],cos,sin)
            if h*HD<hw: q_ref[h*HD:(h+1)*HD,sl]=(turned*(HD**-0.5*LOG2E)).astype(bf16)
            else: kv_ref[h*HD-hw:(h+1)*HD-hw,sl]=turned.astype(bf16)
        kv_ref[hw:,sl]=out[2*hw:].astype(bf16)

VM=pl.BlockSpec(memory_space=pltpu.VMEM)
SM=pl.BlockSpec(memory_space=pltpu.SMEM)
HB=pl.BlockSpec(memory_space=pl.ANY)

def qkv(info,xs,mine,theirs,cos,sin):
    _,feat,n=xs[0].shape; w3=mine.shape[2]; hw=w3//3; width=4*feat
    return pl.pallas_call(qkv_kernel,in_specs=[SM]+[VM]*7,out_specs=[VM,VM],
        out_shape=[jax.ShapeDtypeStruct((hw,4*n),bf16),jax.ShapeDtypeStruct((2*hw,4*n),bf16)],
        scratch_shapes=[pltpu.VMEM((width,w3),bf16),pltpu.VMEM((w3,width),bf16),pltpu.VMEM((width,n),bf16)],
        name="qkv")(info,*xs,mine,theirs,cos,sin)

def finish_dx_kernel(info, *refs):
    (q_ref,own_ref,got_ref,mine_ref,theirs_ref,cos_ref,sin_ref,keep_ref,send_ref,p_ref,w_s)=refs
    hw=q_ref.shape[0]; n=keep_ref.shape[3]; feat=keep_ref.shape[2]; c=info[3]
    place_qkv_weights(info,mine_ref,theirs_ref,w_s)
    p_ref[0:hw,:]=q_ref[...]
    for h in range(hw//HD):
        t=(own_ref[h]+got_ref[h].astype(f32)).T
        p_ref[hw+h*HD:hw+(h+1)*HD,:]=pair_turn(t[:HD]*LN2,cos_ref[...],-sin_ref[...]).astype(bf16)
        p_ref[2*hw+h*HD:2*hw+(h+1)*HD,:]=t[HD:].astype(bf16)
    for k,dr in ((3,send_ref),(2,send_ref),(1,keep_ref),(0,keep_ref)):
        sl=slice(k*n,(k+1)*n)
        base=xor(info[0],z_step(c,k))
        for r in range(4):
            dr[k%2,row_step(c,xor(r,base))]=mm(w_s[r*feat:(r+1)*feat,:],p_ref[:,sl]).astype(dr.dtype)

def finish_dx(info,dq,own,got,mine,theirs,cos,sin):
    w3=mine.shape[2]; half=mine.shape[1]; feat=2*half; width=4*feat; n=dq.shape[1]//4
    S=jax.ShapeDtypeStruct
    return pl.pallas_call(finish_dx_kernel,in_specs=[SM]+[VM]*7,out_specs=[VM]*3,
        out_shape=[S((2,4,feat,n),f32),S((2,4,feat,n),bf16),S((w3,4*n),bf16)],
        scratch_shapes=[pltpu.VMEM((width,w3),bf16)],
        cost_estimate=pl.CostEstimate(flops=int(0.0*(8*width*w3*n))+1,bytes_accessed=int(0.0*(8*width*n*4))+1,transcendentals=int(0.0*(0))+1),
        name="finish_dx")(info,dq,own,got,mine,theirs,cos,sin)

def finish_dw_kernel(info, p_ref, xa,xb,xc, keep_ref, give_ref, x_s, g_s):
    n=xa.shape[2]; half=keep_ref.shape[1]
    for k,xr in enumerate(token_refs(xa,xb,xc)):
        place_tokens(info,xr,k,x_s.at[:,k*n:(k+1)*n])
    g_s[...]=mm(x_s[...],p_ref[...],NT)
    c=info[3]; row=info[0]
    for r in range(4):
        mine_rows=pl.ds(pl.multiple_of((2*r+c)*half,32),half); their_rows=pl.ds(pl.multiple_of((2*r+1-c)*half,32),half)
        keep_ref[xor(r,row)]=g_s[mine_rows,:]
        give_ref[xor(r,row)]=g_s[their_rows,:].astype(bf16)

def finish_dw(info,proj,xs):
    _,feat,n=xs[0].shape; w3=proj.shape[0]; width=4*feat; half=feat//2
    return pl.pallas_call(finish_dw_kernel,in_specs=[SM]+[VM]*4,out_specs=[VM]*2,
        out_shape=[jax.ShapeDtypeStruct((4,half,w3),f32),jax.ShapeDtypeStruct((4,half,w3),bf16)],
        scratch_shapes=[pltpu.VMEM((width,4*n),bf16),pltpu.VMEM((width,w3),f32)],
        cost_estimate=pl.CostEstimate(flops=int(6.0*(8*width*w3*n))+1,bytes_accessed=int(6.0*(8*width*n*2))+1,transcendentals=int(6.0*(0))+1),
        name="finish_dw")(info,proj,*xs)

def middle_kernel(info, a0,a1,a2, x_ref, c0,c1,c2, *refs):
    chunk_a=refs[:8]; chunk_b=refs[8:16]
    (mixk_ref, mixs_ref, ek_ref, es_ref, g1_ref, attnT_ref, hidT_ref, outT_ref, bl_ref, act_ref, il_ref, norm_ref,
                  win, woT, wo, wpk, gp_s, t_s, f_s, sems)=refs[16:]
    row=info[0]; z=info[1]; y=info[2]; c=info[3]; group=info[5]
    feat=a0.shape[1]; n=a0.shape[2]; width=4*feat; ffc=chunk_a[0].shape[2]; half=feat//2; fh=ffc//2; third=half//3
    def go(src,dst,s): pltpu.make_async_copy(src,dst,sems.at[s]).start()
    def each(chunk):
        for kc in range(2):
            core=xor(c,kc)
            for spot,ref in enumerate(chunk[4*kc:4*kc+4]):
                first,second=spot%2,spot//2
                kx=jnp.where(core==0,second,first); ky=jnp.where(core==0,first,second)
                g=xor(group,kx); col=xor(y,ky)*2+core
                for i in range(4):
                    step=row_step(core,i)
                    yield ref.at[i],xor(row,step),g,col,kc+spot
    for ref,r,g,col,_ in each(chunk_a):
        go(ref.at[half:half+third,:],wpk.at[r,col*2+g],0)
    for ref,r,g,col,_ in each(chunk_a):
        go(ref.at[0:half,:],win.at[pl.ds(pl.multiple_of(r*feat+g*half,16),half),pl.ds(pl.multiple_of(col*ffc,128),ffc)],1)
    for ref,r,g,col,_ in each(chunk_b):
        go(ref,woT.at[pl.ds(pl.multiple_of(r*feat,64),feat),pl.ds(pl.multiple_of((col*2+g)*fh,128),fh)],2)
    def group_of(s):
        return xor(y,y_step(c,s))*2+xor(z,z_step(c,s))
    def row_of(s):
        return xor(row,row_step(c,s))
    for s,ar in enumerate(slots((a0,a1,a2))):
        attnT_ref[rows_at(group_of(s),feat,64),:]=ar[...]
    for s in range(4):
        t_s[rows_at(row_of(s),feat,64),:]=x_ref[s]
    attn=attnT_ref[...].T
    x=t_s[...].T.astype(f32)
    pltpu.make_async_copy(wpk,wpk,sems.at[0]).wait()
    for r in range(4):
        for q in range(8):
            for j in range(3):
                wo[r,q*half+j*third:q*half+(j+1)*third,:]=wpk[r,q,:,j*256:(j+1)*256]
    wide=256-feat; pieces=feat//wide
    addends=[sum(wpk[r,0,0:16,j*256+feat:(j+1)*256].astype(f32) for j in range(3)) for r in range(4)]
    def vector(which):
        return jnp.concatenate([addends[r][which*pieces+t:which*pieces+t+1] for r in range(4) for t in range(pieces)],axis=1)
    gain1=vector(0); shift1=vector(1); gain2=vector(2); shift2=vector(3)
    branch=jnp.concatenate([mm(attn,wo[r])[:,:feat] for r in range(4)],axis=1)
    def stats(v):
        mean=jnp.sum(v,axis=1,keepdims=True)*(1.0/width)
        var=jnp.sum(v*v,axis=1,keepdims=True)*(1.0/width)-mean*mean
        inv=lax.rsqrt(var+1e-5)
        return (v-mean)*inv,inv
    cent1,inv1=stats(x+branch)
    hidden=cent1*gain1+shift1
    hid=hidden.astype(bf16)
    hidT_ref[...]=hid.T
    pltpu.make_async_copy(win,win,sems.at[1]).wait()
    pltpu.make_async_copy(woT,woT,sems.at[2]).wait()
    f_s[...]=jnp.zeros_like(f_s)
    nb=1; bw=ffc//nb
    def forward(j,carry):
        sl=pl.ds(pl.multiple_of(j*bw,128),bw)
        inner=mm(hid,win[:,sl])
        cdf=0.5+0.5*lax.erf(inner*0.7071067811865476)
        act=(inner*cdf).astype(bf16)
        gp_s[:,sl]=cdf+inner*(jnp.exp(inner*inner*-0.5)*0.3989422804014327)
        act_ref[:,sl]=act
        f_s[...]+=mm(act,woT[:,sl],NT)
        return carry
    lax.fori_loop(0,4*nb,forward,0)
    cent2,inv2=stats(hidden+f_s[...])
    t_s[...]=(cent2*gain2+shift2).astype(bf16).T
    for s in range(4):
        (mixk_ref,mixs_ref)[s//2][s%2]=t_s[rows_at(row_of(s),feat,64),:]
    for s,cr in enumerate(slots((c0,c1,c2))):
        t_s[rows_at(row_of(s),feat,64),:]=cr[...]
    valid=(lax.broadcasted_iota(jnp.int32,(n,1),0)<info[4]).astype(f32)
    cot=t_s[...].T.astype(f32)*valid
    sums2=(jnp.sum(cot*cent2,axis=0,keepdims=True),jnp.sum(cot,axis=0,keepdims=True))
    def back(e,cent,inv):
        first=jnp.sum(e,axis=1,keepdims=True)*(1.0/width)
        second=jnp.sum(e*cent,axis=1,keepdims=True)*(1.0/width)
        return inv*(e-first-cent*second)
    grad2=back(cot*gain2,cent2,inv2)
    low=grad2.astype(bf16)
    outT_ref[...]=low.T
    f_s[...]=grad2
    def backward(j,carry):
        sl=pl.ds(pl.multiple_of(j*bw,128),bw)
        il=(mm(low,woT[:,sl])*gp_s[:,sl]).astype(bf16)
        il_ref[:,sl]=il
        f_s[...]+=mm(il,win[:,sl],NT)
        return carry
    lax.fori_loop(0,4*nb,backward,0)
    gh=f_s[...]
    sums=jnp.concatenate((jnp.sum(gh*cent1,axis=0,keepdims=True),jnp.sum(gh,axis=0,keepdims=True))+sums2+(jnp.zeros((4,width),f32),),axis=0)
    for r in range(4):
        lines=[sums[i:i+1,r*feat+t*wide:r*feat+(t+1)*wide] for i in range(4) for t in range(pieces)]
        lines=jnp.concatenate(lines+[jnp.zeros((third-4*pieces,wide),f32)],axis=0)
        norm_ref[r]=jnp.concatenate([jnp.zeros((third,feat),f32),lines],axis=1)
    grad1=back(gh*gain1,cent1,inv1)
    bl=grad1.astype(bf16)
    da=jnp.zeros((width,n),f32)
    for r in range(4):
        piece=jnp.concatenate([bl[:,r*feat:(r+1)*feat],jnp.zeros((n,wide),bf16)],axis=1)
        bl_ref[r]=piece
        da=da+mm(wo[r],piece,NT)
    t_s[...]=da.astype(bf16)
    for s in range(4):
        (ek_ref,es_ref)[s//2][s%2]=t_s[rows_at(group_of(s),feat,64),:]
    f2=grad1.T
    for r in range(4):
        g1_ref[row_step(c,xor(r,row))]=f2[r*feat:(r+1)*feat]

def middle(info,attn_parts,x_own,cot_parts,chunk_a,chunk_b):
    _,feat,n=attn_parts[0].shape; width=4*feat; ff=4*chunk_a[0].shape[2]
    S=jax.ShapeDtypeStruct
    return pl.pallas_call(middle_kernel,in_specs=[SM]+[VM]*7+[HB]*16,out_specs=[VM]*12,
        out_shape=[S((2,feat,n),bf16)]*4+[S((4,feat,n),f32),S((width,n),bf16),S((width,n),bf16),S((width,n),bf16),
                   S((4,n,256),bf16),S((n,ff),bf16),S((n,ff),bf16),S((4,feat//6,256),f32)],
        scratch_shapes=[pltpu.VMEM((width,ff),bf16),pltpu.VMEM((width,ff),bf16),pltpu.VMEM((4,width,256),bf16),pltpu.VMEM((4,8,feat//6,width),bf16),
                        pltpu.VMEM((n,ff),f32),pltpu.VMEM((width,n),bf16),pltpu.VMEM((n,width),f32),pltpu.SemaphoreType.DMA((4,))],
        compiler_params=pltpu.CompilerParams(vmem_limit_bytes=56*1024*1024),
        cost_estimate=pl.CostEstimate(flops=int(6.0*(12*n*width*ff*2))+1,bytes_accessed=int(6.0*(24*width*ff))+1,transcendentals=int(6.0*(2*n*ff))+1),
        name="middle")(info,*attn_parts,x_own,*cot_parts,*chunk_a,*chunk_b)

def plane_target(info,core,slot):
    kx=jnp.where(core==0,slot//2,slot%2); ky=jnp.where(core==0,slot%2,slot//2)
    return xor(info[5],kx),xor(info[2],ky)*2+core

def target(info,which,a,b):
    core=xor(info[3],which)
    return (core,)+plane_target(info,core,2*a+b)

def outer_blocks(info,which,a,b,refs,put):
    outT_ref,act_near,act_far=refs
    core=xor(info[3],which)
    half=outT_ref.shape[0]//8; fh=act_near.shape[1]//2
    rows=outT_ref[rows_at(xor(info[0],row_step(core,2*a+b)),2*half,64),:]
    for ky,act_ref in enumerate((act_near,act_far)):
        value=mm(rows,act_ref[...])
        for g in range(2):
            kx=xor(g,info[5])
            slot=jnp.where(core==0,2*kx+ky,2*ky+kx)
            put(slot,slice(0,2*half),slice(0,fh),value[:,g*fh:(g+1)*fh])

def inner_blocks(info,which,a,b,refs,put):
    hidT_ref,il_ref,attnT_ref,bl_ref,norm_ref=refs
    core,g,col=target(info,which,a,b)
    half=hidT_ref.shape[0]//8; third=half//3
    rows=[xor(info[0],row_step(core,s)) for s in range(4)]
    lhs=jnp.concatenate([hidT_ref[rows_at(r*2+g,half,32),:] for r in rows],axis=0)
    value=mm(lhs,il_ref[...])
    heads=attnT_ref[rows_at(col*2+g,half,32),:]
    for s,r in enumerate(rows):
        put(s,slice(0,half),slice(None),value[s*half:(s+1)*half])
        outs=mm(heads,bl_ref[r])
        for j in range(3):
            piece=outs[j*third:(j+1)*third]
            if j==0: piece=piece+norm_ref[r]
            put(s,slice(half,half+third),slice(j*256,(j+1)*256),piece)

def give_kernel(blocks,info,*refs):
    out=refs[-1]
    def put(s,rows,lanes,value): out[0,0,s,rows,lanes]=value.astype(bf16)
    blocks(info,1,pl.program_id(0),pl.program_id(1),refs[:-1],put)

def first_kernel(blocks,info,*refs):
    got,out=refs[-2:]
    def put(s,rows,lanes,value): out[0,s,rows,lanes]=(value+got[0,0,s,rows,lanes].astype(f32)).astype(bf16)
    blocks(info,0,1,pl.program_id(0),refs[:-2],put)

def second_kernel(blocks,info,*refs):
    got,came,keep,send=refs[-4:]
    for b,out in ((0,keep),(1,send)):
        def put(s,rows,lanes,value):
            out[s,rows,lanes]=(value+got[0,0,s,rows,lanes].astype(f32)+came[0,s,rows,lanes].astype(f32)).astype(bf16)
        @pl.when(pl.program_id(0)==b)
        def _(): blocks(info,0,0,b,refs[:-4],put)

def grad_call(kind,stage,info,args,got=None,came=None):
    S=jax.ShapeDtypeStruct
    width,n=args[0].shape; ffc=args[1].shape[1]//4; half=width//8
    a={"give":None,"first":1,"second":0}[stage]; which=1 if stage=="give" else 0
    def at(index):
        if stage=="give": return lambda i,j,s:index(i,j,s)
        return lambda j,s:index(a,j,s)
    whole=pl.BlockSpec((width,n),at(lambda i,j,s:(0,0)))
    if kind=="inner":
        blocks,rows,lanes=inner_blocks,half+half//3,ffc
        specs=[whole,pl.BlockSpec((n,ffc),at(lambda i,j,s:(0,target(s,which,i,j)[2]))),whole,
               pl.BlockSpec((4,n,256),at(lambda i,j,s:(0,0,0))),pl.BlockSpec((4,half//3,256),at(lambda i,j,s:(0,0,0)))]
    else:
        blocks,rows,lanes=outer_blocks,2*half,ffc//2
        args=(args[0],args[1],args[1])
        def column(ky): return at(lambda i,j,s:(0,xor(s[2],ky)*2+xor(s[3],which)))
        specs=[whole,pl.BlockSpec((n,ffc),column(0)),pl.BlockSpec((n,ffc),column(1))]
    weight={"give":4,"first":2,"second":0}[stage]
    cost=pl.CostEstimate(flops=int(6.0*(weight*width*n*ffc))+1,bytes_accessed=int(6.0*(4*weight*rows*ffc))+1,transcendentals=int(6.0*(0))+1)
    name=kind+"_"+stage
    five=(1,1,4,rows,lanes)
    if stage=="give":
        return pl.pallas_call(functools.partial(give_kernel,blocks),
            grid_spec=pltpu.PrefetchScalarGridSpec(num_scalar_prefetch=1,grid=(2,2),in_specs=specs,out_specs=pl.BlockSpec(five,lambda i,j,s:(i,j,0,0,0))),
            out_shape=S((2,2,4,rows,lanes),bf16),cost_estimate=cost,name=name)(info,*args)
    got_spec=pl.BlockSpec(five,lambda j,s:(a,j,0,0,0)); one=pl.BlockSpec((1,4,rows,lanes),lambda j,s:(j,0,0,0))
    if stage=="first":
        return pl.pallas_call(functools.partial(first_kernel,blocks),
            grid_spec=pltpu.PrefetchScalarGridSpec(num_scalar_prefetch=1,grid=(2,),in_specs=specs+[got_spec],out_specs=one),
            out_shape=S((2,4,rows,lanes),bf16),cost_estimate=cost,name=name)(info,*args,got)
    full=pl.BlockSpec((4,rows,lanes),lambda j,s:(0,0,0))
    return pl.pallas_call(functools.partial(second_kernel,blocks),
        grid_spec=pltpu.PrefetchScalarGridSpec(num_scalar_prefetch=1,grid=(2,),in_specs=specs+[got_spec,one],out_specs=[full,full]),
        out_shape=[S((4,rows,lanes),bf16)]*2,cost_estimate=cost,name=name)(info,*args,got,came)

def core_swap(value):
    return lax.ppermute(value, "cc", [(0, 1), (1, 0)])


def swap_by(blocks, index):
    pairs = blocks.reshape((2, 2) + blocks.shape[1:])
    pairs = jnp.where((index // 2) == 1, pairs[::-1], pairs)
    pairs = jnp.where((index % 2) == 1, pairs[:, ::-1], pairs)
    return pairs.reshape(blocks.shape)


def dp_halves(value, c):
    if lax.axis_size("dp") != 2:
        whole = lax.all_gather(value, "dp", axis=0, tiled=True)
        halves = whole.reshape((2, whole.shape[0] // 2) + whole.shape[1:])
        return jnp.where(c == 0, halves[0], halves[1]), jnp.where(c == 0, halves[1], halves[0])
    other = swap2(value, "dp")
    same = lax.axis_index("dp") == c
    return jnp.where(same, value, other), jnp.where(same, other, value)


def dp_sum(this_half, other_half, c):
    whole = jnp.concatenate(
        [jnp.where(c == 0, this_half, other_half), jnp.where(c == 0, other_half, this_half)], axis=0
    )
    return lax.psum_scatter(whole.astype(bf16), "dp", scatter_dimension=0, tiled=True).astype(f32)


def pack_output(part, norms):
    third = part.shape[0] // 3
    wide = 256 - part.shape[1]
    addends = jnp.pad(norms.reshape(3, -1, wide), ((0, 0), (0, third - norms.shape[1] // wide), (0, 0)))
    pieces = []
    for j in range(3):
        pieces += [part[j * third : (j + 1) * third], addends[j]]
    return jnp.concatenate(pieces, axis=1)


def unpack_output(packed, feat):
    return jnp.concatenate([packed[:, j * 256 : j * 256 + feat] for j in range(3)], axis=0)


def pack_norms(first_gain, first_shift, second_gain, second_shift):
    line = jnp.concatenate([first_gain, first_shift, second_gain, second_shift])
    high = lax.reduce_precision(line, 8, 7)
    middle_part = lax.reduce_precision(line - high, 8, 7)
    return jnp.stack([high, middle_part, line - high - middle_part]).astype(bf16)


def after(value, *earlier):
    return lax.optimization_barrier((value,) + earlier)[0]


def swap2(value, axis):
    return lax.ppermute(value, axis, [(0, 1), (1, 0)])


def crossed(value, axes, first):
    pairs = []
    for u in range(2):
        for v in range(2):
            for core in range(2):
                along = first ^ core
                pairs.append(((u * 2 + v) * 2 + core, ((u ^ (1 - along)) * 2 + (v ^ along)) * 2 + core))
    return lax.ppermute(value, axes + ("cc",), pairs)


PLANE = ("dp", "cy")


def scatter_steps(keep, send, axes, *between):
    first = after(crossed(send, axes, 0), *between)
    second = crossed(jnp.stack([keep[1], first[1]]), axes, 1)
    return keep, first, second


def by_slot(three):
    keep, first, second = three
    return [keep[0], second[0], first[0], second[1]]


def row_pair(block, *between):
    return jnp.stack([block, after(crossed(block, ROW, 1), *between)])


def row_rest(pair, *between):
    return jnp.concatenate([pair, after(crossed(pair, ROW, 0), *between)], axis=0)


def core_copies(arrays, ties):
    return arrays + [core_swap(after(array, *tie)) for array, tie in zip(arrays, ties)]


def gather_generic(w_output, w_inner, w_outer, norms, row, y, c):
    inner, outer, output = (lax.all_gather(w, "dp", axis=0, tiled=True) for w in (w_inner, w_outer, w_output))
    chunks = []
    for which in range(2):
        halves = []
        for g in range(2):
            parts = [w.reshape((2, w.shape[0] // 2) + w.shape[1:])[g] for w in (inner, outer, output)]
            if which == 0:
                halves.append(jnp.concatenate([parts[0], pack_output(parts[2], norms)], axis=0))
            else:
                halves.append(parts[1].T)
        whole = lax.all_gather(jnp.stack(halves), GROUP)
        flat = whole.reshape((-1,) + whole.shape[2:])
        arrays = []
        for kc in range(2):
            core = c ^ kc
            for spot in range(4):
                first, second = spot % 2, spot // 2
                kx = jnp.where(core == 0, second, first)
                ky = jnp.where(core == 0, first, second)
                steps = [jnp.where(core == 0, i, (i % 2) * 2 + i // 2) for i in range(4)]
                spots = jnp.stack([((row ^ k) * 4 + (y ^ ky) * 2 + core) * 2 + kx for k in steps])
                arrays.append(jnp.take(flat, spots, axis=0))
        chunks.append(arrays)
    return chunks


def add_parts(parts):
    total = parts[0].astype(f32)
    for part in parts[1:]:
        total = total + part.astype(f32)
    return total


def halve(stack):
    pass_on = crossed(stack[2:], ROW, 0)
    pair = (stack[:2].astype(f32) + pass_on.astype(f32)).astype(bf16)
    return pair[0].astype(f32) + crossed(pair[1], ROW, 1).astype(f32)


def generic_inner(first, keep, send, c):
    parts = [keep, send, first[0], first[1]]
    by_x = [
        (parts[0], jnp.where(c == 0, parts[1], parts[2])),
        (jnp.where(c == 0, parts[2], parts[1]), parts[3]),
    ]
    planes = [add_parts([own, swap2(other, "cy")]).astype(bf16) for own, other in by_x]
    return [halve(plane) for plane in planes]


def generic_outer(row_sum, c):
    by_x = [
        (row_sum[0], jnp.where(c == 0, row_sum[1], row_sum[2])),
        (jnp.where(c == 0, row_sum[2], row_sum[1]), row_sum[3]),
    ]
    return [add_parts([own, swap2(other, "cy")]) for own, other in by_x]


def local(
    tokens, w_query, w_key, w_value, w_output, w_inner, w_outer,
    first_gain, first_shift, second_gain, second_shift, seq_lengths, out_grad,
):
    feat = tokens.shape[1]
    cols = tokens.shape[2]
    half = cols // 2
    head_width = w_query.shape[1]
    heads = head_width // HD
    two = lax.axis_size("dp") == 2
    row = lax.axis_index(ROW)
    group = lax.axis_index("dp")
    m = lax.axis_index("rm")
    z = lax.axis_index("rz")
    y = lax.axis_index("cy")
    c = lax.axis_index("cc")
    length = lax.dynamic_index_in_dim(seq_lengths[m], group, keepdims=False)
    own_start = (y * 2 + c) * cols + z * half
    info = jnp.stack([
        row, z, y, c, length - own_start, group if two else 0 * group, 0 * y, 0 * y,
    ]).astype(jnp.int32)

    def turn(blocks):
        pairs = blocks.reshape((2, 2) + blocks.shape[1:])
        return jnp.where(c == 0, pairs, pairs.swapaxes(0, 1)).reshape(blocks.shape)

    def to_slots(array):
        blocks = array.reshape(2, feat, 2, half).transpose(0, 2, 1, 3).reshape(4, feat, half)
        return turn(swap_by(blocks, row))

    def from_slots(parts):
        back = swap_by(turn(jnp.stack(parts)), row)
        return back.reshape(2, 2, feat, half).transpose(0, 2, 1, 3).reshape(2, feat, cols)

    token_blocks = to_slots(tokens)
    this_half, other_half = dp_halves(jnp.concatenate([after(w_query, token_blocks), w_key, w_value], axis=1), c)
    token_three = scatter_steps(token_blocks[:2], token_blocks[2:], ROW)
    x_own = jnp.stack(by_slot(token_three))
    other_columns = core_swap(other_half)
    norms = pack_norms(first_gain, first_shift, second_gain, second_shift)
    if two:
        block_a = jnp.concatenate([after(w_inner, token_blocks), pack_output(w_output, norms)], axis=0)
        pair_a = row_pair(block_a)
        block_b = w_outer.T
        near_b = crossed(after(block_b, token_blocks), ROW, 1)
    pieces = []
    for s in range(4):
        step = jnp.where(c == 0, s % 2, s // 2)
        pieces.append(jnp.where((z ^ step) == c, this_half, other_columns))
    mine = jnp.stack(by_slot(scatter_steps(jnp.stack(pieces[:2]), jnp.stack(pieces[2:]), ROW)))
    theirs = core_swap(mine)
    if two:
        row_a = row_rest(pair_a)
        x_own = after(x_own, pair_a)
    x_second = crossed(x_own, SQUARE, 1)
    xs = (x_own, x_second, crossed(jnp.stack([x_own, x_second]), SQUARE, 0))
    if two:
        xs = (after(x_own, row_a),) + xs[1:]

    starts = []
    for kc in range(2):
        core = c ^ kc
        for s in range(4):
            z_here = z ^ jnp.where(core == 0, s // 2, s % 2)
            y_here = y ^ jnp.where(core == 0, s % 2, s // 2)
            starts.append((y_here * 2 + core) * cols + z_here * half)
    positions = (jnp.stack(starts)[:, None] + jnp.arange(half, dtype=jnp.int32)[None, :]).reshape(-1)
    invalid = jnp.where(positions < length, 0.0, masked_score)
    bias = jnp.where(jnp.arange(HD)[:, None] == 0, invalid[None, :], 0.0).astype(bf16)
    frequency = 10000.0 ** (-2.0 * jnp.arange(HD // 2, dtype=f32) / HD)
    frequency = after(frequency, token_three[1])
    angles = frequency[:, None] * positions[: 4 * half].astype(f32)[None, :]
    cosine = jnp.repeat(jnp.cos(angles), 2, axis=0)
    sines = jnp.sin(angles)
    sine = jnp.stack([-sines, sines], axis=1).reshape(HD, 4 * half)

    q_rot, kv_own = qkv(info, xs, mine, theirs, cosine, sine)
    kv_other = core_swap(kv_own)
    out_b, log_b, low_b = attend(1, q_rot, kv_own, kv_other, bias)
    low_first = crossed(low_b, SQUARE, 0)
    cot_blocks = to_slots(after(out_grad, kv_own))
    cot_first = after(crossed(cot_blocks[2:], ROW, 0), low_b)
    cot_pass = jnp.stack([cot_blocks[1], cot_first[1]])
    cot_second = crossed(cot_pass, ROW, 1)
    cot_three = (cot_blocks[:2], cot_first, cot_second)
    q_second = after(q_rot, low_b, cot_pass)
    if two:
        near_a, far_a = crossed(row_a, PLANE, 1), crossed(row_a, PLANE, 0)
        both_a = crossed(after(near_a, kv_own), PLANE, 0)
        row_a_swapped = core_swap(row_a)
        far_a = after(far_a, low_b)
        both_a = after(both_a, low_b)
        pair_b = jnp.stack([block_b, after(near_b, xs[1])])
        row_b = row_rest(pair_b, low_b)
        q_second = after(q_second, row_a_swapped, far_a, row_b)
        near_b, far_b = crossed(row_b, PLANE, 1), crossed(row_b, PLANE, 0)
    out_a, log_a, low_a = attend(0, q_second, kv_own, kv_other, bias)
    low_pass = jnp.stack([low_a[1], after(low_first, low_a)[1]])
    low_second = crossed(low_pass, SQUARE, 1)
    attn_three = (low_a, low_first, low_second)
    if two:
        both_b = crossed(after(near_b, low_second, cot_second), PLANE, 0)
        chunk_a = [row_a, near_a, far_a, both_a, row_a_swapped] + [core_swap(after(part, low_a)) for part in (near_a, far_a, both_a)]
        chunk_b = core_copies([row_b, near_b, far_b, both_b], [(low_a,), (low_pass,), (low_pass,), (low_pass,)])
    else:
        chunk_a, chunk_b = gather_generic(w_output, w_inner, w_outer, norms, row, y, c)
    mixed_keep, mixed_send, e_keep, e_send, grad_one, attn_t, hidden_t, outer_t, branch_low, act_low, inner_low, norm_sums = middle(
        info, attn_three, x_own, cot_three, chunk_a, chunk_b
    )
    inner_args = (hidden_t, inner_low, attn_t, branch_low, norm_sums)
    outer_args = (outer_t, act_low)

    def tied(args, *earlier):
        return (after(args[0], *earlier),) + args[1:]

    def head_back(first, count, *earlier):
        return attend_back(
            first, count, after(q_rot, *earlier), kv_own, kv_other, bias, (out_a, out_b), (log_a, log_b), grads, cosine, sine
        )

    give_outer = grad_call("outer", "give", info, outer_args)
    got_outer = core_swap(give_outer)
    grads_first = after(crossed(e_send, SQUARE, 0), give_outer)
    grads_pass = jnp.stack([e_keep[1], grads_first[1]])
    grads = (e_keep, grads_first, crossed(grads_pass, SQUARE, 1))
    give_inner = grad_call("inner", "give", info, tied(inner_args, give_outer, grads_pass))
    got_inner = core_swap(give_inner)
    mixed_first = after(crossed(mixed_send, ROW, 0), give_inner)
    mixed_pass = jnp.stack([mixed_keep[1], mixed_first[1]])
    first_outer = grad_call("outer", "first", info, tied(outer_args, mixed_pass, grads[2]), got_outer)
    came_outer = crossed(first_outer, ROW, 0)
    first_inner = grad_call("inner", "first", info, tied(inner_args, first_outer, mixed_pass), got_inner)
    came_inner = crossed(first_inner, PLANE, 0) if two else jnp.zeros_like(first_inner)
    mixed_second = crossed(mixed_pass, ROW, 1)
    dq, own, send = head_back(0, heads, first_inner, mixed_second)
    came_outer = after(came_outer, dq)
    own = after(own, came_outer)
    dkv_got = core_swap(send)
    dx_keep, dx_send, proj = finish_dx(info, dq, own, dkv_got, mine, theirs, cosine, sine)
    dx_first = crossed(dx_send, SQUARE, 0)
    keep_outer, pass_outer = grad_call(
        "outer", "second", info, tied(outer_args, dx_keep), got_outer, after(came_outer, dx_keep)
    )
    keep_inner, pass_inner = grad_call(
        "inner", "second", info, tied(inner_args, keep_outer), got_inner, after(came_inner, keep_outer)
    )
    dx_first = after(dx_first, keep_inner)
    dx_pass = (dx_keep[1] + dx_first[1].astype(f32)).astype(bf16)
    dx_second = crossed(dx_pass, SQUARE, 1)
    keep, give = finish_dw(info, after(proj, dx_pass), xs)
    got = core_swap(give)
    dx_second = after(dx_second, give)
    d_x = add_parts([grad_one, dx_keep[0], dx_first[0], dx_second]).astype(bf16)
    d_x_first = crossed(d_x[2:], ROW, 0)
    by_row_step = keep + after(got, d_x).astype(f32)
    if two:
        here = group == c
        across = lax.ppermute(
            by_row_step.astype(bf16), ("dp", "cc"), [(2, 0), (1, 3)]
        )
    plane_parts = (keep_inner, after(crossed(pass_inner, PLANE, 1), by_row_step)) if two else None
    if two:
        plane_inner = add_parts(plane_parts).astype(bf16)
        pass_on_inner = crossed(plane_inner[2:], ROW, 0)
    row_outer = add_parts([keep_outer, after(crossed(pass_outer, ROW, 1), by_row_step)]).astype(bf16)
    if two:
        pass_on_outer = crossed(row_outer[2:], PLANE, 0)
        d_x_first = after(d_x_first, plane_inner, row_outer)
    d_x_pass = jnp.stack([d_x[1], d_x_first[1]])
    d_x_second = crossed(d_x_pass, ROW, 1)
    if two:
        summed = by_row_step + after(across, d_x_pass).astype(f32)
        active = [(g * 5 + 2 * side, g * 5 + 2 * (1 - side)) for g in range(2) for side in range(2)]
        passed_m = lax.ppermute(summed[2:].astype(bf16), ("dp", "rm", "cc"), active)
        pair_inner = (plane_inner[:2].astype(f32) + after(pass_on_inner, summed).astype(f32)).astype(bf16)
        last_inner = crossed(pair_inner[1], ROW, 1)
        pair_outer = (row_outer[:2].astype(f32) + after(pass_on_outer, pair_inner).astype(f32)).astype(bf16)
        last_outer = crossed(pair_outer[1], PLANE, 1)
        near_far = summed[:2] + after(passed_m, pair_outer).astype(f32)
        far_low = lax.ppermute(near_far[1].astype(bf16), ("dp", "rz", "cc"), active)
        d_x_second = after(d_x_second, near_far)
        d_input = from_slots(by_slot((d_x[:2], d_x_first, d_x_second))).astype(f32)
        near_sum = near_far[0]
        far_sum = after(far_low, d_x_second).astype(f32)
        kept = jnp.where(z == c, near_sum, far_sum)
        passed = core_swap(jnp.where(z == c, far_sum, near_sum).astype(bf16)).astype(f32)
        g_qkv = jnp.where(here, kept, passed)
        inner_sums = [pair_inner[0].astype(f32) + after(last_inner, far_sum).astype(f32)]
        outer_sums = [pair_outer[0].astype(f32) + after(last_outer, far_sum).astype(f32)]
    else:
        near_far = by_row_step[:2] + swap2(by_row_step[2:].astype(bf16), "rm").astype(f32)
        near_sum = near_far[0]
        far_sum = swap2(near_far[1].astype(bf16), "rz").astype(f32)
        kept = jnp.where(z == c, near_sum, far_sum)
        passed = core_swap(jnp.where(z == c, far_sum, near_sum).astype(bf16)).astype(f32)
        d_input = from_slots(by_slot((d_x[:2], d_x_first, d_x_second))).astype(f32)
        g_qkv = dp_sum(kept, passed, c)
        outer_sums = generic_outer(row_outer, c)
        inner_sums = generic_inner(first_inner, keep_inner, pass_inner, c)
    mixed_out = from_slots(by_slot((mixed_keep, mixed_first, mixed_second)))

    half_rows = feat // 2
    third = half_rows // 3
    g_outer = jnp.concatenate([part.T for part in outer_sums], axis=0)
    g_inner = jnp.concatenate([part[:half_rows] for part in inner_sums], axis=0)
    g_output = jnp.concatenate(
        [unpack_output(part[half_rows : half_rows + third], feat) for part in inner_sums], axis=0
    )
    g_norms = inner_sums[0][half_rows : half_rows + 4 * feat // (256 - feat), feat:256].reshape(4, feat)
    if not two:
        g_outer, g_inner, g_output = (
            lax.psum_scatter(g.astype(bf16), "dp", scatter_dimension=0, tiled=True).astype(f32)
            for g in (g_outer, g_inner, g_output)
        )
        g_norms = lax.psum(g_norms, "dp")

    return (
        mixed_out, d_input,
        g_qkv[:, :head_width], g_qkv[:, head_width : 2 * head_width], g_qkv[:, 2 * head_width :],
        g_output, g_inner, g_outer,
        g_norms[0], g_norms[1], g_norms[2], g_norms[3],
    )


def solution(mesh):
    shape = mesh.devices.shape
    fine = Mesh(mesh.devices.reshape(shape[0], 2, shape[1] // 2, 2, shape[2] // 2), EVERY)
    col = ("cy", "cc")
    acts = P(None, ROW, ("dp",) + col)
    by_row = P(ROW + ("dp",), col)
    by_col = P(col + ("dp",), ROW)
    vec = P(ROW)
    return jax.shard_map(
        local,
        mesh=fine,
        in_specs=(
            acts, by_row, by_row, by_row, by_col, by_row, by_col, vec, vec, vec, vec, P(), acts,
        ),
        out_specs=(
            acts, acts, by_row, by_row, by_row, by_col, by_row, by_col, vec, vec, vec, vec,
        ),
        check_vma=False,
    )
```

```python
import functools

import jax
import jax.numpy as jnp
from jax import lax
from jax.experimental import pallas as pl
from jax.experimental.pallas import tpu as pltpu
from jax.sharding import Mesh, PartitionSpec as P

HD = 64
EVERY = ("dp", "rm", "rz", "cy", "cc")
GROUP = ("rm", "rz", "cy", "cc")
ROW = ("rm", "rz")
SQUARE = ("rz", "cy")
bf16=jnp.bfloat16; f32=jnp.float32
LOG2E=1.4426950408889634
LN2=0.6931471805599453
masked_score=-1e30

def mm(a,b,dims=((1,),(0,))):
    return lax.dot_general(a,b,(dims,((),())),preferred_element_type=f32)
NT=((1,),(1,))

def pair_turn(values, cosine, signed_sine):
    shape = values.shape
    v3 = values.reshape(shape[0]//8, 8, shape[1])
    up = pltpu.roll(v3, 7, 1); down = pltpu.roll(v3, 1, 1)
    even = (lax.broadcasted_iota(jnp.int32, v3.shape, 1) % 2) == 0
    other = jnp.where(even, up, down).reshape(shape)
    return values*cosine + other*signed_sine

KB=1024
QB=2
def one_row(shape, dtype, value=1.0):
    return jnp.where(lax.broadcasted_iota(jnp.int32, shape, 0)==0, value, 0.0).astype(dtype)

def attend_kernel(q_ref, ko_ref, vo_ref, kx_ref, vx_ref, bias_ref, o_ref, lse_ref, low_ref, kaug, vall):
    span=ko_ref.shape[1]
    for part,(kr,vr) in enumerate(((ko_ref,vo_ref),(kx_ref,vx_ref))):
        aug=jnp.concatenate([kr[...], bias_ref[:, part*span:(part+1)*span]],axis=0)
        kaug[part*span:(part+1)*span,:]=aug.T
        vall[:, part*span:(part+1)*span]=vr[...]
    n=q_ref.shape[1]
    qaug=jnp.concatenate([q_ref[...], one_row((HD,n),bf16)],axis=0)
    top=jnp.full((1,n),-3e38,f32); total=jnp.zeros((1,n),f32); acc=jnp.zeros((HD,n),f32)
    s=mm(kaug[0:KB,:],qaug)
    for kb in range(0,2*span,KB):
        following=mm(kaug[kb+KB:kb+2*KB,:],qaug) if kb+KB<2*span else None
        new=jnp.maximum(top,jnp.max(s,axis=0,keepdims=True))
        alpha=jnp.exp2(top-new)
        p=jnp.exp2(s-new)
        total=total*alpha+jnp.sum(p,axis=0,keepdims=True)
        acc=acc*alpha+mm(vall[:,kb:kb+KB],p.astype(bf16))
        top=new
        s=following
    out=acc/total
    o_ref[...]=out
    lse_ref[0]=top+jnp.log2(total)
    low=out.astype(bf16)
    for b in range(2):
        low_ref[b]=low[:,b*(n//2):(b+1)*(n//2)]

def attend(part,q,kv,kvx,bias):
    width,n4=q.shape; heads=width//HD; n=n4//2; span=kv.shape[1]
    kspec=pl.BlockSpec((HD,span),lambda h:(h,0)); vspec=pl.BlockSpec((HD,span),lambda h:(heads+h,0))
    return pl.pallas_call(attend_kernel,grid=(heads,),
        in_specs=[pl.BlockSpec((HD,n),lambda h:(h,part)),kspec,vspec,kspec,vspec,pl.BlockSpec((HD,2*span),lambda h:(0,0))],
        out_specs=[pl.BlockSpec((HD,n),lambda h:(h,0)),pl.BlockSpec((1,1,n),lambda h:(h,0,0)),pl.BlockSpec((2,HD,n//2),lambda h:(0,h,0))],
        out_shape=[jax.ShapeDtypeStruct((width,n),f32),jax.ShapeDtypeStruct((heads,1,n),f32),jax.ShapeDtypeStruct((2,width,n//2),bf16)],
        scratch_shapes=[pltpu.VMEM((2*span,2*HD),bf16),pltpu.VMEM((HD,2*span),bf16)],
        cost_estimate=pl.CostEstimate(flops=int(6.0*(2*width*n4//HD*2*span*256))+1,bytes_accessed=int(6.0*(2*n4*2*span))+1,transcendentals=int(6.0*(heads*n*2*span))+1),
        name="attend")(q,kv,kv,kvx,kvx,bias)

BKB=512
def attend_back_kernel(q_ref, ko_ref, vo_ref, kx_ref, vx_ref, bias_ref, oa_ref, ob_ref, lsea_ref, lseb_ref, g0,g1,g2,g3, cos_ref, sin_ref,
                       dq_ref, own_ref, give_ref, kaug, vtm, kall, acc):
    qb=pl.program_id(1)
    span=ko_ref.shape[1]; n=q_ref.shape[1]
    @pl.when(qb==0)
    def _():
        for part,(kr,vr) in enumerate(((ko_ref,vo_ref),(kx_ref,vx_ref))):
            sl=slice(part*span,(part+1)*span)
            kaug[sl,:]=jnp.concatenate([kr[...], bias_ref[:, sl]],axis=0).T
            vtm[sl,:]=jnp.concatenate([vr[...], jnp.zeros((HD,span),bf16)],axis=0).T
            kall[:,sl]=kr[...]
        acc[...]=jnp.zeros_like(acc)
    q=q_ref[...]
    zeros=jnp.zeros((HD,n),bf16)
    qaug=jnp.concatenate([q, one_row((HD,n),bf16)],axis=0)
    g=jnp.concatenate([jnp.where(qb==0,g0[...],g2[...]),jnp.where(qb==0,g1[...],g3[...])],axis=1)
    o=jnp.where(qb==0,oa_ref[...],ob_ref[...])
    qpad=jnp.concatenate([q,zeros],axis=0).T
    gpad=jnp.concatenate([zeros,g],axis=0).T
    gaug=jnp.concatenate([g,zeros],axis=0)
    delta=jnp.sum(g.astype(f32)*o,axis=0,keepdims=True)
    lse=jnp.where(qb==0,lsea_ref[0],lseb_ref[0])
    dq=jnp.zeros((HD,n),f32)
    s=mm(kaug[0:BKB,:],qaug); dp=mm(vtm[0:BKB,:],gaug)
    for kb in range(0,2*span,BKB):
        last=kb+BKB>=2*span
        s_next=None if last else mm(kaug[kb+BKB:kb+2*BKB,:],qaug)
        dp_next=None if last else mm(vtm[kb+BKB:kb+2*BKB,:],gaug)
        p=jnp.exp2(s-lse)
        ds=(p*(dp-delta)).astype(bf16)
        dq=dq+mm(kall[:,kb:kb+BKB],ds)
        acc[kb:kb+BKB,:]=acc[kb:kb+BKB,:]+mm(ds,qpad)+mm(p.astype(bf16),gpad)
        s=s_next; dp=dp_next
    dq_ref[...]=pair_turn(dq*(HD**-0.5),cos_ref[...],-sin_ref[...]).astype(bf16)
    @pl.when(qb==4//QB-1)
    def _():
        own_ref[...]=acc[:span,:]
        give_ref[...]=acc[span:,:].astype(bf16)

def attend_back(first,count,q,kv,kvx,bias,os,lses,grads,cos,sin):
    width,n4=q.shape; heads=width//HD; n=n4//4*QB; span=kv.shape[1]
    kspec=pl.BlockSpec((HD,span),lambda h,b:(first+h,0)); vspec=pl.BlockSpec((HD,span),lambda h,b:(heads+first+h,0))
    gspec=lambda i:pl.BlockSpec((None,HD,n4//4),lambda h,b:(i,first+h,0)); tb=pl.BlockSpec((HD,n),lambda h,b:(0,b))
    dspec=pl.BlockSpec((None,span,2*HD),lambda h,b:(h,0,0)); ospec=pl.BlockSpec((HD,n),lambda h,b:(first+h,0)); lspec=pl.BlockSpec((1,1,n),lambda h,b:(first+h,0,0))
    return pl.pallas_call(attend_back_kernel,grid=(count,4//QB),
        in_specs=[pl.BlockSpec((HD,n),lambda h,b:(first+h,b)),kspec,vspec,kspec,vspec,pl.BlockSpec((HD,2*span),lambda h,b:(0,0)),ospec,ospec,lspec,lspec,gspec(0),gspec(0),gspec(0),gspec(1),tb,tb],
        out_specs=[pl.BlockSpec((HD,n),lambda h,b:(h,b)),dspec,dspec],
        out_shape=[jax.ShapeDtypeStruct((count*HD,n4),bf16),jax.ShapeDtypeStruct((count,span,2*HD),f32),jax.ShapeDtypeStruct((count,span,2*HD),bf16)],
        scratch_shapes=[pltpu.VMEM((2*span,2*HD),bf16),pltpu.VMEM((2*span,2*HD),bf16),pltpu.VMEM((HD,2*span),bf16),pltpu.VMEM((2*span,2*HD),f32)],
        cost_estimate=pl.CostEstimate(flops=int(6.0*(count*10*n4*2*span*256))+1,bytes_accessed=int(6.0*(count*4*n4*2*span))+1,transcendentals=int(6.0*(count*n4*2*span))+1),
        name="attend_back")(q,kv,kv,kvx,kvx,bias,*os,*lses,grads[0],grads[2],grads[1],grads[2],cos,sin)
def xor(a,b):
    return lax.bitwise_xor(jnp.asarray(a,jnp.int32),jnp.asarray(b,jnp.int32))

def rows_at(index,size,align):
    return pl.ds(pl.multiple_of(index*size,align),size)

def row_step(core,slot):
    return jnp.where(core==0,slot,(slot%2)*2+slot//2)

def z_step(core,slot):
    return jnp.where(core==0,slot//2,slot%2)

def y_step(core,slot):
    return jnp.where(core==0,slot%2,slot//2)

def slots(three):
    keep,first,second=three
    return (keep.at[0],second.at[0],first.at[0],second.at[1])

def place_qkv_weights(info, mine_ref, theirs_ref, w_s):
    row=info[0]; c=info[3]
    half=mine_ref.shape[1]
    for r in range(4):
        k=xor(r,row)
        w_s[pl.ds(pl.multiple_of((2*r+c)*half,32),half),:]=mine_ref[row_step(c,k)]
        w_s[pl.ds(pl.multiple_of((2*r+1-c)*half,32),half),:]=theirs_ref[row_step(1-c,k)]

def place_tokens(info, x_ref, slot, x_s):
    feat=x_ref.shape[1]; c=info[3]; base=xor(info[0],z_step(c,slot))
    for r in range(4):
        x_s[r*feat:(r+1)*feat,:]=x_ref[row_step(c,xor(r,base))]

def token_refs(own, second, others):
    return (own, second, others.at[0], others.at[1])

def qkv_kernel(info, xa,xb,xc, mine_ref, theirs_ref, cos_ref, sin_ref, q_ref, kv_ref, w_s, wt_s, x_s):
    place_qkv_weights(info,mine_ref,theirs_ref,w_s)
    wt_s[...]=w_s[...].T
    hw=q_ref.shape[0]; n=xa.shape[2]
    for k,xr in enumerate(token_refs(xa,xb,xc)):
        place_tokens(info,xr,k,x_s)
        out=mm(wt_s[...],x_s[...])
        sl=slice(k*n,(k+1)*n)
        cos=cos_ref[:,sl]; sin=sin_ref[:,sl]
        for h in range(2*hw//HD):
            turned=pair_turn(out[h*HD:(h+1)*HD],cos,sin)
            if h*HD<hw: q_ref[h*HD:(h+1)*HD,sl]=(turned*(HD**-0.5*LOG2E)).astype(bf16)
            else: kv_ref[h*HD-hw:(h+1)*HD-hw,sl]=turned.astype(bf16)
        kv_ref[hw:,sl]=out[2*hw:].astype(bf16)

VM=pl.BlockSpec(memory_space=pltpu.VMEM)
SM=pl.BlockSpec(memory_space=pltpu.SMEM)
HB=pl.BlockSpec(memory_space=pl.ANY)

def qkv(info,xs,mine,theirs,cos,sin):
    _,feat,n=xs[0].shape; w3=mine.shape[2]; hw=w3//3; width=4*feat
    return pl.pallas_call(qkv_kernel,in_specs=[SM]+[VM]*7,out_specs=[VM,VM],
        out_shape=[jax.ShapeDtypeStruct((hw,4*n),bf16),jax.ShapeDtypeStruct((2*hw,4*n),bf16)],
        scratch_shapes=[pltpu.VMEM((width,w3),bf16),pltpu.VMEM((w3,width),bf16),pltpu.VMEM((width,n),bf16)],
        name="qkv")(info,*xs,mine,theirs,cos,sin)

def finish_dx_kernel(info, *refs):
    (q_ref,own_ref,got_ref,mine_ref,theirs_ref,cos_ref,sin_ref,keep_ref,send_ref,p_ref,w_s)=refs
    hw=q_ref.shape[0]; n=keep_ref.shape[3]; feat=keep_ref.shape[2]; c=info[3]
    place_qkv_weights(info,mine_ref,theirs_ref,w_s)
    p_ref[0:hw,:]=q_ref[...]
    for h in range(hw//HD):
        t=(own_ref[h]+got_ref[h].astype(f32)).T
        p_ref[hw+h*HD:hw+(h+1)*HD,:]=pair_turn(t[:HD]*LN2,cos_ref[...],-sin_ref[...]).astype(bf16)
        p_ref[2*hw+h*HD:2*hw+(h+1)*HD,:]=t[HD:].astype(bf16)
    for k,dr in ((3,send_ref),(2,send_ref),(1,keep_ref),(0,keep_ref)):
        sl=slice(k*n,(k+1)*n)
        base=xor(info[0],z_step(c,k))
        for r in range(4):
            dr[k%2,row_step(c,xor(r,base))]=mm(w_s[r*feat:(r+1)*feat,:],p_ref[:,sl]).astype(dr.dtype)

def finish_dx(info,dq,own,got,mine,theirs,cos,sin):
    w3=mine.shape[2]; half=mine.shape[1]; feat=2*half; width=4*feat; n=dq.shape[1]//4
    S=jax.ShapeDtypeStruct
    return pl.pallas_call(finish_dx_kernel,in_specs=[SM]+[VM]*7,out_specs=[VM]*3,
        out_shape=[S((2,4,feat,n),f32),S((2,4,feat,n),bf16),S((w3,4*n),bf16)],
        scratch_shapes=[pltpu.VMEM((width,w3),bf16)],
        cost_estimate=pl.CostEstimate(flops=int(0.0*(8*width*w3*n))+1,bytes_accessed=int(0.0*(8*width*n*4))+1,transcendentals=int(0.0*(0))+1),
        name="finish_dx")(info,dq,own,got,mine,theirs,cos,sin)

def finish_dw_kernel(info, p_ref, xa,xb,xc, keep_ref, give_ref, x_s, g_s):
    n=xa.shape[2]; half=keep_ref.shape[1]
    for k,xr in enumerate(token_refs(xa,xb,xc)):
        place_tokens(info,xr,k,x_s.at[:,k*n:(k+1)*n])
    g_s[...]=mm(x_s[...],p_ref[...],NT)
    c=info[3]; row=info[0]
    for r in range(4):
        mine_rows=pl.ds(pl.multiple_of((2*r+c)*half,32),half); their_rows=pl.ds(pl.multiple_of((2*r+1-c)*half,32),half)
        keep_ref[xor(r,row)]=g_s[mine_rows,:]
        give_ref[xor(r,row)]=g_s[their_rows,:].astype(bf16)

def finish_dw(info,proj,xs):
    _,feat,n=xs[0].shape; w3=proj.shape[0]; width=4*feat; half=feat//2
    return pl.pallas_call(finish_dw_kernel,in_specs=[SM]+[VM]*4,out_specs=[VM]*2,
        out_shape=[jax.ShapeDtypeStruct((4,half,w3),f32),jax.ShapeDtypeStruct((4,half,w3),bf16)],
        scratch_shapes=[pltpu.VMEM((width,4*n),bf16),pltpu.VMEM((width,w3),f32)],
        cost_estimate=pl.CostEstimate(flops=int(6.0*(8*width*w3*n))+1,bytes_accessed=int(6.0*(8*width*n*2))+1,transcendentals=int(6.0*(0))+1),
        name="finish_dw")(info,proj,*xs)

def middle_kernel(info, a0,a1,a2, x_ref, c0,c1,c2, *refs):
    chunk_a=refs[:8]; chunk_b=refs[8:16]
    (mixk_ref, mixs_ref, ek_ref, es_ref, g1_ref, attnT_ref, hidT_ref, outT_ref, bl_ref, act_ref, il_ref, norm_ref,
                  win, woT, wo, wpk, gp_s, t_s, f_s, sems)=refs[16:]
    row=info[0]; z=info[1]; y=info[2]; c=info[3]; group=info[5]
    feat=a0.shape[1]; n=a0.shape[2]; width=4*feat; ffc=chunk_a[0].shape[2]; half=feat//2; fh=ffc//2; third=half//3
    def go(src,dst,s): pltpu.make_async_copy(src,dst,sems.at[s]).start()
    def each(chunk):
        for kc in range(2):
            core=xor(c,kc)
            for spot,ref in enumerate(chunk[4*kc:4*kc+4]):
                first,second=spot%2,spot//2
                kx=jnp.where(core==0,second,first); ky=jnp.where(core==0,first,second)
                g=xor(group,kx); col=xor(y,ky)*2+core
                for i in range(4):
                    step=row_step(core,i)
                    yield ref.at[i],xor(row,step),g,col,kc+spot
    for ref,r,g,col,_ in each(chunk_a):
        go(ref.at[half:half+third,:],wpk.at[r,col*2+g],0)
    for ref,r,g,col,_ in each(chunk_a):
        go(ref.at[0:half,:],win.at[pl.ds(pl.multiple_of(r*feat+g*half,16),half),pl.ds(pl.multiple_of(col*ffc,128),ffc)],1)
    for ref,r,g,col,_ in each(chunk_b):
        go(ref,woT.at[pl.ds(pl.multiple_of(r*feat,64),feat),pl.ds(pl.multiple_of((col*2+g)*fh,128),fh)],2)
    def group_of(s):
        return xor(y,y_step(c,s))*2+xor(z,z_step(c,s))
    def row_of(s):
        return xor(row,row_step(c,s))
    for s,ar in enumerate(slots((a0,a1,a2))):
        attnT_ref[rows_at(group_of(s),feat,64),:]=ar[...]
    for s in range(4):
        t_s[rows_at(row_of(s),feat,64),:]=x_ref[s]
    attn=attnT_ref[...].T
    x=t_s[...].T.astype(f32)
    pltpu.make_async_copy(wpk,wpk,sems.at[0]).wait()
    for r in range(4):
        for q in range(8):
            for j in range(3):
                wo[r,q*half+j*third:q*half+(j+1)*third,:]=wpk[r,q,:,j*256:(j+1)*256]
    wide=256-feat; pieces=feat//wide
    addends=[sum(wpk[r,0,0:16,j*256+feat:(j+1)*256].astype(f32) for j in range(3)) for r in range(4)]
    def vector(which):
        return jnp.concatenate([addends[r][which*pieces+t:which*pieces+t+1] for r in range(4) for t in range(pieces)],axis=1)
    gain1=vector(0); shift1=vector(1); gain2=vector(2); shift2=vector(3)
    branch=jnp.concatenate([mm(attn,wo[r])[:,:feat] for r in range(4)],axis=1)
    def stats(v):
        mean=jnp.sum(v,axis=1,keepdims=True)*(1.0/width)
        var=jnp.sum(v*v,axis=1,keepdims=True)*(1.0/width)-mean*mean
        inv=lax.rsqrt(var+1e-5)
        return (v-mean)*inv,inv
    cent1,inv1=stats(x+branch)
    hidden=cent1*gain1+shift1
    hid=hidden.astype(bf16)
    hidT_ref[...]=hid.T
    pltpu.make_async_copy(win,win,sems.at[1]).wait()
    pltpu.make_async_copy(woT,woT,sems.at[2]).wait()
    f_s[...]=jnp.zeros_like(f_s)
    bw=2*ffc
    def forward(j,carry):
        sl=pl.ds(pl.multiple_of(j*bw,128),bw)
        inner=mm(hid,win[:,sl])
        cdf=0.5+0.5*lax.erf(inner*0.7071067811865476)
        act=(inner*cdf).astype(bf16)
        gp_s[:,sl]=cdf+inner*(jnp.exp(inner*inner*-0.5)*0.3989422804014327)
        act_ref[:,sl]=act
        f_s[...]+=mm(act,woT[:,sl],NT)
        return carry
    lax.fori_loop(0,2,forward,0)
    cent2,inv2=stats(hidden+f_s[...])
    t_s[...]=(cent2*gain2+shift2).astype(bf16).T
    for s in range(4):
        (mixk_ref,mixs_ref)[s//2][s%2]=t_s[rows_at(row_of(s),feat,64),:]
    for s,cr in enumerate(slots((c0,c1,c2))):
        t_s[rows_at(row_of(s),feat,64),:]=cr[...]
    valid=(lax.broadcasted_iota(jnp.int32,(n,1),0)<info[4]).astype(f32)
    cot=t_s[...].T.astype(f32)*valid
    sums2=(jnp.sum(cot*cent2,axis=0,keepdims=True),jnp.sum(cot,axis=0,keepdims=True))
    def back(e,cent,inv):
        first=jnp.sum(e,axis=1,keepdims=True)*(1.0/width)
        second=jnp.sum(e*cent,axis=1,keepdims=True)*(1.0/width)
        return inv*(e-first-cent*second)
    grad2=back(cot*gain2,cent2,inv2)
    low=grad2.astype(bf16)
    outT_ref[...]=low.T
    f_s[...]=grad2
    def backward(j,carry):
        sl=pl.ds(pl.multiple_of(j*bw,128),bw)
        il=(mm(low,woT[:,sl])*gp_s[:,sl]).astype(bf16)
        il_ref[:,sl]=il
        f_s[...]+=mm(il,win[:,sl],NT)
        return carry
    lax.fori_loop(0,2,backward,0)
    gh=f_s[...]
    sums=jnp.concatenate((jnp.sum(gh*cent1,axis=0,keepdims=True),jnp.sum(gh,axis=0,keepdims=True))+sums2+(jnp.zeros((4,width),f32),),axis=0)
    for r in range(4):
        lines=[sums[i:i+1,r*feat+t*wide:r*feat+(t+1)*wide] for i in range(4) for t in range(pieces)]
        lines=jnp.concatenate(lines+[jnp.zeros((third-4*pieces,wide),f32)],axis=0)
        norm_ref[r]=jnp.concatenate([jnp.zeros((third,feat),f32),lines],axis=1)
    grad1=back(gh*gain1,cent1,inv1)
    bl=grad1.astype(bf16)
    da=jnp.zeros((width,n),f32)
    for r in range(4):
        piece=jnp.concatenate([bl[:,r*feat:(r+1)*feat],jnp.zeros((n,wide),bf16)],axis=1)
        bl_ref[r]=piece
        da=da+mm(wo[r],piece,NT)
    t_s[...]=da.astype(bf16)
    for s in range(4):
        (ek_ref,es_ref)[s//2][s%2]=t_s[rows_at(group_of(s),feat,64),:]
    f2=grad1.T
    for r in range(4):
        g1_ref[row_step(c,xor(r,row))]=f2[r*feat:(r+1)*feat]

def middle(info,attn_parts,x_own,cot_parts,chunk_a,chunk_b):
    _,feat,n=attn_parts[0].shape; width=4*feat; ff=4*chunk_a[0].shape[2]
    S=jax.ShapeDtypeStruct
    return pl.pallas_call(middle_kernel,in_specs=[SM]+[VM]*7+[HB]*16,out_specs=[VM]*12,
        out_shape=[S((2,feat,n),bf16)]*4+[S((4,feat,n),f32),S((width,n),bf16),S((width,n),bf16),S((width,n),bf16),
                   S((4,n,256),bf16),S((n,ff),bf16),S((n,ff),bf16),S((4,feat//6,256),f32)],
        scratch_shapes=[pltpu.VMEM((width,ff),bf16),pltpu.VMEM((width,ff),bf16),pltpu.VMEM((4,width,256),bf16),pltpu.VMEM((4,8,feat//6,width),bf16),
                        pltpu.VMEM((n,ff),f32),pltpu.VMEM((width,n),bf16),pltpu.VMEM((n,width),f32),pltpu.SemaphoreType.DMA((4,))],
        compiler_params=pltpu.CompilerParams(vmem_limit_bytes=56*1024*1024),
        cost_estimate=pl.CostEstimate(flops=int(6.0*(12*n*width*ff*2))+1,bytes_accessed=int(6.0*(24*width*ff))+1,transcendentals=int(6.0*(2*n*ff))+1),
        name="middle")(info,*attn_parts,x_own,*cot_parts,*chunk_a,*chunk_b)

def plane_target(info,core,slot):
    kx=jnp.where(core==0,slot//2,slot%2); ky=jnp.where(core==0,slot%2,slot//2)
    return xor(info[5],kx),xor(info[2],ky)*2+core

def target(info,which,a,b):
    core=xor(info[3],which)
    return (core,)+plane_target(info,core,2*a+b)

def outer_blocks(info,which,a,b,refs,put):
    outT_ref,act_near,act_far=refs
    core=xor(info[3],which)
    half=outT_ref.shape[0]//8; fh=act_near.shape[1]//2
    rows=outT_ref[rows_at(xor(info[0],row_step(core,2*a+b)),2*half,64),:]
    for ky,act_ref in enumerate((act_near,act_far)):
        value=mm(rows,act_ref[...])
        for g in range(2):
            kx=xor(g,info[5])
            slot=jnp.where(core==0,2*kx+ky,2*ky+kx)
            put(slot,slice(0,2*half),slice(0,fh),value[:,g*fh:(g+1)*fh])

def inner_blocks(info,which,a,b,refs,put):
    hidT_ref,il_ref,attnT_ref,bl_ref,norm_ref=refs
    core,g,col=target(info,which,a,b)
    half=hidT_ref.shape[0]//8; third=half//3
    rows=[xor(info[0],row_step(core,s)) for s in range(4)]
    lhs=jnp.concatenate([hidT_ref[rows_at(r*2+g,half,32),:] for r in rows],axis=0)
    value=mm(lhs,il_ref[...])
    heads=attnT_ref[rows_at(col*2+g,half,32),:]
    for s,r in enumerate(rows):
        put(s,slice(0,half),slice(None),value[s*half:(s+1)*half])
        outs=mm(heads,bl_ref[r])
        for j in range(3):
            piece=outs[j*third:(j+1)*third]
            if j==0: piece=piece+norm_ref[r]
            put(s,slice(half,half+third),slice(j*256,(j+1)*256),piece)

def give_kernel(blocks,info,*refs):
    out=refs[-1]
    def put(s,rows,lanes,value): out[0,0,s,rows,lanes]=value.astype(bf16)
    blocks(info,1,pl.program_id(0),pl.program_id(1),refs[:-1],put)

def first_kernel(blocks,info,*refs):
    got,out=refs[-2:]
    def put(s,rows,lanes,value): out[0,s,rows,lanes]=(value+got[0,0,s,rows,lanes].astype(f32)).astype(bf16)
    blocks(info,0,1,pl.program_id(0),refs[:-2],put)

def second_kernel(blocks,info,*refs):
    got,came,keep,send=refs[-4:]
    for b,out in ((0,keep),(1,send)):
        def put(s,rows,lanes,value):
            out[s,rows,lanes]=(value+got[0,0,s,rows,lanes].astype(f32)+came[0,s,rows,lanes].astype(f32)).astype(bf16)
        @pl.when(pl.program_id(0)==b)
        def _(): blocks(info,0,0,b,refs[:-4],put)

def grad_call(kind,stage,info,args,got=None,came=None):
    S=jax.ShapeDtypeStruct
    width,n=args[0].shape; ffc=args[1].shape[1]//4; half=width//8
    a={"give":None,"first":1,"second":0}[stage]; which=1 if stage=="give" else 0
    def at(index):
        if stage=="give": return lambda i,j,s:index(i,j,s)
        return lambda j,s:index(a,j,s)
    whole=pl.BlockSpec((width,n),at(lambda i,j,s:(0,0)))
    if kind=="inner":
        blocks,rows,lanes=inner_blocks,half+half//3,ffc
        specs=[whole,pl.BlockSpec((n,ffc),at(lambda i,j,s:(0,target(s,which,i,j)[2]))),whole,
               pl.BlockSpec((4,n,256),at(lambda i,j,s:(0,0,0))),pl.BlockSpec((4,half//3,256),at(lambda i,j,s:(0,0,0)))]
    else:
        blocks,rows,lanes=outer_blocks,2*half,ffc//2
        args=(args[0],args[1],args[1])
        def column(ky): return at(lambda i,j,s:(0,xor(s[2],ky)*2+xor(s[3],which)))
        specs=[whole,pl.BlockSpec((n,ffc),column(0)),pl.BlockSpec((n,ffc),column(1))]
    weight={"give":4,"first":2,"second":0}[stage]
    cost=pl.CostEstimate(flops=int(6.0*(weight*width*n*ffc))+1,bytes_accessed=int(6.0*(4*weight*rows*ffc))+1,transcendentals=int(6.0*(0))+1)
    name=kind+"_"+stage
    five=(1,1,4,rows,lanes)
    if stage=="give":
        return pl.pallas_call(functools.partial(give_kernel,blocks),
            grid_spec=pltpu.PrefetchScalarGridSpec(num_scalar_prefetch=1,grid=(2,2),in_specs=specs,out_specs=pl.BlockSpec(five,lambda i,j,s:(i,j,0,0,0))),
            out_shape=S((2,2,4,rows,lanes),bf16),cost_estimate=cost,name=name)(info,*args)
    got_spec=pl.BlockSpec(five,lambda j,s:(a,j,0,0,0)); one=pl.BlockSpec((1,4,rows,lanes),lambda j,s:(j,0,0,0))
    if stage=="first":
        return pl.pallas_call(functools.partial(first_kernel,blocks),
            grid_spec=pltpu.PrefetchScalarGridSpec(num_scalar_prefetch=1,grid=(2,),in_specs=specs+[got_spec],out_specs=one),
            out_shape=S((2,4,rows,lanes),bf16),cost_estimate=cost,name=name)(info,*args,got)
    full=pl.BlockSpec((4,rows,lanes),lambda j,s:(0,0,0))
    return pl.pallas_call(functools.partial(second_kernel,blocks),
        grid_spec=pltpu.PrefetchScalarGridSpec(num_scalar_prefetch=1,grid=(2,),in_specs=specs+[got_spec,one],out_specs=[full,full]),
        out_shape=[S((4,rows,lanes),bf16)]*2,cost_estimate=cost,name=name)(info,*args,got,came)

def core_swap(value):
    return lax.ppermute(value, "cc", [(0, 1), (1, 0)])


def swap_by(blocks, index):
    pairs = blocks.reshape((2, 2) + blocks.shape[1:])
    pairs = jnp.where((index // 2) == 1, pairs[::-1], pairs)
    pairs = jnp.where((index % 2) == 1, pairs[:, ::-1], pairs)
    return pairs.reshape(blocks.shape)


def dp_halves(value, c):
    if lax.axis_size("dp") != 2:
        whole = lax.all_gather(value, "dp", axis=0, tiled=True)
        halves = whole.reshape((2, whole.shape[0] // 2) + whole.shape[1:])
        return jnp.where(c == 0, halves[0], halves[1]), jnp.where(c == 0, halves[1], halves[0])
    other = swap2(value, "dp")
    same = lax.axis_index("dp") == c
    return jnp.where(same, value, other), jnp.where(same, other, value)


def dp_sum(this_half, other_half, c):
    whole = jnp.concatenate(
        [jnp.where(c == 0, this_half, other_half), jnp.where(c == 0, other_half, this_half)], axis=0
    )
    return lax.psum_scatter(whole.astype(bf16), "dp", scatter_dimension=0, tiled=True).astype(f32)


def pack_output(part, norms):
    third = part.shape[0] // 3
    wide = 256 - part.shape[1]
    addends = jnp.pad(norms.reshape(3, -1, wide), ((0, 0), (0, third - norms.shape[1] // wide), (0, 0)))
    pieces = []
    for j in range(3):
        pieces += [part[j * third : (j + 1) * third], addends[j]]
    return jnp.concatenate(pieces, axis=1)


def unpack_output(packed, feat):
    return jnp.concatenate([packed[:, j * 256 : j * 256 + feat] for j in range(3)], axis=0)


def pack_norms(first_gain, first_shift, second_gain, second_shift):
    line = jnp.concatenate([first_gain, first_shift, second_gain, second_shift])
    high = lax.reduce_precision(line, 8, 7)
    middle_part = lax.reduce_precision(line - high, 8, 7)
    return jnp.stack([high, middle_part, line - high - middle_part]).astype(bf16)


def after(value, *earlier):
    return lax.optimization_barrier((value,) + earlier)[0]


def swap2(value, axis):
    return lax.ppermute(value, axis, [(0, 1), (1, 0)])


def crossed(value, axes, first):
    pairs = []
    for u in range(2):
        for v in range(2):
            for core in range(2):
                along = first ^ core
                pairs.append(((u * 2 + v) * 2 + core, ((u ^ (1 - along)) * 2 + (v ^ along)) * 2 + core))
    return lax.ppermute(value, axes + ("cc",), pairs)


PLANE = ("dp", "cy")


def scatter_steps(keep, send, axes, *between):
    first = after(crossed(send, axes, 0), *between)
    second = crossed(jnp.stack([keep[1], first[1]]), axes, 1)
    return keep, first, second


def by_slot(three):
    keep, first, second = three
    return [keep[0], second[0], first[0], second[1]]


def row_pair(block, *between):
    return jnp.stack([block, after(crossed(block, ROW, 1), *between)])


def row_rest(pair, *between):
    return jnp.concatenate([pair, after(crossed(pair, ROW, 0), *between)], axis=0)


def core_copies(arrays, ties):
    return arrays + [core_swap(after(array, *tie)) for array, tie in zip(arrays, ties)]


def gather_generic(w_output, w_inner, w_outer, norms, row, y, c):
    inner, outer, output = (lax.all_gather(w, "dp", axis=0, tiled=True) for w in (w_inner, w_outer, w_output))
    chunks = []
    for which in range(2):
        halves = []
        for g in range(2):
            parts = [w.reshape((2, w.shape[0] // 2) + w.shape[1:])[g] for w in (inner, outer, output)]
            if which == 0:
                halves.append(jnp.concatenate([parts[0], pack_output(parts[2], norms)], axis=0))
            else:
                halves.append(parts[1].T)
        whole = lax.all_gather(jnp.stack(halves), GROUP)
        flat = whole.reshape((-1,) + whole.shape[2:])
        arrays = []
        for kc in range(2):
            core = c ^ kc
            for spot in range(4):
                first, second = spot % 2, spot // 2
                kx = jnp.where(core == 0, second, first)
                ky = jnp.where(core == 0, first, second)
                steps = [jnp.where(core == 0, i, (i % 2) * 2 + i // 2) for i in range(4)]
                spots = jnp.stack([((row ^ k) * 4 + (y ^ ky) * 2 + core) * 2 + kx for k in steps])
                arrays.append(jnp.take(flat, spots, axis=0))
        chunks.append(arrays)
    return chunks


def add_parts(parts):
    total = parts[0].astype(f32)
    for part in parts[1:]:
        total = total + part.astype(f32)
    return total


def halve(stack):
    pass_on = crossed(stack[2:], ROW, 0)
    pair = (stack[:2].astype(f32) + pass_on.astype(f32)).astype(bf16)
    return pair[0].astype(f32) + crossed(pair[1], ROW, 1).astype(f32)


def generic_inner(first, keep, send, c):
    parts = [keep, send, first[0], first[1]]
    by_x = [
        (parts[0], jnp.where(c == 0, parts[1], parts[2])),
        (jnp.where(c == 0, parts[2], parts[1]), parts[3]),
    ]
    planes = [add_parts([own, swap2(other, "cy")]).astype(bf16) for own, other in by_x]
    return [halve(plane) for plane in planes]


def generic_outer(row_sum, c):
    by_x = [
        (row_sum[0], jnp.where(c == 0, row_sum[1], row_sum[2])),
        (jnp.where(c == 0, row_sum[2], row_sum[1]), row_sum[3]),
    ]
    return [add_parts([own, swap2(other, "cy")]) for own, other in by_x]


def local(
    tokens, w_query, w_key, w_value, w_output, w_inner, w_outer,
    first_gain, first_shift, second_gain, second_shift, seq_lengths, out_grad,
):
    feat = tokens.shape[1]
    cols = tokens.shape[2]
    half = cols // 2
    head_width = w_query.shape[1]
    heads = head_width // HD
    two = lax.axis_size("dp") == 2
    row = lax.axis_index(ROW)
    group = lax.axis_index("dp")
    m = lax.axis_index("rm")
    z = lax.axis_index("rz")
    y = lax.axis_index("cy")
    c = lax.axis_index("cc")
    length = lax.dynamic_index_in_dim(seq_lengths[m], group, keepdims=False)
    own_start = (y * 2 + c) * cols + z * half
    info = jnp.stack([
        row, z, y, c, length - own_start, group if two else 0 * group, 0 * y, 0 * y,
    ]).astype(jnp.int32)

    def turn(blocks):
        pairs = blocks.reshape((2, 2) + blocks.shape[1:])
        return jnp.where(c == 0, pairs, pairs.swapaxes(0, 1)).reshape(blocks.shape)

    def to_slots(array):
        blocks = array.reshape(2, feat, 2, half).transpose(0, 2, 1, 3).reshape(4, feat, half)
        return turn(swap_by(blocks, row))

    def from_slots(parts):
        back = swap_by(turn(jnp.stack(parts)), row)
        return back.reshape(2, 2, feat, half).transpose(0, 2, 1, 3).reshape(2, feat, cols)

    token_blocks = to_slots(tokens)
    this_half, other_half = dp_halves(jnp.concatenate([after(w_query, token_blocks), w_key, w_value], axis=1), c)
    token_three = scatter_steps(token_blocks[:2], token_blocks[2:], ROW)
    x_own = jnp.stack(by_slot(token_three))
    other_columns = core_swap(other_half)
    norms = pack_norms(first_gain, first_shift, second_gain, second_shift)
    if two:
        block_a = jnp.concatenate([after(w_inner, token_blocks), pack_output(w_output, norms)], axis=0)
        pair_a = row_pair(block_a)
        block_b = w_outer.T
        near_b = crossed(after(block_b, token_blocks), ROW, 1)
    pieces = []
    for s in range(4):
        step = jnp.where(c == 0, s % 2, s // 2)
        pieces.append(jnp.where((z ^ step) == c, this_half, other_columns))
    mine = jnp.stack(by_slot(scatter_steps(jnp.stack(pieces[:2]), jnp.stack(pieces[2:]), ROW)))
    theirs = core_swap(mine)
    if two:
        row_a = row_rest(pair_a)
        x_own = after(x_own, pair_a)
    x_second = crossed(x_own, SQUARE, 1)
    xs = (x_own, x_second, crossed(jnp.stack([x_own, x_second]), SQUARE, 0))
    if two:
        xs = (after(x_own, row_a),) + xs[1:]

    starts = []
    for kc in range(2):
        core = c ^ kc
        for s in range(4):
            z_here = z ^ jnp.where(core == 0, s // 2, s % 2)
            y_here = y ^ jnp.where(core == 0, s % 2, s // 2)
            starts.append((y_here * 2 + core) * cols + z_here * half)
    positions = (jnp.stack(starts)[:, None] + jnp.arange(half, dtype=jnp.int32)[None, :]).reshape(-1)
    invalid = jnp.where(positions < length, 0.0, masked_score)
    bias = jnp.where(jnp.arange(HD)[:, None] == 0, invalid[None, :], 0.0).astype(bf16)
    frequency = 10000.0 ** (-2.0 * jnp.arange(HD // 2, dtype=f32) / HD)
    frequency = after(frequency, token_three[1])
    angles = frequency[:, None] * positions[: 4 * half].astype(f32)[None, :]
    cosine = jnp.repeat(jnp.cos(angles), 2, axis=0)
    sines = jnp.sin(angles)
    sine = jnp.stack([-sines, sines], axis=1).reshape(HD, 4 * half)

    q_rot, kv_own = qkv(info, xs, mine, theirs, cosine, sine)
    kv_other = core_swap(kv_own)
    out_b, log_b, low_b = attend(1, q_rot, kv_own, kv_other, bias)
    low_first = crossed(low_b, SQUARE, 0)
    cot_blocks = to_slots(after(out_grad, kv_own))
    cot_first = after(crossed(cot_blocks[2:], ROW, 0), low_b)
    cot_pass = jnp.stack([cot_blocks[1], cot_first[1]])
    cot_second = crossed(cot_pass, ROW, 1)
    cot_three = (cot_blocks[:2], cot_first, cot_second)
    q_second = after(q_rot, low_b, cot_pass)
    if two:
        near_a, far_a = crossed(row_a, PLANE, 1), crossed(row_a, PLANE, 0)
        both_a = crossed(after(near_a, kv_own), PLANE, 0)
        row_a_swapped = core_swap(row_a)
        far_a = after(far_a, low_b)
        both_a = after(both_a, low_b)
        pair_b = jnp.stack([block_b, after(near_b, xs[1])])
        row_b = row_rest(pair_b, low_b)
        q_second = after(q_second, row_a_swapped, far_a, row_b)
        near_b, far_b = crossed(row_b, PLANE, 1), crossed(row_b, PLANE, 0)
    out_a, log_a, low_a = attend(0, q_second, kv_own, kv_other, bias)
    low_pass = jnp.stack([low_a[1], after(low_first, low_a)[1]])
    low_second = crossed(low_pass, SQUARE, 1)
    attn_three = (low_a, low_first, low_second)
    if two:
        both_b = crossed(after(near_b, low_second, cot_second), PLANE, 0)
        chunk_a = [row_a, near_a, far_a, both_a, row_a_swapped] + [core_swap(after(part, low_a)) for part in (near_a, far_a, both_a)]
        chunk_b = core_copies([row_b, near_b, far_b, both_b], [(low_a,), (low_pass,), (low_pass,), (low_pass,)])
    else:
        chunk_a, chunk_b = gather_generic(w_output, w_inner, w_outer, norms, row, y, c)
    mixed_keep, mixed_send, e_keep, e_send, grad_one, attn_t, hidden_t, outer_t, branch_low, act_low, inner_low, norm_sums = middle(
        info, attn_three, x_own, cot_three, chunk_a, chunk_b
    )
    inner_args = (hidden_t, inner_low, attn_t, branch_low, norm_sums)
    outer_args = (outer_t, act_low)

    def tied(args, *earlier):
        return (after(args[0], *earlier),) + args[1:]

    def head_back(first, count, *earlier):
        return attend_back(
            first, count, after(q_rot, *earlier), kv_own, kv_other, bias, (out_a, out_b), (log_a, log_b), grads, cosine, sine
        )

    give_outer = grad_call("outer", "give", info, outer_args)
    got_outer = core_swap(give_outer)
    grads_first = after(crossed(e_send, SQUARE, 0), give_outer)
    grads_pass = jnp.stack([e_keep[1], grads_first[1]])
    grads = (e_keep, grads_first, crossed(grads_pass, SQUARE, 1))
    give_inner = grad_call("inner", "give", info, tied(inner_args, give_outer, grads_pass))
    got_inner = core_swap(give_inner)
    mixed_first = after(crossed(mixed_send, ROW, 0), give_inner)
    mixed_pass = jnp.stack([mixed_keep[1], mixed_first[1]])
    first_outer = grad_call("outer", "first", info, tied(outer_args, mixed_pass, grads[2]), got_outer)
    came_outer = crossed(first_outer, ROW, 0)
    first_inner = grad_call("inner", "first", info, tied(inner_args, first_outer, mixed_pass), got_inner)
    came_inner = crossed(first_inner, PLANE, 0) if two else jnp.zeros_like(first_inner)
    mixed_second = crossed(mixed_pass, ROW, 1)
    dq, own, send = head_back(0, heads, first_inner, mixed_second)
    came_outer = after(came_outer, dq)
    own = after(own, came_outer)
    dkv_got = core_swap(send)
    dx_keep, dx_send, proj = finish_dx(info, dq, own, dkv_got, mine, theirs, cosine, sine)
    dx_first = crossed(dx_send, SQUARE, 0)
    keep_outer, pass_outer = grad_call(
        "outer", "second", info, tied(outer_args, dx_keep), got_outer, after(came_outer, dx_keep)
    )
    keep_inner, pass_inner = grad_call(
        "inner", "second", info, tied(inner_args, keep_outer), got_inner, after(came_inner, keep_outer)
    )
    dx_first = after(dx_first, keep_inner)
    dx_pass = (dx_keep[1] + dx_first[1].astype(f32)).astype(bf16)
    dx_second = crossed(dx_pass, SQUARE, 1)
    keep, give = finish_dw(info, after(proj, dx_pass), xs)
    got = core_swap(give)
    dx_second = after(dx_second, give)
    d_x = add_parts([grad_one, dx_keep[0], dx_first[0], dx_second]).astype(bf16)
    d_x_first = crossed(d_x[2:], ROW, 0)
    by_row_step = keep + after(got, d_x).astype(f32)
    if two:
        here = group == c
        across = lax.ppermute(
            by_row_step.astype(bf16), ("dp", "cc"), [(2, 0), (1, 3)]
        )
    plane_parts = (keep_inner, after(crossed(pass_inner, PLANE, 1), by_row_step)) if two else None
    if two:
        plane_inner = add_parts(plane_parts).astype(bf16)
        pass_on_inner = crossed(plane_inner[2:], ROW, 0)
    row_outer = add_parts([keep_outer, after(crossed(pass_outer, ROW, 1), by_row_step)]).astype(bf16)
    if two:
        pass_on_outer = crossed(row_outer[2:], PLANE, 0)
        d_x_first = after(d_x_first, plane_inner, row_outer)
    d_x_pass = jnp.stack([d_x[1], d_x_first[1]])
    d_x_second = crossed(d_x_pass, ROW, 1)
    if two:
        summed = by_row_step + after(across, d_x_pass).astype(f32)
        active = [(g * 5 + 2 * side, g * 5 + 2 * (1 - side)) for g in range(2) for side in range(2)]
        passed_m = lax.ppermute(summed[2:].astype(bf16), ("dp", "rm", "cc"), active)
        pair_inner = (plane_inner[:2].astype(f32) + after(pass_on_inner, summed).astype(f32)).astype(bf16)
        last_inner = crossed(pair_inner[1], ROW, 1)
        pair_outer = (row_outer[:2].astype(f32) + after(pass_on_outer, pair_inner).astype(f32)).astype(bf16)
        last_outer = crossed(pair_outer[1], PLANE, 1)
        near_far = summed[:2] + after(passed_m, pair_outer).astype(f32)
        far_low = lax.ppermute(near_far[1].astype(bf16), ("dp", "rz", "cc"), active)
        d_x_second = after(d_x_second, near_far)
        d_input = from_slots(by_slot((d_x[:2], d_x_first, d_x_second))).astype(f32)
        near_sum = near_far[0]
        far_sum = after(far_low, d_x_second).astype(f32)
        kept = jnp.where(z == c, near_sum, far_sum)
        passed = core_swap(jnp.where(z == c, far_sum, near_sum).astype(bf16)).astype(f32)
        g_qkv = jnp.where(here, kept, passed)
        inner_sums = [pair_inner[0].astype(f32) + after(last_inner, far_sum).astype(f32)]
        outer_sums = [pair_outer[0].astype(f32) + after(last_outer, far_sum).astype(f32)]
    else:
        near_far = by_row_step[:2] + swap2(by_row_step[2:].astype(bf16), "rm").astype(f32)
        near_sum = near_far[0]
        far_sum = swap2(near_far[1].astype(bf16), "rz").astype(f32)
        kept = jnp.where(z == c, near_sum, far_sum)
        passed = core_swap(jnp.where(z == c, far_sum, near_sum).astype(bf16)).astype(f32)
        d_input = from_slots(by_slot((d_x[:2], d_x_first, d_x_second))).astype(f32)
        g_qkv = dp_sum(kept, passed, c)
        outer_sums = generic_outer(row_outer, c)
        inner_sums = generic_inner(first_inner, keep_inner, pass_inner, c)
    mixed_out = from_slots(by_slot((mixed_keep, mixed_first, mixed_second)))

    half_rows = feat // 2
    third = half_rows // 3
    g_outer = jnp.concatenate([part.T for part in outer_sums], axis=0)
    g_inner = jnp.concatenate([part[:half_rows] for part in inner_sums], axis=0)
    g_output = jnp.concatenate(
        [unpack_output(part[half_rows : half_rows + third], feat) for part in inner_sums], axis=0
    )
    g_norms = inner_sums[0][half_rows : half_rows + 4 * feat // (256 - feat), feat:256].reshape(4, feat)
    if not two:
        g_outer, g_inner, g_output = (
            lax.psum_scatter(g.astype(bf16), "dp", scatter_dimension=0, tiled=True).astype(f32)
            for g in (g_outer, g_inner, g_output)
        )
        g_norms = lax.psum(g_norms, "dp")

    return (
        mixed_out, d_input,
        g_qkv[:, :head_width], g_qkv[:, head_width : 2 * head_width], g_qkv[:, 2 * head_width :],
        g_output, g_inner, g_outer,
        g_norms[0], g_norms[1], g_norms[2], g_norms[3],
    )


def solution(mesh):
    shape = mesh.devices.shape
    fine = Mesh(mesh.devices.reshape(shape[0], 2, shape[1] // 2, 2, shape[2] // 2), EVERY)
    col = ("cy", "cc")
    acts = P(None, ROW, ("dp",) + col)
    by_row = P(ROW + ("dp",), col)
    by_col = P(col + ("dp",), ROW)
    vec = P(ROW)
    return jax.shard_map(
        local,
        mesh=fine,
        in_specs=(
            acts, by_row, by_row, by_row, by_col, by_row, by_col, vec, vec, vec, vec, P(), acts,
        ),
        out_specs=(
            acts, acts, by_row, by_row, by_row, by_col, by_row, by_col, vec, vec, vec, vec,
        ),
        check_vma=False,
    )
```
